128 devices in a mesh: teacher: 4 (over y_hi, core), seq: 32 (over x, y_lo, z).
Axes of the slice: x: 4, y: 4 (y_hi: 2, y_lo: 2; y = y_hi * 2 + y_lo), z: 4, core: 2. Of those that a mesh axis runs over, the one named last changes fastest.
Arguments:
- activations: bfloat16 [20, 2048, 1536], P('teacher', 'seq'), may hold values from -150 to 150
- teacher_maps: bfloat16 [4, 20, 2048, 1536], P('teacher', None, 'seq'), may hold values from -6 to 6
- projection: bfloat16 [4, 1536, 1536], P('teacher', 'seq'), may hold values from -0.625 to 0.625
- dilated_weight: bfloat16 [1536, 3, 768], P('seq'), may hold values from -0.09375 to 0.09375
- pointwise_weight: bfloat16 [768, 1536], P('seq'), may hold values from -0.21875 to 0.21875
Outputs:
- loss_mean: float32 [], replicated
- dilated_grad: float32 [1536, 3, 768], P('seq')
- pointwise_grad: float32 [768, 1536], P('seq')
The draws below stay inside these ranges and needn't reach their ends.
All inputs are finite; a program needn't handle non-finite values.
Results may differ from the reference program's by a relative error of at most 0.00081.
Values may be sent and summed in bfloat16 or wider, within the bound.
No kernel may reach another device: no remote copies, remote signals or barrier semaphores. Data moves between devices by JAX's collectives and lax.ppermute only.
A program may use at most 128 MiB of HBM per device.

```python
import jax
import jax.numpy as jnp
from jax import lax

STUDENT_CHANNELS = 1536
CH = 768
CT = 1536
TAP_DILATION = 16
TEACHERS = 4
WINDOWS = 20
WINDOW_BINS = 2048


def draw_activations(key, part):
    keyed = jax.random.fold_in(key, 17)
    key_base, key_rows, key_cols = jax.random.split(keyed, 3)
    full_shape = (WINDOWS, WINDOW_BINS, STUDENT_CHANNELS)
    baseline = jnp.clip(jax.random.normal(key_base, full_shape, jnp.float32), -6.0, 6.0)
    rise_factor = 3.0
    roughness = jnp.exp(jax.random.uniform(key_rows, (WINDOWS, WINDOW_BINS, 1), jnp.float32, 0.0, 2.302585))
    columns_scale = jnp.exp(jax.random.uniform(key_cols, (1, 1, STUDENT_CHANNELS), jnp.float32, 0.0, 2.302585))
    trend_rise = jnp.exp(jnp.log(rise_factor) * (1.0 - jnp.arange(WINDOW_BINS, dtype=jnp.float32) / WINDOW_BINS)).reshape(1, WINDOW_BINS, 1)
    return (0.05 * baseline * roughness * columns_scale * trend_rise).astype(jnp.bfloat16)


def raised(array, stream_key, source, target, shards_of, factor):
    owner, partner = [(jnp.arange(array.shape[axis_at]) // (array.shape[axis_at] // shards_of)).reshape([-1 if axis == axis_at else 1 for axis in range(array.ndim)]) for axis_at in (source, target)]
    chosen = jax.random.permutation(stream_key, shards_of)[partner]
    strong = (owner == chosen) | (owner == (partner + shards_of // 2) % shards_of)
    return jnp.where(strong, factor * array, array)


def steps_of(key, shape, shards, low, largest):
    level, own = 1.0, jax.random.fold_in(key, 6)
    for dim, parts in shards:
        heights = jnp.exp(jax.random.uniform(jax.random.fold_in(own, dim), (parts,), jnp.float32, low / len(shards), largest / len(shards)))
        level = level * jnp.repeat(heights, shape[dim] // parts).reshape([-1 if axis == dim else 1 for axis in range(len(shape))])
    return level


def scatter_about(rng, shape, width, limit, pieces=(), held_as=jnp.bfloat16):
    result = jax.random.normal(rng, shape, jnp.float32) * width
    if len(pieces) > 0:
        result = steps_of(rng, shape, pieces, -0.22, 0.18) * result
    return jnp.clip(result, min=-limit, max=limit).astype(held_as)


def heavy_noise(key, extent, width, most, pieces, heavy, kind=jnp.bfloat16):
    array = width * jax.random.normal(key, extent, jnp.float32)
    if pieces:
        array = array * steps_of(key, extent, pieces, -0.22, 0.18)
    return jnp.clip(raised(array, jax.random.fold_in(key, 3), *heavy), -most, most).astype(kind)


def setup_inputs(seed: int = 0) -> dict:
    arg_keys = jax.random.split(jax.random.key(seed), 6)
    return {
        "activations": draw_activations(jax.random.fold_in(arg_keys[5], 71), 0),
        "teacher_maps": scatter_about(arg_keys[1], (TEACHERS, WINDOWS, WINDOW_BINS, CT), 1.0, 6.0, ((0, 4), (2, 32))),
        "projection": heavy_noise(arg_keys[2], (TEACHERS, CT, STUDENT_CHANNELS), (CT // 4) ** -0.5, 0.625, ((0, 4), (1, 32)), (1, 2, 32, 2.75)),
        "dilated_weight": scatter_about(arg_keys[3], (STUDENT_CHANNELS, 3, CH), (3 * STUDENT_CHANNELS) ** -0.5, 0.09375, ((0, 32),)),
        "pointwise_weight": scatter_about(arg_keys[4], (CH, STUDENT_CHANNELS), CH ** -0.5, 0.21875, ((0, 32),)),
    }


slope_const = 0.7978845608
cubic_const = 0.044715

def gelu_tanh(value):
    inside = slope_const * (value + cubic_const * value * value * value)
    return 0.5 * value * (1.0 + jnp.tanh(inside))

def gelu_slope(value):
    inside = slope_const * (value + cubic_const * value * value * value)
    tangent = jnp.tanh(inside)
    return 0.5 * (1.0 + tangent) + 0.5 * value * (1.0 - tangent * tangent) * slope_const * (1.0 + 3.0 * cubic_const * value * value)

def reference(activations, teacher_maps, projection, dilated_weight, pointwise_weight):
    count_of_rows = WINDOWS * WINDOW_BINS
    target = jnp.zeros((count_of_rows, STUDENT_CHANNELS), jnp.float32)
    for teacher_id in range(TEACHERS):
        maps_flat = teacher_maps[teacher_id].reshape(count_of_rows, CT)
        rounded = lax.optimization_barrier(jnp.dot(maps_flat, projection[teacher_id], preferred_element_type=jnp.float32).astype(jnp.bfloat16))
        target = target + rounded.astype(jnp.float32)
    target = target / TEACHERS
    inputs_f = activations.reshape(count_of_rows, STUDENT_CHANNELS).astype(jnp.float32)
    channel_mean = lax.optimization_barrier(jnp.sum(inputs_f, axis=0)) / count_of_rows
    channel_var = lax.optimization_barrier(jnp.sum(inputs_f * inputs_f, axis=0)) / count_of_rows - channel_mean * channel_mean
    normed = (inputs_f - channel_mean) * lax.rsqrt(channel_var + 1e-05)
    hidden_state = gelu_tanh(normed).astype(jnp.bfloat16).reshape(WINDOWS, WINDOW_BINS, STUDENT_CHANNELS)
    padded_input = jnp.pad(hidden_state, ((0, 0), (TAP_DILATION, TAP_DILATION), (0, 0)))
    tap_weights = [padded_input[:, offset_index * TAP_DILATION:offset_index * TAP_DILATION + WINDOW_BINS].reshape(count_of_rows, STUDENT_CHANNELS) for offset_index in range(3)]
    preact = jnp.zeros((count_of_rows, CH), jnp.float32)
    for offset_index in range(3):
        preact = preact + jnp.dot(tap_weights[offset_index], dilated_weight[:, offset_index, :], preferred_element_type=jnp.float32)
    activated = gelu_tanh(preact).astype(jnp.bfloat16)
    student = inputs_f + jnp.dot(activated, pointwise_weight, preferred_element_type=jnp.float32)
    misfit = student - target
    loss_mean = 0.5 * jnp.sum(misfit * misfit) / (STUDENT_CHANNELS * count_of_rows)
    out_grad = (misfit / STUDENT_CHANNELS).astype(jnp.bfloat16)
    pointwise_grad = lax.dot_general(activated, out_grad, (((0,), (0,)), ((), ())), preferred_element_type=jnp.float32)
    back_grad = lax.dot_general(out_grad, pointwise_weight, (((1,), (1,)), ((), ())), preferred_element_type=jnp.float32)
    preact_grad = (back_grad * gelu_slope(preact)).astype(jnp.bfloat16)
    dilated_grad = jnp.stack([lax.dot_general(tap_weights[offset_index], preact_grad, (((0,), (0,)), ((), ())), preferred_element_type=jnp.float32) for offset_index in range(3)], axis=1)
    return (loss_mean, dilated_grad, pointwise_grad)
```

```python
import jax
import jax.numpy as jnp
import numpy as np
from jax import lax
from jax.experimental import pallas as pl
from jax.experimental.pallas import tpu as pltpu
from jax.sharding import PartitionSpec as P

TAP_DILATION = 16
AXES = ("teacher", "seq")
SHAPE = (2, 2, 4, 2, 4)
STEPS = (0, -1, 1, 2)

slope_const = 0.7978845608
cubic_const = 0.044715


def pairs_of(move):
    pairs = []
    for source in range(int(np.prod(SHAPE))):
        at = [int(v) for v in np.unravel_index(source, SHAPE)]
        pairs.append((source, int(np.ravel_multi_index(move(*at), SHAPE))))
    return pairs


def along(first, step):
    def move(yh, core, x, yl, z):
        if (core == 0) == first:
            return (yh, core, (x + step) % 4, yl, z)
        return (yh, core, x, yl, (z + step) % 4)

    return pairs_of(move)


CORE = pairs_of(lambda yh, core, x, yl, z: (yh, 1 - core, x, yl, z))
FAR = pairs_of(lambda yh, core, x, yl, z: (1 - yh, core, x, yl, z))
NEAR = pairs_of(lambda yh, core, x, yl, z: (yh, core, x, 1 - yl, z))
RING = {(first, step): along(first, step) for first in (True, False) for step in (1, -1, 2)}


def send(value, pairs):
    return lax.ppermute(value, AXES, pairs)


def gelu_tanh(value):
    inside = slope_const * (value + cubic_const * value * value * value)
    return 0.5 * value * (1.0 + jnp.tanh(inside))


def gelu_slope(value):
    inside = slope_const * (value + cubic_const * value * value * value)
    tangent = jnp.tanh(inside)
    return 0.5 * (1.0 + tangent) + 0.5 * value * (1.0 - tangent * tangent) * slope_const * (
        1.0 + 3.0 * cubic_const * value * value
    )


def block_order(core, x, yl, z):
    first = jnp.where(core == 0, x, z)
    second = jnp.where(core == 0, z, x)
    order = []
    for far in STEPS:
        for near in STEPS:
            for side in (0, 1):
                one = (first + near + 4) % 4
                two = (second + far + 4) % 4
                at_x = jnp.where(core == 0, one, two)
                at_z = jnp.where(core == 0, two, one)
                order.append((at_x * 2 + (yl + side) % 2) * 4 + at_z)
    return jnp.stack(order).astype(jnp.int32)


def ring_gather(value, first):
    return [value] + [send(value, RING[first, -step]) for step in STEPS[1:3]] + [send(value, RING[first, 2])]


def gather(value):
    value = value[None]
    value = jnp.concatenate([value, send(value, NEAR)])
    value = jnp.concatenate(ring_gather(value, True))
    return ring_gather(value, False)


def ring_reduce(chunks, first):
    own, low, high, across = chunks
    return (
        own
        + send(low, RING[first, -1])
        + send(high, RING[first, 1])
        + send(across, RING[first, 2])
    )


def reduce(chunks):
    own = ring_reduce(chunks, False)
    own = ring_reduce([own[2 * i : 2 * i + 2] for i in range(4)], True)
    return own[0] + send(own[1], NEAR)


def load_blocks(order, pieces, whole, sem):
    copies = []
    for place in range(32):
        source = pieces[place // 8].at[place % 8]
        row = pl.multiple_of(order[place] * 48, 16)
        copies.append(pltpu.make_async_copy(source, whole.at[pl.ds(row, 48), :], sem))
    for copy in copies:
        copy.start()
    for copy in copies:
        copy.wait()


def place_kernel(order, p0, p1, p2, p3, whole, sem):
    load_blocks(order, (p0, p1, p2, p3), whole, sem)


def place(order, pieces):
    width = pieces[0].shape[2]
    return pl.pallas_call(
        place_kernel,
        grid_spec=pltpu.PrefetchScalarGridSpec(
            num_scalar_prefetch=1,
            grid=(1,),
            in_specs=[pl.BlockSpec(memory_space=pl.ANY)] * 4,
            out_specs=pl.BlockSpec((1536, width), lambda i, order: (0, 0)),
            scratch_shapes=[pltpu.SemaphoreType.DMA(())],
        ),
        out_shape=jax.ShapeDtypeStruct((1536, width), pieces[0].dtype),
        name="place",
    )(order, *pieces)


def teacher_kernel(order, groups, maps, p0, p1, p2, p3, out, whole, sem):
    @pl.when(pl.program_id(0) == 0)
    def _():
        load_blocks(order, (p0, p1, p2, p3), whole, sem)

    out[0] = jnp.dot(maps[0], whole[...], preferred_element_type=jnp.float32).astype(jnp.bfloat16)


def teacher_terms(order, groups, maps, pieces):
    count = groups.shape[0]
    rows, width = maps.shape[1:]
    return pl.pallas_call(
        teacher_kernel,
        grid_spec=pltpu.PrefetchScalarGridSpec(
            num_scalar_prefetch=2,
            grid=(count,),
            in_specs=[pl.BlockSpec((1, rows, width), lambda i, order, groups: (groups[i], 0, 0))]
            + [pl.BlockSpec(memory_space=pl.ANY)] * 4,
            out_specs=pl.BlockSpec((1, rows, 1536), lambda i, order, groups: (i, 0, 0)),
            scratch_shapes=[pltpu.VMEM((1536, 1536), jnp.bfloat16), pltpu.SemaphoreType.DMA(())],
        ),
        out_shape=jax.ShapeDtypeStruct((count, rows, 1536), jnp.bfloat16),
        name="teacher",
    )(order, groups, maps, *pieces)


def split_kernel(order, g0, g1, g2, g3, c0, c1, c2, c3):
    outs = (c0, c1, c2, c3)
    for place in range(32):
        row = pl.multiple_of(order[place] * 48, 8)
        for col, g in enumerate((g0, g1, g2, g3)):
            outs[place // 8][place % 8, :, col * 384 : (col + 1) * 384] = g[pl.ds(row, 48), :]


def split(order, parts):
    return pl.pallas_call(
        split_kernel,
        grid_spec=pltpu.PrefetchScalarGridSpec(
            num_scalar_prefetch=1,
            grid=(1,),
            in_specs=[pl.BlockSpec((1536, 384), lambda i, order: (0, 0))] * 4,
            out_specs=[pl.BlockSpec((8, 48, 1536), lambda i, order: (0, 0, 0))] * 4,
        ),
        out_shape=[jax.ShapeDtypeStruct((8, 48, 1536), jnp.float32)] * 4,
        name="split",
    )(order, *parts)


def column_product(left, right):
    return lax.dot_general(
        left, right, (((0,), (0,)), ((), ())), preferred_element_type=jnp.float32
    )


def in_order(core, own, other, axis):
    return jnp.where(
        core == 0,
        jnp.concatenate([own, other], axis=axis),
        jnp.concatenate([other, own], axis=axis),
    )


def half_of(value, index, axis):
    size = value.shape[axis] // 2
    return lax.dynamic_slice_in_dim(value, index * size, size, axis)


def sum_everywhere(values):
    spread = lax.all_to_all(values.reshape(128, -1), AXES, 0, 0, tiled=True)
    part = jnp.sum(spread, axis=0, keepdims=True)
    return lax.all_to_all(jnp.broadcast_to(part, spread.shape), AXES, 0, 0, tiled=True).reshape(-1)


def shards(activations, teacher_maps, projection, dilated_weight, pointwise_weight):
    teacher = lax.axis_index("teacher")
    seq = lax.axis_index("seq")
    yh, core = teacher // 2, teacher % 2
    x, yl, z = seq // 8, (seq // 4) % 2, seq % 4
    wins, bins, channels = activations.shape
    rows = wins * bins
    total_rows = rows * 128
    branch = dilated_weight.shape[2]
    half = branch // 2
    order = block_order(core, x, yl, z)

    pieces = gather(projection[0])

    inputs_f = activations.reshape(rows, channels).astype(jnp.float32)
    sums = sum_everywhere(
        jnp.concatenate([jnp.sum(inputs_f, axis=0), jnp.sum(inputs_f * inputs_f, axis=0)])
        .reshape(2, 128, channels // 128)
        .transpose(1, 0, 2)
        .reshape(-1)
    )
    sums = sums.reshape(128, 2, channels // 128).transpose(1, 0, 2).reshape(2, channels)
    channel_mean = sums[0] / total_rows
    channel_var = sums[1] / total_rows - channel_mean * channel_mean
    normed = (inputs_f - channel_mean) * lax.rsqrt(channel_var + 1e-05)
    hidden = gelu_tanh(normed).astype(jnp.bfloat16).reshape(wins, bins, channels)
    forward = [(g * 32 + i, g * 32 + i + 1) for g in range(4) for i in range(31)]
    backward = [(b, a) for a, b in forward]
    low = send(hidden[:, -TAP_DILATION:], forward)
    high = send(hidden[:, :TAP_DILATION], backward)
    padded = jnp.concatenate([low, hidden, high], axis=1)
    padded_other = send(padded, CORE)

    own_dil = lax.dynamic_slice_in_dim(dilated_weight, core * half, half, 2).reshape(48, 3 * half)
    own_pw = half_of(pointwise_weight, core, 1)
    own_block = jnp.concatenate(
        [own_dil, jnp.concatenate([own_pw[:, :half], own_pw[:, half:]], axis=0)], axis=1
    )
    weights = place(order, gather(own_block))
    weights_other = send(weights, CORE)

    maps = teacher_maps.reshape(4, rows, teacher_maps.shape[3])
    far_groups = jnp.stack([(1 - yh) * 2 + 1 - core, (1 - yh) * 2 + core]).astype(jnp.int32)
    near_groups = jnp.stack([yh * 2 + 1 - core, yh * 2 + core]).astype(jnp.int32)
    far_terms = teacher_terms(order, far_groups, maps, pieces)
    far_sum = far_terms[1].astype(jnp.float32) + send(far_terms[0], CORE).astype(jnp.float32)
    peak = jnp.max(jnp.abs(far_sum), keepdims=True) + 1e-30
    arrived_scale = send(jnp.broadcast_to(peak, (8, 128)), FAR)[:1, :1]
    arrived = send((far_sum * (16384.0 / peak)).astype(jnp.float16), FAR)
    near_terms = teacher_terms(order, near_groups, maps, pieces)
    near_sum = near_terms[1].astype(jnp.float32) + send(near_terms[0], CORE).astype(jnp.float32)
    target = (near_sum + arrived.astype(jnp.float32) * (arrived_scale / 16384.0)) / 4

    taps = [
        padded[:, k * TAP_DILATION : k * TAP_DILATION + bins].reshape(rows, channels) for k in range(3)
    ]
    taps_other = [
        padded_other[:, k * TAP_DILATION : k * TAP_DILATION + bins].reshape(rows, channels)
        for k in range(3)
    ]

    def conv(w):
        running = jnp.zeros((rows, half), jnp.float32)
        for k in range(3):
            running = running + jnp.dot(
                taps[k], w[:, k * half : (k + 1) * half], preferred_element_type=jnp.float32
            )
        return running

    preact = in_order(core, conv(weights), conv(weights_other), 1)
    activated = gelu_tanh(preact).astype(jnp.bfloat16)

    def columns(w):
        return w[:, 3 * half :].reshape(32, 2, branch // 32, half).transpose(0, 2, 1, 3).reshape(branch, branch)

    pointwise = in_order(core, columns(weights), columns(weights_other), 1)
    student = inputs_f + jnp.dot(activated, pointwise, preferred_element_type=jnp.float32)
    misfit = student - target
    squared = jnp.sum(misfit * misfit)
    out_grad = (misfit / channels).astype(jnp.bfloat16)
    back_grad = lax.dot_general(
        out_grad, pointwise, (((1,), (1,)), ((), ())), preferred_element_type=jnp.float32
    )
    preact_grad = (back_grad * gelu_slope(preact)).astype(jnp.bfloat16)

    act_both = jnp.concatenate([activated, send(activated, CORE)])
    out_both = jnp.concatenate([half_of(out_grad, core, 1), send(half_of(out_grad, 1 - core, 1), CORE)])
    pre_both = jnp.concatenate(
        [half_of(preact_grad, core, 1), send(half_of(preact_grad, 1 - core, 1), CORE)]
    )
    pw_part = (
        column_product(act_both, out_both)
        .reshape(32, branch // 32, 2, half)
        .transpose(0, 2, 1, 3)
        .reshape(channels, half)
    )
    parts = [column_product(jnp.concatenate([taps[k], taps_other[k]]), pre_both) for k in range(3)]
    block = reduce(split(order, parts + [pw_part]))
    block = block + send(block, FAR)
    other = send(block, CORE)
    dilated_grad = in_order(
        core, block[:, : 3 * half].reshape(48, 3, half), other[:, : 3 * half].reshape(48, 3, half), 2
    )

    def pw_columns(value):
        return value[:, 3 * half :].reshape(2, branch // 32, half).transpose(1, 0, 2).reshape(branch // 32, branch)

    pointwise_grad = in_order(core, pw_columns(block), pw_columns(other), 1)
    squares = lax.all_to_all(jnp.broadcast_to(squared, (128, 1)), AXES, 0, 0, tiled=True)
    loss_mean = 0.5 * jnp.sum(squares) / (channels * total_rows)
    return (loss_mean, dilated_grad, pointwise_grad)


def solution(mesh):
    in_specs = (
        P("teacher", "seq", None),
        P("teacher", None, "seq", None),
        P("teacher", "seq", None),
        P("seq", None, None),
        P("seq", None),
    )
    out_specs = (P(), P("seq", None, None), P("seq", None))
    return jax.shard_map(shards, mesh=mesh, in_specs=in_specs, out_specs=out_specs, check_vma=False)
```

```python
import jax
import jax.numpy as jnp
import numpy as np
from jax import lax
from jax.experimental import pallas as pl
from jax.experimental.pallas import tpu as pltpu
from jax.sharding import PartitionSpec as P

TAP_DILATION = 16
AXES = ("teacher", "seq")
SHAPE = (2, 2, 4, 2, 4)
STEPS = (0, -1, 1, 2)

slope_const = 0.7978845608
cubic_const = 0.044715


def pairs_of(move):
    pairs = []
    for source in range(int(np.prod(SHAPE))):
        at = [int(v) for v in np.unravel_index(source, SHAPE)]
        pairs.append((source, int(np.ravel_multi_index(move(*at), SHAPE))))
    return pairs


def along(first, step):
    def move(yh, core, x, yl, z):
        if (core == 0) == first:
            return (yh, core, (x + step) % 4, yl, z)
        return (yh, core, x, yl, (z + step) % 4)

    return pairs_of(move)


CORE = pairs_of(lambda yh, core, x, yl, z: (yh, 1 - core, x, yl, z))
FAR = pairs_of(lambda yh, core, x, yl, z: (1 - yh, core, x, yl, z))
NEAR = pairs_of(lambda yh, core, x, yl, z: (yh, core, x, 1 - yl, z))
FAR_NEAR = pairs_of(lambda yh, core, x, yl, z: (1 - yh, core, x, 1 - yl, z))
RING = {(first, step): along(first, step) for first in (True, False) for step in (1, -1, 2)}


def send(value, pairs):
    return lax.ppermute(value, AXES, pairs)


def gelu_tanh(value):
    inside = slope_const * (value + cubic_const * value * value * value)
    return 0.5 * value * (1.0 + jnp.tanh(inside))


def gelu_slope(value):
    inside = slope_const * (value + cubic_const * value * value * value)
    tangent = jnp.tanh(inside)
    return 0.5 * (1.0 + tangent) + 0.5 * value * (1.0 - tangent * tangent) * slope_const * (
        1.0 + 3.0 * cubic_const * value * value
    )


def block_order(core, x, yl, z):
    first = jnp.where(core == 0, x, z)
    second = jnp.where(core == 0, z, x)
    order = []
    for far in STEPS:
        for near in STEPS:
            for side in (0, 1):
                one = (first + near + 4) % 4
                two = (second + far + 4) % 4
                at_x = jnp.where(core == 0, one, two)
                at_z = jnp.where(core == 0, two, one)
                order.append((at_x * 2 + (yl + side) % 2) * 4 + at_z)
    return jnp.stack(order).astype(jnp.int32)


def concat(*values):
    return jnp.concatenate(values)


def after(value, *earlier):
    return lax.optimization_barrier((value, *earlier))[0]


def gather_near(value):
    return concat(value[None], send(value[None], NEAR))


def gather_first(value):
    return concat(
        value,
        send(value, RING[True, 1]),
        send(value, RING[True, -1]),
        send(value, RING[True, 2]),
    )


def gather_second(value):
    return send(value, RING[False, 1]), send(value, RING[False, -1])


def gather_rest(value, low, high):
    half = value.shape[0] // 2
    return [value, low, high, send(low[:half], RING[False, 1]), send(high[half:], RING[False, -1])]


def pack(value, peak):
    power = jnp.clip(jnp.floor(jnp.log2(jnp.maximum(peak, 1e-30))) - 13.0, -110.0, 127.0).reshape(1, 1)
    scaled = (value * jnp.exp2(-power)).astype(jnp.float16)
    return concat(scaled, jnp.broadcast_to(power, (16, value.shape[1])).astype(jnp.float16))


def unpack(value):
    power = value[-16:-15, :1].astype(jnp.float32)
    return value[:-16].astype(jnp.float32) * jnp.exp2(power)


def ring_reduce(own, others, peak, first):
    for chunk, step in zip(others, STEPS[1:], strict=True):
        own = own + unpack(send(pack(chunk, peak), RING[first, step]))
    return own


def finish_reduce(own):
    others = [own[96 * i : 96 * i + 96] for i in range(1, 4)]
    own = ring_reduce(own[:96], others, jnp.max(jnp.abs(own)), True)
    keep, give = own[:48], own[48:]
    return keep + send(give, NEAR) + send(keep, FAR) + send(give, FAR_NEAR)


def block_copies(order, pieces, target, sem):
    copies, place = [], 0
    for piece in pieces:
        for at in range(piece.shape[0]):
            row = pl.multiple_of(order[place] * 48, 16)
            copies.append(pltpu.make_async_copy(piece.at[at], target(row), sem))
            place += 1
    return copies


def teacher_kernel(order, groups, maps, *refs):
    count = len(refs) - 3
    out, whole, sem = refs[count:]
    width = refs[0].shape[2]

    @pl.when(pl.program_id(0) == 0)
    def _():
        copies = []
        for part in range(count // 5):
            copies += block_copies(
                order,
                refs[5 * part : 5 * part + 5],
                lambda row, part=part: whole.at[pl.ds(row, 48), part * width : (part + 1) * width],
                sem,
            )
        for copy in copies:
            copy.start()
        for copy in copies:
            copy.wait()

    out[0] = jnp.dot(maps[0], whole[...], preferred_element_type=jnp.float32).astype(jnp.bfloat16)


def teacher_terms(order, groups, maps, pieces):
    count = groups.shape[0]
    rows, depth = maps.shape[1:]
    width = pieces[0].shape[2] * len(pieces) // 5
    return pl.pallas_call(
        teacher_kernel,
        grid_spec=pltpu.PrefetchScalarGridSpec(
            num_scalar_prefetch=2,
            grid=(count,),
            in_specs=[pl.BlockSpec((1, rows, depth), lambda i, order, groups: (groups[i], 0, 0))]
            + [pl.BlockSpec(memory_space=pl.ANY)] * len(pieces),
            out_specs=pl.BlockSpec((1, rows, width), lambda i, order, groups: (i, 0, 0)),
            scratch_shapes=[pltpu.VMEM((depth, width), jnp.bfloat16), pltpu.SemaphoreType.DMA(())],
        ),
        out_shape=jax.ShapeDtypeStruct((count, rows, width), jnp.bfloat16),
        name="teacher",
    )(order, groups, maps, *pieces)


def forward_kernel(orders, cores, padded, inputs, *refs):
    pieces = refs[:10]
    preact, activated, student, pointwise, whole, sem = refs[10:]
    copies = []
    for part in range(2):
        copies += block_copies(
            orders.at[part],
            pieces[5 * part : 5 * part + 5],
            lambda row, part=part: whole.at[cores[part], pl.ds(row, 48), :],
            sem,
        )
    for copy in copies:
        copy.start()
    for copy in copies:
        copy.wait()
    for core in range(2):
        for pair in range(16):
            rows = whole[core, 96 * pair : 96 * pair + 96, 1152:].astype(jnp.float32)
            for part in range(2):
                pointwise[48 * pair : 48 * pair + 48, core * 768 + part * 384 : core * 768 + part * 384 + 384] = (
                    concat(rows[24 * part : 24 * part + 24], rows[48 + 24 * part : 72 + 24 * part]).astype(jnp.bfloat16)
                )
    for core in range(2):
        running = jnp.zeros((320, 384), jnp.float32)
        for k in range(3):
            tap = padded[:, k * TAP_DILATION : k * TAP_DILATION + 64, :].reshape(320, 1536)
            running = running + jnp.dot(
                tap, whole[core, :, k * 384 : k * 384 + 384], preferred_element_type=jnp.float32
            )
        preact[:, core * 384 : core * 384 + 384] = running
        activated[:, core * 384 : core * 384 + 384] = gelu_tanh(running).astype(jnp.bfloat16)
    student[...] = inputs[...].astype(jnp.float32) + jnp.dot(
        activated[...], pointwise[...], preferred_element_type=jnp.float32
    )


def whole_block(shape):
    return pl.BlockSpec(shape, lambda *i: (0,) * len(shape))


def forward_pass(orders, cores, padded, inputs, pieces):
    outs = [((320, 768), jnp.float32), ((320, 768), jnp.bfloat16), ((320, 1536), jnp.float32), ((768, 1536), jnp.bfloat16)]
    return pl.pallas_call(
        forward_kernel,
        grid_spec=pltpu.PrefetchScalarGridSpec(
            num_scalar_prefetch=2,
            grid=(1,),
            in_specs=[whole_block(padded.shape), whole_block(inputs.shape)]
            + [pl.BlockSpec(memory_space=pl.ANY)] * 10,
            out_specs=[whole_block(shape) for shape, _ in outs],
            scratch_shapes=[pltpu.VMEM((2, 1536, 1536), jnp.bfloat16), pltpu.SemaphoreType.DMA(())],
        ),
        out_shape=[jax.ShapeDtypeStruct(shape, kind) for shape, kind in outs],
        name="forward",
    )(orders, cores, padded, inputs, *pieces)


def gradient_kernel(taps, order, *refs):
    refs = list(refs)
    scratch = refs.pop()
    peak = refs.pop()
    outs = [refs.pop() for _ in range(4)][::-1]
    contract = (((0,), (0,)), ((), ()))
    most = jnp.zeros((8, 128), jnp.float32)
    column = 0
    if taps[0] is None:
        activated, activated_other, out_grad, out_grad_other = [refs.pop(0) for _ in range(4)]
        product = lax.dot_general(activated[...], out_grad[...], contract, preferred_element_type=jnp.float32)
        product = product + lax.dot_general(
            activated_other[...], out_grad_other[...], contract, preferred_element_type=jnp.float32
        )
        most = jnp.maximum(most, jnp.max(jnp.abs(product)))
        scratch[:768, :] = product
        for place in range(32):
            rows = scratch[pl.ds(pl.multiple_of(order[place] * 24, 8), 24), :]
            outs[place // 8][place % 8, :24, :384] = rows[:, :384]
            outs[place // 8][place % 8, 24:, :384] = rows[:, 384:]
        column = 384
    padded, padded_other, preact_grad, preact_grad_other = refs
    for k in taps:
        if k is None:
            continue
        low = k * TAP_DILATION
        product = lax.dot_general(
            padded[:, low : low + 64, :].reshape(320, 1536), preact_grad[...], contract,
            preferred_element_type=jnp.float32,
        )
        product = product + lax.dot_general(
            padded_other[:, low : low + 64, :].reshape(320, 1536), preact_grad_other[...], contract,
            preferred_element_type=jnp.float32,
        )
        most = jnp.maximum(most, jnp.max(jnp.abs(product)))
        scratch[:, :384] = product
        for place in range(32):
            outs[place // 8][place % 8, :, column : column + 384] = scratch[
                pl.ds(pl.multiple_of(order[place] * 48, 8), 48), :384
            ]
        column += 384
    peak[...] = most


def gradient_chunks(taps, order, args):
    return pl.pallas_call(
        lambda *refs: gradient_kernel(taps, *refs),
        grid_spec=pltpu.PrefetchScalarGridSpec(
            num_scalar_prefetch=1,
            grid=(1,),
            in_specs=[whole_block(arg.shape) for arg in args],
            out_specs=[whole_block((8, 48, 768))] * 4 + [whole_block((8, 128))],
            scratch_shapes=[pltpu.VMEM((1536, 768), jnp.float32)],
        ),
        out_shape=[jax.ShapeDtypeStruct((8, 48, 768), jnp.float32)] * 4
        + [jax.ShapeDtypeStruct((8, 128), jnp.float32)],
        name="gradient",
    )(order, *args)


def in_order(core, own, other, axis):
    return jnp.where(
        core == 0,
        jnp.concatenate([own, other], axis=axis),
        jnp.concatenate([other, own], axis=axis),
    )


def half_of(value, index, axis):
    size = value.shape[axis] // 2
    return lax.dynamic_slice_in_dim(value, index * size, size, axis)


def sum_everywhere(values):
    spread = lax.all_to_all(values.reshape(128, -1), AXES, 0, 0, tiled=True)
    part = jnp.sum(spread, axis=0, keepdims=True)
    return lax.all_to_all(jnp.broadcast_to(part, spread.shape), AXES, 0, 0, tiled=True).reshape(-1)


def shards(activations, teacher_maps, projection, dilated_weight, pointwise_weight):
    teacher = lax.axis_index("teacher")
    seq = lax.axis_index("seq")
    yh, core = teacher // 2, teacher % 2
    x, yl, z = seq // 8, (seq // 4) % 2, seq % 4
    wins, bins, channels = activations.shape
    rows = wins * bins
    total_rows = rows * 128
    branch = dilated_weight.shape[2]
    half = branch // 2
    order = block_order(core, x, yl, z)
    order_other = block_order(1 - core, x, yl, z)

    own_dil = lax.dynamic_slice_in_dim(dilated_weight, core * half, half, 2).reshape(48, 3 * half)
    own_pw = half_of(pointwise_weight, core, 1)
    own_block = jnp.concatenate([own_dil, concat(own_pw[:, :half], own_pw[:, half:])], axis=1)

    near = gather_near(projection[0])
    near_w = gather_near(own_block)
    first_a = gather_first(near[:, :, : channels // 2])
    first_b = gather_first(near[:, :, channels // 2 :])
    second_a = gather_second(first_a)
    first_w = gather_first(after(near_w, first_a))
    pieces_a = gather_rest(first_a, *second_a)
    second_b = gather_second(after(first_b, second_a[0]))
    pieces_b = gather_rest(first_b, *second_b)
    second_w = gather_second(after(first_w, second_b[0]))
    pieces_w = gather_rest(first_w, *second_w)
    pieces_other = [send(piece, CORE) for piece in pieces_w]

    inputs = activations.reshape(rows, channels)
    inputs_f = inputs.astype(jnp.float32)
    local = (
        jnp.concatenate([jnp.sum(inputs_f, axis=0), jnp.sum(inputs_f * inputs_f, axis=0)])
        .reshape(2, 128, channels // 128)
        .transpose(1, 0, 2)
        .reshape(-1)
    )
    sums = sum_everywhere(after(local, first_a))
    sums = sums.reshape(128, 2, channels // 128).transpose(1, 0, 2).reshape(2, channels)
    channel_mean = sums[0] / total_rows
    channel_var = sums[1] / total_rows - channel_mean * channel_mean
    normed = (inputs_f - channel_mean) * lax.rsqrt(channel_var + 1e-05)
    hidden = gelu_tanh(normed).astype(jnp.bfloat16).reshape(wins, bins, channels)
    forward = [(g * 32 + i, g * 32 + i + 1) for g in range(4) for i in range(31)]
    backward = [(b, a) for a, b in forward]
    low = send(hidden[:, -TAP_DILATION:], forward)
    high = send(hidden[:, :TAP_DILATION], backward)
    padded = jnp.concatenate([low, hidden, high], axis=1)
    padded_other = send(padded, CORE)

    maps = teacher_maps.reshape(4, rows, teacher_maps.shape[3])
    far_groups = jnp.stack([(1 - yh) * 2 + 1 - core, (1 - yh) * 2 + core]).astype(jnp.int32)
    near_groups = jnp.stack([yh * 2 + 1 - core, yh * 2 + core]).astype(jnp.int32)
    arrived = []
    for pieces in (pieces_a, pieces_b):
        terms = teacher_terms(order, far_groups, maps, pieces)
        far_sum = terms[1].astype(jnp.float32) + send(terms[0], CORE).astype(jnp.float32)
        arrived.append(unpack(send(pack(far_sum, jnp.max(jnp.abs(far_sum))), FAR)))
    terms = teacher_terms(order, near_groups, maps, pieces_a + pieces_b)
    near_sum = terms[1].astype(jnp.float32) + send(terms[0], CORE).astype(jnp.float32)
    target = (near_sum + jnp.concatenate(arrived, axis=1)) / 4

    preact, activated, student, pointwise = forward_pass(
        jnp.stack([order, order_other]),
        jnp.stack([core, 1 - core]).astype(jnp.int32),
        padded,
        inputs,
        pieces_w + pieces_other,
    )
    misfit = student - target
    squared = jnp.sum(misfit * misfit)
    out_grad = (misfit / channels).astype(jnp.bfloat16)
    back_grad = lax.dot_general(
        out_grad, pointwise, (((1,), (1,)), ((), ())), preferred_element_type=jnp.float32
    )
    preact_grad = (back_grad * gelu_slope(preact)).astype(jnp.bfloat16)

    pre = [padded, padded_other, half_of(preact_grad, core, 1), send(half_of(preact_grad, 1 - core, 1), CORE)]
    act = [activated, send(activated, CORE), half_of(out_grad, core, 1), send(half_of(out_grad, 1 - core, 1), CORE)]
    one = gradient_chunks((None, 1), order, act + pre)
    two = gradient_chunks((0, 2), order, pre)
    sums = []
    for own, low, high, across, peak in (one, two):
        others = [v.reshape(384, 768) for v in (low, high, across)]
        sums.append(ring_reduce(own.reshape(384, 768), others, peak[:1, :1], False))
    squares = lax.all_to_all(
        jnp.broadcast_to(after(squared, two[4]), (128, 1)), AXES, 0, 0, tiled=True
    )
    loss_mean = 0.5 * jnp.sum(squares) / (channels * total_rows)
    block = jnp.stack([finish_reduce(after(sums[0], loss_mean)), finish_reduce(sums[1])])
    other = send(block, CORE)

    def dilated_columns(v):
        return jnp.stack([v[1, :, :half], v[0, :, half:], v[1, :, half:]], axis=1)

    def pw_columns(v):
        return v[0, :, :half].reshape(2, branch // 32, half).transpose(1, 0, 2).reshape(branch // 32, branch)

    dilated_grad = in_order(core, dilated_columns(block), dilated_columns(other), 2)
    pointwise_grad = in_order(core, pw_columns(block), pw_columns(other), 1)
    return (loss_mean, dilated_grad, pointwise_grad)


def solution(mesh):
    in_specs = (
        P("teacher", "seq", None),
        P("teacher", None, "seq", None),
        P("teacher", "seq", None),
        P("seq", None, None),
        P("seq", None),
    )
    out_specs = (P(), P("seq", None, None), P("seq", None))
    return jax.shard_map(shards, mesh=mesh, in_specs=in_specs, out_specs=out_specs, check_vma=False)
```

```python
import jax
import jax.numpy as jnp
import numpy as np
from jax import lax
from jax.experimental import pallas as pl
from jax.experimental.pallas import tpu as pltpu
from jax.sharding import PartitionSpec as P

TAP_DILATION = 16
AXES = ("teacher", "seq")
SHAPE = (2, 2, 4, 2, 4)
STEPS = (0, -1, 1, 2)

slope_const = 0.7978845608
cubic_const = 0.044715


def pairs_of(move):
    pairs = []
    for source in range(int(np.prod(SHAPE))):
        at = [int(v) for v in np.unravel_index(source, SHAPE)]
        pairs.append((source, int(np.ravel_multi_index(move(*at), SHAPE))))
    return pairs


def along(first, step):
    def move(yh, core, x, yl, z):
        if (core == 0) == first:
            return (yh, core, (x + step) % 4, yl, z)
        return (yh, core, x, yl, (z + step) % 4)

    return pairs_of(move)


CORE = pairs_of(lambda yh, core, x, yl, z: (yh, 1 - core, x, yl, z))
FAR = pairs_of(lambda yh, core, x, yl, z: (1 - yh, core, x, yl, z))
NEAR = pairs_of(lambda yh, core, x, yl, z: (yh, core, x, 1 - yl, z))
FAR_NEAR = pairs_of(lambda yh, core, x, yl, z: (1 - yh, core, x, 1 - yl, z))
RING = {(first, step): along(first, step) for first in (True, False) for step in (1, -1, 2)}


def send(value, pairs):
    return lax.ppermute(value, AXES, pairs)


def gelu_tanh(value):
    inside = slope_const * (value + cubic_const * value * value * value)
    return 0.5 * value * (1.0 + jnp.tanh(inside))


def gelu_slope(value):
    inside = slope_const * (value + cubic_const * value * value * value)
    tangent = jnp.tanh(inside)
    return 0.5 * (1.0 + tangent) + 0.5 * value * (1.0 - tangent * tangent) * slope_const * (
        1.0 + 3.0 * cubic_const * value * value
    )


def block_order(core, x, yl, z):
    first = jnp.where(core == 0, x, z)
    second = jnp.where(core == 0, z, x)
    order = []
    for far in STEPS:
        for near in STEPS:
            for side in (0, 1):
                one = (first + near + 4) % 4
                two = (second + far + 4) % 4
                at_x = jnp.where(core == 0, one, two)
                at_z = jnp.where(core == 0, two, one)
                order.append((at_x * 2 + (yl + side) % 2) * 4 + at_z)
    return jnp.stack(order).astype(jnp.int32)


def concat(*values):
    return jnp.concatenate(values)


def after(value, *earlier):
    return lax.optimization_barrier((value, *earlier))[0]


def gather_near(value):
    return concat(value[None], send(value[None], NEAR))


def gather_first(value):
    return [value] + [send(value, RING[True, step]) for step in (1, -1, 2)]


def gather_second(low, high):
    return [send(part, RING[False, step]) for step in (1, -1) for part in (low, high)]


def gather_rest(low, high, second):
    return [low, high, *second, send(second[0], RING[False, 1]), send(second[3], RING[False, -1])]


def power_of(peak):
    return jnp.clip(jnp.floor(jnp.log2(jnp.maximum(peak, 1e-30))) - 13.0, -110.0, 127.0)


def pack(value):
    power = power_of(jnp.max(jnp.abs(value), axis=0, keepdims=True))
    scaled = (value * jnp.exp2(-power)).astype(jnp.float16)
    return concat(scaled, jnp.broadcast_to(power, (16, value.shape[1])).astype(jnp.float16))


def unpack(value):
    return value[:-16].astype(jnp.float32) * jnp.exp2(value[-16:-15].astype(jnp.float32))


def second_reduce(own, others):
    for chunk, step in zip(others, STEPS[1:], strict=True):
        own = own + unpack(send(chunk.astype(jnp.float16), RING[False, step]))
    return own


def sum_everywhere(value):
    value = value + send(value, CORE)
    for first in (True, False):
        value = value + send(value, RING[first, 1]) + send(value, RING[first, -1]) + send(value, RING[first, 2])
    return value + send(value, NEAR) + send(value, FAR) + send(value, FAR_NEAR)


def finish_reduce(own):
    total = own[:96]
    for i, step in enumerate(STEPS[1:]):
        total = total + send(own[96 * i + 96 : 96 * i + 192], RING[True, step])
    keep, give = total[:48], total[48:]
    return keep + send(give, NEAR) + send(keep, FAR) + send(give, FAR_NEAR)


def block_copies(order, pieces, target, sem):
    copies, place = [], 0
    for piece in pieces:
        for at in range(piece.shape[0]):
            row = pl.multiple_of(order[place] * 48, 16)
            copies.append(pltpu.make_async_copy(piece.at[at], target(row), sem))
            place += 1
    return copies


def teacher_kernel(order, groups, maps, *refs):
    count = len(refs) - 3
    out, whole, sem = refs[count:]
    width = refs[0].shape[2]

    @pl.when(pl.program_id(0) == 0)
    def _():
        copies = []
        for part in range(count // 8):
            copies += block_copies(
                order,
                refs[8 * part : 8 * part + 8],
                lambda row, part=part: whole.at[pl.ds(row, 48), part * width : (part + 1) * width],
                sem,
            )
        for copy in copies:
            copy.start()
        for copy in copies:
            copy.wait()

    out[0] = jnp.dot(maps[0], whole[...], preferred_element_type=jnp.float32).astype(jnp.bfloat16)


def teacher_terms(order, groups, maps, pieces):
    count = groups.shape[0]
    rows, depth = maps.shape[1:]
    width = pieces[0].shape[2] * len(pieces) // 8
    return pl.pallas_call(
        teacher_kernel,
        grid_spec=pltpu.PrefetchScalarGridSpec(
            num_scalar_prefetch=2,
            grid=(count,),
            in_specs=[pl.BlockSpec((1, rows, depth), lambda i, order, groups: (groups[i], 0, 0))]
            + [pl.BlockSpec(memory_space=pl.ANY)] * len(pieces),
            out_specs=pl.BlockSpec((1, rows, width), lambda i, order, groups: (i, 0, 0)),
            scratch_shapes=[pltpu.VMEM((depth, width), jnp.bfloat16), pltpu.SemaphoreType.DMA(())],
        ),
        out_shape=jax.ShapeDtypeStruct((count, rows, width), jnp.bfloat16),
        name="teacher",
    )(order, groups, maps, *pieces)


def forward_kernel(orders, cores, padded, inputs, *refs):
    pieces = refs[:16]
    preact, activated, student, pointwise, whole, sem = refs[16:]
    copies = []
    for part in range(2):
        copies += block_copies(
            orders.at[part],
            pieces[8 * part : 8 * part + 8],
            lambda row, part=part: whole.at[cores[part], pl.ds(row, 48), :],
            sem,
        )
    for copy in copies:
        copy.start()
    for copy in copies:
        copy.wait()
    for core in range(2):
        for pair in range(16):
            rows = whole[core, 96 * pair : 96 * pair + 96, 1152:].astype(jnp.float32)
            for part in range(2):
                pointwise[48 * pair : 48 * pair + 48, core * 768 + part * 384 : core * 768 + part * 384 + 384] = (
                    concat(rows[24 * part : 24 * part + 24], rows[48 + 24 * part : 72 + 24 * part]).astype(jnp.bfloat16)
                )
    for core in range(2):
        running = jnp.zeros((320, 384), jnp.float32)
        for k in range(3):
            tap = padded[:, k * TAP_DILATION : k * TAP_DILATION + 64, :].reshape(320, 1536)
            running = running + jnp.dot(
                tap, whole[core, :, k * 384 : k * 384 + 384], preferred_element_type=jnp.float32
            )
        preact[:, core * 384 : core * 384 + 384] = running
        activated[:, core * 384 : core * 384 + 384] = gelu_tanh(running).astype(jnp.bfloat16)
    student[...] = inputs[...].astype(jnp.float32) + jnp.dot(
        activated[...], pointwise[...], preferred_element_type=jnp.float32
    )


def whole_block(shape):
    return pl.BlockSpec(shape, lambda *i: (0,) * len(shape))


def forward_pass(orders, cores, padded, inputs, pieces):
    outs = [((320, 768), jnp.float32), ((320, 768), jnp.bfloat16), ((320, 1536), jnp.float32), ((768, 1536), jnp.bfloat16)]
    return pl.pallas_call(
        forward_kernel,
        grid_spec=pltpu.PrefetchScalarGridSpec(
            num_scalar_prefetch=2,
            grid=(1,),
            in_specs=[whole_block(padded.shape), whole_block(inputs.shape)]
            + [pl.BlockSpec(memory_space=pl.ANY)] * 16,
            out_specs=[whole_block(shape) for shape, _ in outs],
            scratch_shapes=[pltpu.VMEM((2, 1536, 1536), jnp.bfloat16), pltpu.SemaphoreType.DMA(())],
        ),
        out_shape=[jax.ShapeDtypeStruct(shape, kind) for shape, kind in outs],
        name="forward",
    )(orders, cores, padded, inputs, *pieces)


def gradient_kernel(taps, order, *refs):
    refs = list(refs)
    scratch = refs.pop()
    own = refs[-4]
    outs = refs[-3:]
    refs = refs[:-4]
    contract = (((0,), (0,)), ((), ()))

    def product_of(left, left_other, right, right_other):
        product = lax.dot_general(left, right, contract, preferred_element_type=jnp.float32)
        return product + lax.dot_general(left_other, right_other, contract, preferred_element_type=jnp.float32)

    def store(place, row, column, value, factor):
        slot = place % 8 * 48 + row
        rows = value.shape[0]
        if place < 8:
            own[slot : slot + rows, column : column + 384] = value
        else:
            outs[place // 8 - 1][slot : slot + rows, column : column + 384] = value * factor

    def scale(peak, column):
        power = power_of(peak)
        for out in outs:
            out[384:, column : column + 384] = jnp.broadcast_to(power, (16, 384))
        return jnp.exp2(-power)

    column = 0
    if taps[0] is None:
        activated, activated_other, out_grad, out_grad_other = refs[:4]
        refs = refs[4:]
        product = product_of(activated[...], activated_other[...], out_grad[...], out_grad_other[...])
        peak = jnp.max(jnp.abs(product), axis=0, keepdims=True)
        factor = scale(jnp.maximum(peak[:, :384], peak[:, 384:]), 0)
        scratch[:768, :] = product
        for place in range(32):
            row = pl.multiple_of(order[place] * 24, 8)
            store(place, 0, 0, scratch[pl.ds(row, 24), :384], factor)
            store(place, 24, 0, scratch[pl.ds(row, 24), 384:], factor)
        column = 384
    padded, padded_other, preact_grad, preact_grad_other = refs
    for k in taps:
        if k is None:
            continue
        low = k * TAP_DILATION
        product = product_of(
            padded[:, low : low + 64, :].reshape(320, 1536),
            padded_other[:, low : low + 64, :].reshape(320, 1536),
            preact_grad[...],
            preact_grad_other[...],
        )
        factor = scale(jnp.max(jnp.abs(product), axis=0, keepdims=True), column)
        scratch[:, :384] = product
        for place in range(32):
            row = pl.multiple_of(order[place] * 48, 8)
            store(place, 0, column, scratch[pl.ds(row, 48), :384], factor)
        column += 384


def gradient_chunks(taps, order, args):
    shapes = [(384, 768)] + [(400, 768)] * 3
    return pl.pallas_call(
        lambda *refs: gradient_kernel(taps, *refs),
        grid_spec=pltpu.PrefetchScalarGridSpec(
            num_scalar_prefetch=1,
            grid=(1,),
            in_specs=[whole_block(arg.shape) for arg in args],
            out_specs=[whole_block(shape) for shape in shapes],
            scratch_shapes=[pltpu.VMEM((1536, 768), jnp.float32)],
        ),
        out_shape=[jax.ShapeDtypeStruct(shape, jnp.float32) for shape in shapes],
        name="gradient",
    )(order, *args)


def in_order(core, own, other, axis):
    return jnp.where(
        core == 0,
        jnp.concatenate([own, other], axis=axis),
        jnp.concatenate([other, own], axis=axis),
    )


def half_of(value, index, axis):
    size = value.shape[axis] // 2
    return lax.dynamic_slice_in_dim(value, index * size, size, axis)


def shards(activations, teacher_maps, projection, dilated_weight, pointwise_weight):
    teacher = lax.axis_index("teacher")
    seq = lax.axis_index("seq")
    yh, core = teacher // 2, teacher % 2
    x, yl, z = seq // 8, (seq // 4) % 2, seq % 4
    wins, bins, channels = activations.shape
    rows = wins * bins
    total_rows = rows * 128
    branch = dilated_weight.shape[2]
    half = branch // 2
    order = block_order(core, x, yl, z)
    order_other = block_order(1 - core, x, yl, z)

    own_dil = lax.dynamic_slice_in_dim(dilated_weight, core * half, half, 2).reshape(48, 3 * half)
    own_pw = half_of(pointwise_weight, core, 1)
    own_block = jnp.concatenate([own_dil, concat(own_pw[:, :half], own_pw[:, half:])], axis=1)

    wide = channels // 2
    near = gather_near(projection[0])
    near_w = gather_near(own_block)
    first = gather_first(near)
    low_a, high_a, low_b, high_b = [
        concat(*[v[:, :, column : column + wide] for v in pair])
        for column in (0, wide)
        for pair in (first[:2], first[2:])
    ]
    second_a = gather_second(low_a, high_a)
    first_w = gather_first(after(near_w, first[1]))
    low_w, high_w = concat(*first_w[:2]), concat(*first_w[2:])
    pieces_a = gather_rest(low_a, high_a, second_a)
    second_b = gather_second(after(low_b, second_a[0]), high_b)
    pieces_b = gather_rest(low_b, high_b, second_b)
    second_w = gather_second(after(low_w, second_b[0]), high_w)
    pieces_w = gather_rest(low_w, high_w, second_w)
    pieces_other = [send(piece, CORE) for piece in pieces_w]

    inputs = activations.reshape(rows, channels)
    inputs_f = inputs.astype(jnp.float32)
    local = jnp.concatenate([jnp.sum(inputs_f, axis=0), jnp.sum(inputs_f * inputs_f, axis=0)])
    sums = sum_everywhere(after(local.reshape(24, 128), first[1])).reshape(2, channels)
    channel_mean = sums[0] / total_rows
    channel_var = sums[1] / total_rows - channel_mean * channel_mean
    normed = (inputs_f - channel_mean) * lax.rsqrt(channel_var + 1e-05)
    hidden = gelu_tanh(normed).astype(jnp.bfloat16).reshape(wins, bins, channels)
    forward = [(g * 32 + i, g * 32 + i + 1) for g in range(4) for i in range(31)]
    backward = [(b, a) for a, b in forward]
    low = send(hidden[:, -TAP_DILATION:], forward)
    high = send(hidden[:, :TAP_DILATION], backward)
    padded = jnp.concatenate([low, hidden, high], axis=1)
    padded_other = send(padded, CORE)

    maps = teacher_maps.reshape(4, rows, teacher_maps.shape[3])
    far_groups = jnp.stack([(1 - yh) * 2 + 1 - core, (1 - yh) * 2 + core]).astype(jnp.int32)
    near_groups = jnp.stack([yh * 2 + 1 - core, yh * 2 + core]).astype(jnp.int32)
    arrived = []
    for pieces in (pieces_a, pieces_b):
        terms = teacher_terms(order, far_groups, maps, pieces)
        packed = pack(terms[1].astype(jnp.float32) + send(terms[0], CORE).astype(jnp.float32))
        arrived.append(unpack(send(packed, FAR)))
    terms = teacher_terms(after(order, packed), near_groups, maps, pieces_a + pieces_b)
    near_sum = terms[1].astype(jnp.float32) + send(terms[0], CORE).astype(jnp.float32)
    target = (near_sum + jnp.concatenate(arrived, axis=1)) / 4

    preact, activated, student, pointwise = forward_pass(
        jnp.stack([order, order_other]),
        jnp.stack([core, 1 - core]).astype(jnp.int32),
        padded,
        inputs,
        pieces_w + pieces_other,
    )
    misfit = student - target
    squared = jnp.sum(misfit * misfit)
    out_grad = (misfit / channels).astype(jnp.bfloat16)
    back_grad = lax.dot_general(
        out_grad, pointwise, (((1,), (1,)), ((), ())), preferred_element_type=jnp.float32
    )
    preact_grad = (back_grad * gelu_slope(preact)).astype(jnp.bfloat16)

    pre = [padded, padded_other, half_of(preact_grad, core, 1), send(half_of(preact_grad, 1 - core, 1), CORE)]
    act = [activated, send(activated, CORE), half_of(out_grad, core, 1), send(half_of(out_grad, 1 - core, 1), CORE)]
    one = gradient_chunks((None, 1), order, act + pre)
    two = gradient_chunks((0, 2), order, pre)
    squares = sum_everywhere(jnp.broadcast_to(after(squared, two[0]), (8, 128)))
    loss_mean = 0.5 * squares[0, 0] / (channels * total_rows)
    block = jnp.stack([finish_reduce(second_reduce(v[0], v[1:])) for v in (one, two)])
    other = send(block, CORE)

    def dilated_columns(v):
        return jnp.stack([v[1, :, :half], v[0, :, half:], v[1, :, half:]], axis=1)

    def pw_columns(v):
        return v[0, :, :half].reshape(2, branch // 32, half).transpose(1, 0, 2).reshape(branch // 32, branch)

    dilated_grad = in_order(core, dilated_columns(block), dilated_columns(other), 2)
    pointwise_grad = in_order(core, pw_columns(block), pw_columns(other), 1)
    return (loss_mean, dilated_grad, pointwise_grad)


def solution(mesh):
    in_specs = (
        P("teacher", "seq", None),
        P("teacher", None, "seq", None),
        P("teacher", "seq", None),
        P("seq", None, None),
        P("seq", None),
    )
    out_specs = (P(), P("seq", None, None), P("seq", None))
    return jax.shard_map(shards, mesh=mesh, in_specs=in_specs, out_specs=out_specs, check_vma=False)
```

```python
import jax
import jax.numpy as jnp
import numpy as np
from jax import lax
from jax.experimental import pallas as pl
from jax.experimental.pallas import tpu as pltpu
from jax.sharding import PartitionSpec as P


TAP_DILATION = 16
AXES = ("teacher", "seq")
SHAPE = (2, 2, 4, 2, 4)
STEPS = (0, -1, 1, 2)

slope_const = 0.7978845608
cubic_const = 0.044715


def pairs_of(move):
    pairs = []
    for source in range(int(np.prod(SHAPE))):
        at = [int(v) for v in np.unravel_index(source, SHAPE)]
        pairs.append((source, int(np.ravel_multi_index(move(*at), SHAPE))))
    return pairs


def along(first, step):
    def move(yh, core, x, yl, z):
        if (core == 0) == first:
            return (yh, core, (x + step) % 4, yl, z)
        return (yh, core, x, yl, (z + step) % 4)

    return pairs_of(move)


CORE = pairs_of(lambda yh, core, x, yl, z: (yh, 1 - core, x, yl, z))
FAR = pairs_of(lambda yh, core, x, yl, z: (1 - yh, core, x, yl, z))
NEAR = pairs_of(lambda yh, core, x, yl, z: (yh, core, x, 1 - yl, z))
FAR_NEAR = pairs_of(lambda yh, core, x, yl, z: (1 - yh, core, x, 1 - yl, z))
RING = {(first, step): along(first, step) for first in (True, False) for step in (1, -1, 2)}


def send(value, pairs):
    return lax.ppermute(value, AXES, pairs)


def gelu_tanh(value):
    inside = slope_const * (value + cubic_const * value * value * value)
    return 0.5 * value * (1.0 + jnp.tanh(inside))


def gelu_slope(value):
    inside = slope_const * (value + cubic_const * value * value * value)
    tangent = jnp.tanh(inside)
    return 0.5 * (1.0 + tangent) + 0.5 * value * (1.0 - tangent * tangent) * slope_const * (
        1.0 + 3.0 * cubic_const * value * value
    )


def block_orders(core, x, yl, z):
    first = jnp.where(core == 0, x, z)
    second = jnp.where(core == 0, z, x)

    def block(far, near, side):
        one = (first + near + 4) % 4
        two = (second + far + 4) % 4
        at_x = jnp.where(core == 0, one, two)
        at_z = jnp.where(core == 0, two, one)
        return (at_x * 2 + (yl + side) % 2) * 4 + at_z

    sides = (0, 1)
    inner = [block(far, near, side) for far in STEPS for near in STEPS for side in sides]
    outer = [block(far, near, side) for side in sides for far in STEPS for near in STEPS]
    return jnp.stack(inner).astype(jnp.int32), jnp.stack(outer).astype(jnp.int32)


def concat(*values):
    return jnp.concatenate(values)


def after(value, *earlier):
    return lax.optimization_barrier((value, *earlier))[0]


def ring_gather(value, first):
    return [value] + [send(value, RING[first, step]) for step in (1, -1, 2)]


def power_of(peak):
    return jnp.clip(jnp.floor(jnp.log2(jnp.maximum(peak, 1e-30))) - 13.0, -110.0, 127.0)


def pack(value):
    power = power_of(jnp.max(jnp.abs(value), axis=0, keepdims=True))
    scaled = (value * jnp.exp2(-power)).astype(jnp.float16)
    return concat(scaled, jnp.broadcast_to(power, (16, value.shape[1])).astype(jnp.float16))


def unpack(value):
    return value[:-16].astype(jnp.float32) * jnp.exp2(value[-16:-15].astype(jnp.float32))


def second_reduce(own, others):
    for chunk, step in zip(others, STEPS[1:], strict=True):
        own = own + unpack(send(chunk.astype(jnp.float16), RING[False, step]))
    return own


def spread(values):
    return lax.all_to_all(values, AXES, 0, 0, tiled=True)


def finish_reduce(own):
    total = own[:96]
    for i, step in enumerate(STEPS[1:]):
        total = total + send(own[96 * i + 96 : 96 * i + 192], RING[True, step])
    keep, give = total[:48], total[48:]
    return keep + send(give, NEAR) + send(keep, FAR) + send(give, FAR_NEAR)


def block_copies(order, pieces, target, sem):
    copies, place = [], 0
    for piece in pieces:
        for at in range(piece.shape[0]):
            row = pl.multiple_of(order[place] * 48, 16)
            copies.append(pltpu.make_async_copy(piece.at[at], target(row), sem))
            place += 1
    return copies


def run_copies(copies):
    for copy in copies:
        copy.start()
    for copy in copies:
        copy.wait()


def teacher_kernel(order, groups, maps_other, maps_own, *refs):
    count = len(refs) - 4
    other, own, whole, sem = refs[count:]
    width = refs[0].shape[2]
    copies = []
    for part in range(count // 4):
        copies += block_copies(
            order,
            refs[4 * part : 4 * part + 4],
            lambda row, part=part: whole.at[pl.ds(row, 48), part * width : (part + 1) * width],
            sem,
        )
    run_copies(copies)
    for maps, out in ((maps_other, other), (maps_own, own)):
        out[...] = jnp.dot(maps[0], whole[...], preferred_element_type=jnp.float32).astype(jnp.bfloat16)


def teacher_terms(order, groups, maps, pieces):
    rows, depth = maps.shape[1:]
    width = pieces[0].shape[2] * len(pieces) // 4
    return pl.pallas_call(
        teacher_kernel,
        grid_spec=pltpu.PrefetchScalarGridSpec(
            num_scalar_prefetch=2,
            grid=(1,),
            in_specs=[
                pl.BlockSpec((1, rows, depth), lambda i, order, groups: (groups[0], 0, 0)),
                pl.BlockSpec((1, rows, depth), lambda i, order, groups: (groups[1], 0, 0)),
            ]
            + [pl.BlockSpec(memory_space=pl.ANY)] * len(pieces),
            out_specs=[whole_block((rows, width))] * 2,
            scratch_shapes=[pltpu.VMEM((depth, width), jnp.bfloat16), pltpu.SemaphoreType.DMA(())],
        ),
        out_shape=[jax.ShapeDtypeStruct((rows, width), jnp.bfloat16)] * 2,
        name="teacher",
    )(order, groups, maps, maps, *pieces)


def forward_kernel(orders, cores, padded, inputs, near_own, near_other, *refs):
    pieces = refs[:8]
    preact, activated, base_a, base_b, point_a, point_b, whole, sem = refs[8:]
    copies = []
    for part in range(2):
        copies += block_copies(
            orders.at[part],
            pieces[4 * part : 4 * part + 4],
            lambda row, part=part: whole.at[cores[part], pl.ds(row, 48), :],
            sem,
        )
    run_copies(copies)
    for core, point in enumerate((point_a, point_b)):

        def rows_of(pair, carry, core=core, point=point):
            rows = whole[core, pl.ds(pl.multiple_of(96 * pair, 96), 96), 1152:].astype(jnp.float32)
            for part in range(2):
                point[pl.ds(pl.multiple_of(48 * pair, 48), 48), part * 384 : part * 384 + 384] = concat(
                    rows[24 * part : 24 * part + 24], rows[48 + 24 * part : 72 + 24 * part]
                ).astype(jnp.bfloat16)
            return carry

        lax.fori_loop(0, 16, rows_of, 0)
    for core in range(2):
        running = jnp.zeros((320, 384), jnp.float32)
        for k in range(3):
            tap = padded[:, k * TAP_DILATION : k * TAP_DILATION + 64, :].reshape(320, 1536)
            running = running + jnp.dot(
                tap, whole[core, :, k * 384 : k * 384 + 384], preferred_element_type=jnp.float32
            )
        preact[:, core * 384 : core * 384 + 384] = running
        activated[:, core * 384 : core * 384 + 384] = gelu_tanh(running).astype(jnp.bfloat16)
    for part, (base, point) in enumerate(((base_a, point_a), (base_b, point_b))):
        lanes = slice(part * 768, part * 768 + 768)
        near = near_own[:, lanes].astype(jnp.float32) + near_other[:, lanes].astype(jnp.float32)
        base[...] = (
            inputs[:, lanes].astype(jnp.float32)
            + jnp.dot(activated[...], point[...], preferred_element_type=jnp.float32)
        ) - near * 0.25


def whole_block(shape):
    return pl.BlockSpec(shape, lambda *i: (0,) * len(shape))


def forward_pass(orders, cores, arrays, pieces):
    outs = [((320, 768), jnp.float32), ((320, 768), jnp.bfloat16)]
    outs += [((320, 768), jnp.float32)] * 2 + [((768, 768), jnp.bfloat16)] * 2
    return pl.pallas_call(
        forward_kernel,
        grid_spec=pltpu.PrefetchScalarGridSpec(
            num_scalar_prefetch=2,
            grid=(1,),
            in_specs=[whole_block(array.shape) for array in arrays]
            + [pl.BlockSpec(memory_space=pl.ANY)] * len(pieces),
            out_specs=[whole_block(shape) for shape, _ in outs],
            scratch_shapes=[pltpu.VMEM((2, 1536, 1536), jnp.bfloat16), pltpu.SemaphoreType.DMA(())],
        ),
        out_shape=[jax.ShapeDtypeStruct(shape, kind) for shape, kind in outs],
        name="forward",
    )(orders, cores, *arrays, *pieces)


def gradient_kernel(taps, order, cores, *refs):
    refs = list(refs)
    scratch = refs.pop()
    outs = refs[-4:]
    refs = refs[:-4]
    contract = (((0,), (0,)), ((), ()))

    def product_of(left, left_other, right, right_other):
        product = lax.dot_general(left, right, contract, preferred_element_type=jnp.float32)
        return product + lax.dot_general(left_other, right_other, contract, preferred_element_type=jnp.float32)

    def store(column, peak, parts, size):
        power = power_of(peak)
        for index, out in enumerate(outs):
            factor = jnp.exp2(-power) if index else None
            if index:
                out[384:, column : column + 384] = jnp.broadcast_to(power, (16, 384))

            def slot(i, carry, index=index, out=out, factor=factor):
                row = pl.multiple_of(order[8 * index + i] * size, 8)
                for part in range(parts):
                    value = scratch[pl.ds(row, size), 384 * part : 384 * part + 384]
                    to = pl.multiple_of(i * 48 + part * size, 8)
                    out[pl.ds(to, size), column : column + 384] = value * factor if index else value
                return carry

            lax.fori_loop(0, 8, slot, 0)

    column = 0
    if taps[0] is None:
        activated, activated_other, out_grad, out_grad_other = refs[:4]
        refs = refs[4:]
        product = product_of(activated[...], activated_other[...], out_grad[...], out_grad_other[...])
        scratch[:768, :] = product
        peak = jnp.max(jnp.abs(product), axis=0, keepdims=True)
        store(0, jnp.maximum(peak[:, :384], peak[:, 384:]), 2, 24)
        column = 384
    padded, padded_other, preact_grad, preact_grad_other = refs
    own_columns = preact_grad[:, pl.ds(pl.multiple_of(cores[0] * 384, 128), 384)]
    for k in taps:
        if k is None:
            continue
        low = k * TAP_DILATION
        product = product_of(
            padded[:, low : low + 64, :].reshape(320, 1536),
            padded_other[:, low : low + 64, :].reshape(320, 1536),
            own_columns,
            preact_grad_other[...],
        )
        scratch[:, :384] = product
        store(column, jnp.max(jnp.abs(product), axis=0, keepdims=True), 1, 48)
        column += 384


def gradient_chunks(taps, order, cores, args):
    shapes = [(384, 768)] + [(400, 768)] * 3
    return pl.pallas_call(
        lambda *refs: gradient_kernel(taps, *refs),
        grid_spec=pltpu.PrefetchScalarGridSpec(
            num_scalar_prefetch=2,
            grid=(1,),
            in_specs=[whole_block(arg.shape) for arg in args],
            out_specs=[whole_block(shape) for shape in shapes],
            scratch_shapes=[pltpu.VMEM((1536, 768), jnp.float32)],
        ),
        out_shape=[jax.ShapeDtypeStruct(shape, jnp.float32) for shape in shapes],
        name="gradient",
    )(order, cores, *args)


def in_order(core, own, other, axis):
    return jnp.where(
        core == 0,
        jnp.concatenate([own, other], axis=axis),
        jnp.concatenate([other, own], axis=axis),
    )


def half_of(value, index, axis):
    size = value.shape[axis] // 2
    return lax.dynamic_slice_in_dim(value, index * size, size, axis)


def shards(activations, teacher_maps, projection, dilated_weight, pointwise_weight):
    teacher = lax.axis_index("teacher")
    seq = lax.axis_index("seq")
    yh, core = teacher // 2, teacher % 2
    x, yl, z = seq // 8, (seq // 4) % 2, seq % 4
    wins, bins, channels = activations.shape
    rows = wins * bins
    total_rows = rows * 128
    branch = dilated_weight.shape[2]
    half = branch // 2
    order, order_w = block_orders(core, x, yl, z)
    order_other = block_orders(1 - core, x, yl, z)[1]
    cores = jnp.stack([core, 1 - core]).astype(jnp.int32)

    own_dil = lax.dynamic_slice_in_dim(dilated_weight, core * half, half, 2).reshape(48, 3 * half)
    own_pw = half_of(pointwise_weight, core, 1)
    own_block = jnp.concatenate([own_dil, concat(own_pw[:, :half], own_pw[:, half:])], axis=1)

    wide = channels // 2
    block = projection[0][None]
    near = concat(block, send(block, NEAR))
    first_w = concat(*ring_gather(own_block[None], True))
    first = ring_gather(near, True)
    second_w = ring_gather(first_w, False)
    low_w, high_w = concat(*second_w[:2]), concat(*second_w[2:])
    first_a, first_b = [concat(*[v[:, :, column : column + wide] for v in first]) for column in (0, wide)]
    pieces_a = ring_gather(first_a, False)
    pieces_w = [low_w, high_w, send(low_w, NEAR), send(high_w, FAR_NEAR)]
    pieces_b = ring_gather(after(first_b, pieces_a[1]), False)
    pieces_other = [send(piece, CORE) for piece in pieces_w]

    inputs = activations.reshape(rows, channels)
    inputs_f = inputs.astype(jnp.float32)
    local = jnp.stack([jnp.sum(inputs_f, axis=0), jnp.sum(inputs_f * inputs_f, axis=0)])
    local = local.reshape(2, 128, channels // 128).transpose(1, 0, 2).reshape(128, -1)
    parts = spread(after(local, first_a))
    parts = jnp.broadcast_to(jnp.sum(parts, axis=0, keepdims=True), parts.shape)
    sums = spread(parts)
    sums = sums.reshape(128, 2, channels // 128).transpose(1, 0, 2).reshape(2, channels)
    channel_mean = sums[0] / total_rows
    channel_var = sums[1] / total_rows - channel_mean * channel_mean
    normed = (inputs_f - channel_mean) * lax.rsqrt(channel_var + 1e-05)
    hidden = gelu_tanh(normed).astype(jnp.bfloat16).reshape(wins, bins, channels)
    forward = [(g * 32 + i, g * 32 + i + 1) for g in range(4) for i in range(31)]
    backward = [(b, a) for a, b in forward]
    low = send(hidden[:, -TAP_DILATION:], forward)
    high = send(hidden[:, :TAP_DILATION], backward)
    padded = jnp.concatenate([low, hidden, high], axis=1)
    padded_other = send(padded, CORE)

    maps = teacher_maps.reshape(4, rows, teacher_maps.shape[3])
    far_groups = jnp.stack([(1 - yh) * 2 + 1 - core, (1 - yh) * 2 + core]).astype(jnp.int32)
    near_groups = jnp.stack([yh * 2 + 1 - core, yh * 2 + core]).astype(jnp.int32)
    arrived = []
    for pieces in (pieces_a, pieces_b):
        other, own = teacher_terms(order, far_groups, maps, pieces)
        packed = pack(own.astype(jnp.float32) + send(other, CORE).astype(jnp.float32))
        arrived.append(send(packed, FAR))
    other, own = teacher_terms(order, near_groups, maps, pieces_a + pieces_b)

    preact, activated, *base, point_a, point_b = forward_pass(
        jnp.stack([order_w, order_other]), cores, [padded, inputs, own, send(other, CORE)], pieces_w + pieces_other
    )
    out_grads, squared = [], 0.0
    for value, terms in zip(base, arrived, strict=True):
        misfit = value - unpack(terms) * 0.25
        squared = squared + jnp.sum(misfit * misfit)
        out_grads.append((misfit / channels).astype(jnp.bfloat16))
    back_grad = sum(
        lax.dot_general(v, w, (((1,), (1,)), ((), ())), preferred_element_type=jnp.float32)
        for v, w in zip(out_grads, (point_a, point_b), strict=True)
    )
    preact_grad = (back_grad * gelu_slope(preact)).astype(jnp.bfloat16)

    out_own = jnp.where(core == 0, *out_grads)
    out_other = send(jnp.where(core == 0, *out_grads[::-1]), CORE)
    pre = [padded, padded_other, preact_grad, send(half_of(preact_grad, 1 - core, 1), CORE)]
    act = [activated, send(activated, CORE), out_own, out_other]
    one = gradient_chunks((None, 1), order, cores, act + pre)
    two = gradient_chunks((0, 2), order, cores, pre)
    sum_one = second_reduce(one[0], one[1:])
    sum_two = second_reduce(two[0], two[1:])
    squares = spread(jnp.broadcast_to(after(squared, one[0], two[0]), (128, 1)))
    loss_mean = 0.5 * jnp.sum(squares) / (channels * total_rows)
    block = jnp.stack([finish_reduce(sum_one), finish_reduce(sum_two)])
    other = send(block, CORE)

    def dilated_columns(v):
        return jnp.stack([v[1, :, :half], v[0, :, half:], v[1, :, half:]], axis=1)

    def pw_columns(v):
        return v[0, :, :half].reshape(2, branch // 32, half).transpose(1, 0, 2).reshape(branch // 32, branch)

    dilated_grad = in_order(core, dilated_columns(block), dilated_columns(other), 2)
    pointwise_grad = in_order(core, pw_columns(block), pw_columns(other), 1)
    return (loss_mean, dilated_grad, pointwise_grad)


def solution(mesh):
    in_specs = (
        P("teacher", "seq", None),
        P("teacher", None, "seq", None),
        P("teacher", "seq", None),
        P("seq", None, None),
        P("seq", None),
    )
    out_specs = (P(), P("seq", None, None), P("seq", None))

    return jax.shard_map(shards, mesh=mesh, in_specs=in_specs, out_specs=out_specs, check_vma=False)
```

```python
import jax
import jax.numpy as jnp
import numpy as np
from jax import lax
from jax.experimental import pallas as pl
from jax.experimental.pallas import tpu as pltpu
from jax.sharding import PartitionSpec as P


TAP_DILATION = 16
AXES = ("teacher", "seq")
SHAPE = (2, 2, 4, 2, 4)
STEPS = (0, -1, 1, 2)

slope_const = 0.7978845608
cubic_const = 0.044715


def pairs_of(move):
    pairs = []
    for source in range(int(np.prod(SHAPE))):
        at = [int(v) for v in np.unravel_index(source, SHAPE)]
        pairs.append((source, int(np.ravel_multi_index(move(*at), SHAPE))))
    return pairs


def along(first, step):
    def move(yh, core, x, yl, z):
        if (core == 0) == first:
            return (yh, core, (x + step) % 4, yl, z)
        return (yh, core, x, yl, (z + step) % 4)

    return pairs_of(move)


CORE = pairs_of(lambda yh, core, x, yl, z: (yh, 1 - core, x, yl, z))
FAR = pairs_of(lambda yh, core, x, yl, z: (1 - yh, core, x, yl, z))
NEAR = pairs_of(lambda yh, core, x, yl, z: (yh, core, x, 1 - yl, z))
FAR_NEAR = pairs_of(lambda yh, core, x, yl, z: (1 - yh, core, x, 1 - yl, z))
RING = {(first, step): along(first, step) for first in (True, False) for step in (1, -1, 2)}


def send(value, pairs):
    return lax.ppermute(value, AXES, pairs)


def gelu_tanh(value):
    inside = slope_const * (value + cubic_const * value * value * value)
    return 0.5 * value * (1.0 + jnp.tanh(inside))


def gelu_slope(value):
    inside = slope_const * (value + cubic_const * value * value * value)
    tangent = jnp.tanh(inside)
    return 0.5 * (1.0 + tangent) + 0.5 * value * (1.0 - tangent * tangent) * slope_const * (
        1.0 + 3.0 * cubic_const * value * value
    )


def block_orders(core, x, yl, z):
    first = jnp.where(core == 0, x, z)
    second = jnp.where(core == 0, z, x)

    def block(far, near, side):
        one = (first + near + 4) % 4
        two = (second + far + 4) % 4
        at_x = jnp.where(core == 0, one, two)
        at_z = jnp.where(core == 0, two, one)
        return (at_x * 2 + (yl + side) % 2) * 4 + at_z

    sides = (0, 1)
    inner = [block(far, near, side) for far in STEPS for near in STEPS for side in sides]
    outer = [block(far, near, side) for side in sides for far in STEPS for near in STEPS]
    return jnp.stack(inner).astype(jnp.int32), jnp.stack(outer).astype(jnp.int32)


def concat(*values):
    return jnp.concatenate(values)


def after(value, *earlier):
    return lax.optimization_barrier((value, *earlier))[0]


def ring_gather(value, first):
    return [value] + [send(value, RING[first, step]) for step in (1, -1, 2)]


def power_of(peak):
    return jnp.clip(jnp.floor(jnp.log2(jnp.maximum(peak, 1e-30))) - 13.0, -110.0, 127.0)


def pack(value):
    power = power_of(jnp.max(jnp.abs(value), axis=0, keepdims=True))
    scaled = (value * jnp.exp2(-power)).astype(jnp.float16)
    return concat(scaled, jnp.broadcast_to(power, (16, value.shape[1])).astype(jnp.float16))


def unpack(value):
    return value[:-16].astype(jnp.float32) * jnp.exp2(value[-16:-15].astype(jnp.float32))


def second_reduce(chunks):
    own = chunks[0, :-16]
    for chunk, step in zip(chunks[1:], STEPS[1:], strict=True):
        own = own + unpack(send(chunk.astype(jnp.float16), RING[False, step]))
    return own


def spread(values):
    return lax.all_to_all(values, AXES, 0, 0, tiled=True)


def finish_reduce(own):
    rows = own.shape[0] // 8
    total = own[: 2 * rows]
    for i, step in enumerate(STEPS[1:]):
        total = total + send(own[2 * rows * (i + 1) : 2 * rows * (i + 2)], RING[True, step])
    keep, give = total[:rows], total[rows:]
    return keep + send(give, NEAR) + send(keep, FAR) + send(give, FAR_NEAR)


def block_copies(order, pieces, target, sem):
    copies, place = [], 0
    for piece in pieces:
        for at in range(piece.shape[0]):
            row = pl.multiple_of(order[place] * 48, 16)
            copies.append(pltpu.make_async_copy(piece.at[at], target(row), sem))
            place += 1
    return copies


def run_copies(copies):
    for copy in copies:
        copy.start()
    for copy in copies:
        copy.wait()


def teacher_kernel(order, groups, maps_other, maps_own, *refs):
    count = len(refs) - 4
    other, own, whole, sem = refs[count:]
    width = refs[0].shape[2]
    copies = []
    for part in range(count // 4):
        copies += block_copies(
            order,
            refs[4 * part : 4 * part + 4],
            lambda row, part=part: whole.at[pl.ds(row, 48), part * width : (part + 1) * width],
            sem,
        )
    run_copies(copies)
    for maps, out in ((maps_other, other), (maps_own, own)):
        out[...] = jnp.dot(maps[0], whole[...], preferred_element_type=jnp.float32).astype(jnp.bfloat16)


def teacher_terms(order, groups, maps, pieces):
    rows, depth = maps.shape[1:]
    width = pieces[0].shape[2] * len(pieces) // 4
    return pl.pallas_call(
        teacher_kernel,
        grid_spec=pltpu.PrefetchScalarGridSpec(
            num_scalar_prefetch=2,
            grid=(1,),
            in_specs=[
                pl.BlockSpec((1, rows, depth), lambda i, order, groups: (groups[0], 0, 0)),
                pl.BlockSpec((1, rows, depth), lambda i, order, groups: (groups[1], 0, 0)),
            ]
            + [pl.BlockSpec(memory_space=pl.ANY)] * len(pieces),
            out_specs=[whole_block((rows, width))] * 2,
            scratch_shapes=[pltpu.VMEM((depth, width), jnp.bfloat16), pltpu.SemaphoreType.DMA(())],
        ),
        out_shape=[jax.ShapeDtypeStruct((rows, width), jnp.bfloat16)] * 2,
        name="teacher",
    )(order, groups, maps, maps, *pieces)


def forward_kernel(orders, cores, padded, inputs, near_own, near_other, *refs):
    pieces = refs[:8]
    preact, activated, base_a, base_b, point_a, point_b, whole, sem = refs[8:]
    copies = []
    for part in range(2):
        copies += block_copies(
            orders.at[part],
            pieces[4 * part : 4 * part + 4],
            lambda row, part=part: whole.at[cores[part], pl.ds(row, 48), :],
            sem,
        )
    run_copies(copies)
    for core, point in enumerate((point_a, point_b)):

        def rows_of(pair, carry, core=core, point=point):
            rows = whole[core, pl.ds(pl.multiple_of(96 * pair, 96), 96), 1152:].astype(jnp.float32)
            for part in range(2):
                point[pl.ds(pl.multiple_of(48 * pair, 48), 48), part * 384 : part * 384 + 384] = concat(
                    rows[24 * part : 24 * part + 24], rows[48 + 24 * part : 72 + 24 * part]
                ).astype(jnp.bfloat16)
            return carry

        lax.fori_loop(0, 16, rows_of, 0)
    for core in range(2):
        running = jnp.zeros((320, 384), jnp.float32)
        for k in range(3):
            tap = padded[:, k * TAP_DILATION : k * TAP_DILATION + 64, :].reshape(320, 1536)
            running = running + jnp.dot(
                tap, whole[core, :, k * 384 : k * 384 + 384], preferred_element_type=jnp.float32
            )
        preact[:, core * 384 : core * 384 + 384] = running
        activated[:, core * 384 : core * 384 + 384] = gelu_tanh(running).astype(jnp.bfloat16)
    for part, (base, point) in enumerate(((base_a, point_a), (base_b, point_b))):
        lanes = slice(part * 768, part * 768 + 768)
        near = near_own[:, lanes].astype(jnp.float32) + near_other[:, lanes].astype(jnp.float32)
        base[...] = (
            inputs[:, lanes].astype(jnp.float32)
            + jnp.dot(activated[...], point[...], preferred_element_type=jnp.float32)
        ) - near * 0.25


def whole_block(shape):
    return pl.BlockSpec(shape, lambda *i: (0,) * len(shape))


def forward_pass(orders, cores, arrays, pieces):
    outs = [((320, 768), jnp.float32), ((320, 768), jnp.bfloat16)]
    outs += [((320, 768), jnp.float32)] * 2 + [((768, 768), jnp.bfloat16)] * 2
    return pl.pallas_call(
        forward_kernel,
        grid_spec=pltpu.PrefetchScalarGridSpec(
            num_scalar_prefetch=2,
            grid=(1,),
            in_specs=[whole_block(array.shape) for array in arrays]
            + [pl.BlockSpec(memory_space=pl.ANY)] * len(pieces),
            out_specs=[whole_block(shape) for shape, _ in outs],
            scratch_shapes=[pltpu.VMEM((2, 1536, 1536), jnp.bfloat16), pltpu.SemaphoreType.DMA(())],
        ),
        out_shape=[jax.ShapeDtypeStruct(shape, kind) for shape, kind in outs],
        name="forward",
    )(orders, cores, *arrays, *pieces)


def turn_kernel(order, hidden, hidden_other, out, turned):
    for k in range(3):
        low = k * TAP_DILATION
        for part, source in enumerate((hidden, hidden_other)):
            tap = source[:, low : low + 64, :].reshape(320, 1536)
            turned[:, part * 320 : part * 320 + 320] = tap.astype(jnp.float32).T

        def slot(i, carry, k=k):
            row = pl.multiple_of(order[i] * 48, 16)
            to = pl.multiple_of(i * 48, 48)
            out[k, pl.ds(to, 48), :] = turned[pl.ds(row, 48), :].astype(jnp.bfloat16)
            return carry

        lax.fori_loop(0, 32, slot, 0)


def turn(order, hidden, hidden_other):
    return pl.pallas_call(
        turn_kernel,
        grid_spec=pltpu.PrefetchScalarGridSpec(
            num_scalar_prefetch=1,
            grid=(1,),
            in_specs=[whole_block(hidden.shape)] * 2,
            out_specs=whole_block((3, 1536, 640)),
            scratch_shapes=[pltpu.VMEM((1536, 640), jnp.float32)],
        ),
        out_shape=jax.ShapeDtypeStruct((3, 1536, 640), jnp.bfloat16),
        name="turn",
    )(order, hidden, hidden_other)


def turn_act_kernel(order, activated, activated_other, out, turned):
    turned[:, :320] = activated[...].astype(jnp.float32).T
    turned[:, 320:] = activated_other[...].astype(jnp.float32).T

    def pair(i, carry):
        rows = [turned[pl.ds(pl.multiple_of(order[2 * i + j] * 24, 8), 24), :] for j in range(2)]
        out[pl.ds(pl.multiple_of(i * 48, 48), 48), :] = concat(*rows).astype(jnp.bfloat16)
        return carry

    lax.fori_loop(0, 16, pair, 0)


def turn_act(order, activated, activated_other):
    return pl.pallas_call(
        turn_act_kernel,
        grid_spec=pltpu.PrefetchScalarGridSpec(
            num_scalar_prefetch=1,
            grid=(1,),
            in_specs=[whole_block(activated.shape)] * 2,
            out_specs=whole_block((768, 640)),
            scratch_shapes=[pltpu.VMEM((768, 640), jnp.float32)],
        ),
        out_shape=jax.ShapeDtypeStruct((768, 640), jnp.bfloat16),
        name="turn_act",
    )(order, activated, activated_other)


def gradient_kernel(cores, turned, right, right_other, out, both):
    taps, rows, _ = turned.shape
    width = both.shape[1]

    @pl.when(pl.program_id(0) == 0)
    def _():
        if right.shape[1] == width:
            both[:320, :] = right[...]
        else:
            both[:320, :] = right[:, pl.ds(pl.multiple_of(cores[0] * width, 128), width)]
        both[320:, :] = right_other[...]

    for k in range(taps):
        product = jnp.dot(turned[k], both[...], preferred_element_type=jnp.float32)
        power = power_of(jnp.max(jnp.abs(product), axis=0, keepdims=True))
        power = jnp.where(pl.program_id(0) == 0, 0.0, power)
        lanes = slice(k * width, (k + 1) * width)
        out[0, :rows, lanes] = product * jnp.exp2(-power)
        out[0, rows:, lanes] = jnp.broadcast_to(power, (16, width))


def gradient_chunks(cores, turned, right, right_other):
    taps, rows = turned.shape[0], turned.shape[1] // 4
    width = right_other.shape[1]
    return pl.pallas_call(
        gradient_kernel,
        grid_spec=pltpu.PrefetchScalarGridSpec(
            num_scalar_prefetch=1,
            grid=(4,),
            in_specs=[
                pl.BlockSpec((taps, rows, 640), lambda i, cores: (0, i, 0)),
                whole_block(right.shape),
                whole_block(right_other.shape),
            ],
            out_specs=pl.BlockSpec((1, rows + 16, taps * width), lambda i, cores: (i, 0, 0)),
            scratch_shapes=[pltpu.VMEM((640, width), jnp.bfloat16)],
        ),
        out_shape=jax.ShapeDtypeStruct((4, rows + 16, taps * width), jnp.float32),
        name="gradient",
    )(cores, turned, right, right_other)


def in_order(core, own, other, axis):
    return jnp.where(
        core == 0,
        jnp.concatenate([own, other], axis=axis),
        jnp.concatenate([other, own], axis=axis),
    )


def half_of(value, index, axis):
    size = value.shape[axis] // 2
    return lax.dynamic_slice_in_dim(value, index * size, size, axis)


def shards(activations, teacher_maps, projection, dilated_weight, pointwise_weight):
    teacher = lax.axis_index("teacher")
    seq = lax.axis_index("seq")
    yh, core = teacher // 2, teacher % 2
    x, yl, z = seq // 8, (seq // 4) % 2, seq % 4
    wins, bins, channels = activations.shape
    rows = wins * bins
    total_rows = rows * 128
    branch = dilated_weight.shape[2]
    half = branch // 2
    inputs = activations.reshape(rows, channels)
    forward = [(g * 32 + i, g * 32 + i + 1) for g in range(4) for i in range(31)]
    backward = [(b, a) for a, b in forward]
    low = send(activations[:, -TAP_DILATION:], forward)
    high = send(activations[:, :TAP_DILATION], backward)
    padded = jnp.concatenate([low, activations, high], axis=1)
    padded_other = send(padded, CORE)
    order, order_w = block_orders(core, x, yl, z)
    order_other = block_orders(1 - core, x, yl, z)[1]
    cores = jnp.stack([core, 1 - core]).astype(jnp.int32)

    own_dil = lax.dynamic_slice_in_dim(dilated_weight, core * half, half, 2).reshape(48, 3 * half)
    own_pw = half_of(pointwise_weight, core, 1)
    own_block = jnp.concatenate([own_dil, concat(own_pw[:, :half], own_pw[:, half:])], axis=1)

    wide = channels // 2
    block = projection[0][None]
    near = concat(block, send(block, NEAR))
    first_w = concat(*ring_gather(own_block[None], True))
    first = ring_gather(near, True)
    second_w = ring_gather(first_w, False)
    low_w, high_w = concat(*second_w[:2]), concat(*second_w[2:])
    first_a, first_b = [concat(*[v[:, :, column : column + wide] for v in first]) for column in (0, wide)]
    pieces_a = ring_gather(first_a, False)
    pieces_w = [low_w, high_w, send(low_w, NEAR), send(high_w, FAR_NEAR)]
    pieces_b = ring_gather(after(first_b, pieces_a[1]), False)
    pieces_other = [send(piece, CORE) for piece in pieces_w[:2]]
    pieces_other += [send(piece, CORE) for piece in pieces_w[2:]]

    inputs_f = inputs.astype(jnp.float32)
    local = jnp.stack([jnp.sum(inputs_f, axis=0), jnp.sum(inputs_f * inputs_f, axis=0)])
    local = local.reshape(2, 128, channels // 128).transpose(1, 0, 2).reshape(128, -1)
    parts = spread(local)
    parts = jnp.broadcast_to(jnp.sum(parts, axis=0, keepdims=True), parts.shape)
    sums = spread(parts)
    sums = sums.reshape(128, 2, channels // 128).transpose(1, 0, 2).reshape(2, channels)
    channel_mean = sums[0] / total_rows
    channel_var = sums[1] / total_rows - channel_mean * channel_mean
    scale = lax.rsqrt(channel_var + 1e-05)
    place = lax.broadcasted_iota(jnp.int32, (1, bins + 2 * TAP_DILATION, 1), 1) + seq * bins
    inside = (place >= TAP_DILATION) & (place < 32 * bins + TAP_DILATION)

    def hidden_of(value):
        normed = (value.astype(jnp.float32) - channel_mean) * scale
        return jnp.where(inside, gelu_tanh(normed), 0.0).astype(jnp.bfloat16)

    hidden, hidden_other = hidden_of(padded), hidden_of(padded_other)

    maps = teacher_maps.reshape(4, rows, teacher_maps.shape[3])
    far_groups = jnp.stack([(1 - yh) * 2 + 1 - core, (1 - yh) * 2 + core]).astype(jnp.int32)
    near_groups = jnp.stack([yh * 2 + 1 - core, yh * 2 + core]).astype(jnp.int32)
    arrived = []
    for pieces in (pieces_a, pieces_b):
        other, own = teacher_terms(order, far_groups, maps, pieces)
        packed = pack(own.astype(jnp.float32) + send(other, CORE).astype(jnp.float32))
        arrived.append(send(packed, FAR))
    other, own = teacher_terms(order, near_groups, maps, pieces_a + pieces_b)

    preact, activated, *base, point_a, point_b = forward_pass(
        jnp.stack([order_w, order_other]), cores, [hidden, inputs, own, send(other, CORE)], pieces_w + pieces_other
    )
    out_grads, squared = [], 0.0
    for value, terms in zip(base, arrived, strict=True):
        misfit = value - unpack(terms) * 0.25
        squared = squared + jnp.sum(misfit * misfit)
        out_grads.append((misfit / channels).astype(jnp.bfloat16))
    back_grad = sum(
        lax.dot_general(v, w, (((1,), (1,)), ((), ())), preferred_element_type=jnp.float32)
        for v, w in zip(out_grads, (point_a, point_b), strict=True)
    )
    preact_grad = (back_grad * gelu_slope(preact)).astype(jnp.bfloat16)

    turned = turn(order, hidden, hidden_other)
    turned_act = turn_act(order, activated, send(activated, CORE))
    out_own = jnp.where(core == 0, *out_grads)
    out_other = send(jnp.where(core == 0, *out_grads[::-1]), CORE)
    pw_chunks = gradient_chunks(cores, turned_act[None], out_own, out_other)
    pw_sum = second_reduce(pw_chunks)
    pre_other = send(half_of(preact_grad, 1 - core, 1), CORE)
    tap_chunks = gradient_chunks(cores, turned, preact_grad, pre_other)
    tap_sum = second_reduce(tap_chunks)
    squares = spread(jnp.broadcast_to(after(squared, pw_chunks, tap_chunks), (128, 1)))
    loss_mean = 0.5 * jnp.sum(squares) / (channels * total_rows)
    pw_own = finish_reduce(pw_sum)
    pointwise_grad = in_order(core, pw_own, send(pw_own, CORE), 1)
    taps_own = finish_reduce(tap_sum)
    taps_other = send(taps_own, CORE)
    dilated_grad = in_order(
        core, taps_own.reshape(48, 3, half), taps_other.reshape(48, 3, half), 2
    )
    return (loss_mean, dilated_grad, pointwise_grad)


def solution(mesh):
    in_specs = (
        P("teacher", "seq", None),
        P("teacher", None, "seq", None),
        P("teacher", "seq", None),
        P("seq", None, None),
        P("seq", None),
    )
    out_specs = (P(), P("seq", None, None), P("seq", None))

    return jax.shard_map(shards, mesh=mesh, in_specs=in_specs, out_specs=out_specs, check_vma=False)
```

```python
import jax
import jax.numpy as jnp
import numpy as np
from jax import lax
from jax.experimental import pallas as pl
from jax.experimental.pallas import tpu as pltpu
from jax.sharding import PartitionSpec as P


TAP_DILATION = 16
AXES = ("teacher", "seq")
SHAPE = (2, 2, 4, 2, 4)
STEPS = (0, -1, 1, 2)

slope_const = 0.7978845608
cubic_const = 0.044715


def pairs_of(move):
    pairs = []
    for source in range(int(np.prod(SHAPE))):
        at = [int(v) for v in np.unravel_index(source, SHAPE)]
        pairs.append((source, int(np.ravel_multi_index(move(*at), SHAPE))))
    return pairs


def along(first, step):
    def move(yh, core, x, yl, z):
        if (core == 0) == first:
            return (yh, core, (x + step) % 4, yl, z)
        return (yh, core, x, yl, (z + step) % 4)

    return pairs_of(move)


CORE = pairs_of(lambda yh, core, x, yl, z: (yh, 1 - core, x, yl, z))
FAR = pairs_of(lambda yh, core, x, yl, z: (1 - yh, core, x, yl, z))
NEAR = pairs_of(lambda yh, core, x, yl, z: (yh, core, x, 1 - yl, z))
FAR_NEAR = pairs_of(lambda yh, core, x, yl, z: (1 - yh, core, x, 1 - yl, z))
RING = {(first, step): along(first, step) for first in (True, False) for step in (1, -1, 2)}


def send(value, pairs):
    return lax.ppermute(value, AXES, pairs)


def gelu_tanh(value):
    inside = slope_const * (value + cubic_const * value * value * value)
    return 0.5 * value * (1.0 + jnp.tanh(inside))


def gelu_slope(value):
    inside = slope_const * (value + cubic_const * value * value * value)
    tangent = jnp.tanh(inside)
    return 0.5 * (1.0 + tangent) + 0.5 * value * (1.0 - tangent * tangent) * slope_const * (
        1.0 + 3.0 * cubic_const * value * value
    )


def block_orders(core, x, yl, z):
    first = jnp.where(core == 0, x, z)
    second = jnp.where(core == 0, z, x)

    def block(far, near, side):
        one = (first + near + 4) % 4
        two = (second + far + 4) % 4
        at_x = jnp.where(core == 0, one, two)
        at_z = jnp.where(core == 0, two, one)
        return (at_x * 2 + (yl + side) % 2) * 4 + at_z

    sides = (0, 1)
    inner = [block(far, near, side) for far in STEPS for near in STEPS for side in sides]
    outer = [block(far, near, side) for side in sides for far in STEPS for near in STEPS]
    return jnp.stack(inner).astype(jnp.int32), jnp.stack(outer).astype(jnp.int32)


def concat(*values):
    return jnp.concatenate(values)


def after(value, *earlier):
    return lax.optimization_barrier((value, *earlier))[0]


def ring_gather(value, first):
    return [value] + [send(value, RING[first, step]) for step in (1, -1, 2)]


def power_of(peak):
    return jnp.clip(jnp.floor(jnp.log2(jnp.maximum(peak, 1e-30))) - 13.0, -110.0, 127.0)


def pack(value, power):
    scaled = (value * jnp.exp2(-power)).astype(jnp.float16)
    return concat(scaled, jnp.broadcast_to(power, (16, value.shape[1])).astype(jnp.float16))


def power_in(packed):
    return packed[-16:-15].astype(jnp.float32)


def unpack(packed):
    return packed[:-16].astype(jnp.float32) * jnp.exp2(power_in(packed))


def sum_everywhere(value):
    value = value + send(value, CORE)
    for first in (True, False):
        value = value + send(value, RING[first, 1]) + send(value, RING[first, -1]) + send(value, RING[first, 2])
    return value + send(value, NEAR) + send(value, FAR) + send(value, FAR_NEAR)


def add_up(own, own_power, arrived):
    power = own_power
    for packed in arrived:
        own = own + unpack(packed)
        power = jnp.maximum(power, power_in(packed))
    return own, power + 2.0


def finish_reduce(own, power):
    rows = own.shape[0] // 8
    arrived = [
        send(pack(own[2 * rows * (i + 1) : 2 * rows * (i + 2)], power), RING[True, step])
        for i, step in enumerate(STEPS[1:])
    ]
    own, power = add_up(own[: 2 * rows], power, arrived)
    keep, give = pack(own[:rows], power), pack(own[rows:], power)
    arrived = [send(give, NEAR), send(keep, FAR), send(give, FAR_NEAR)]
    return add_up(own[:rows], power, arrived)[0]


def block_copies(order, pieces, target, sem):
    copies, place = [], 0
    for piece in pieces:
        for at in range(piece.shape[0]):
            row = pl.multiple_of(order[place] * 48, 16)
            copies.append(pltpu.make_async_copy(piece.at[at], target(row), sem))
            place += 1
    return copies


def run_copies(copies):
    for copy in copies:
        copy.start()
    for copy in copies:
        copy.wait()


def teacher_kernel(order, groups, maps_other, maps_own, *refs):
    count = len(refs) - 4
    other, own, whole, sem = refs[count:]
    width = refs[0].shape[2]
    copies = []
    for part in range(count // 4):
        copies += block_copies(
            order,
            refs[4 * part : 4 * part + 4],
            lambda row, part=part: whole.at[pl.ds(row, 48), part * width : (part + 1) * width],
            sem,
        )
    run_copies(copies)
    for maps, out in ((maps_other, other), (maps_own, own)):
        out[...] = jnp.dot(maps[0], whole[...], preferred_element_type=jnp.float32).astype(jnp.bfloat16)


def teacher_terms(order, groups, maps, pieces):
    rows, depth = maps.shape[1:]
    width = pieces[0].shape[2] * len(pieces) // 4
    return pl.pallas_call(
        teacher_kernel,
        grid_spec=pltpu.PrefetchScalarGridSpec(
            num_scalar_prefetch=2,
            grid=(1,),
            in_specs=[
                pl.BlockSpec((1, rows, depth), lambda i, order, groups: (groups[0], 0, 0)),
                pl.BlockSpec((1, rows, depth), lambda i, order, groups: (groups[1], 0, 0)),
            ]
            + [pl.BlockSpec(memory_space=pl.ANY)] * len(pieces),
            out_specs=[whole_block((rows, width))] * 2,
            scratch_shapes=[pltpu.VMEM((depth, width), jnp.bfloat16), pltpu.SemaphoreType.DMA(())],
        ),
        out_shape=[jax.ShapeDtypeStruct((rows, width), jnp.bfloat16)] * 2,
        name="teacher",
    )(order, groups, maps, maps, *pieces)


def forward_kernel(orders, cores, padded, inputs, near_own, near_other, *refs):
    pieces = refs[:8]
    preact, activated, base_a, base_b, point_a, point_b, whole, sem = refs[8:]
    copies = []
    for part in range(2):
        copies += block_copies(
            orders.at[part],
            pieces[4 * part : 4 * part + 4],
            lambda row, part=part: whole.at[cores[part], pl.ds(row, 48), :],
            sem,
        )
    run_copies(copies)
    for core, point in enumerate((point_a, point_b)):

        def rows_of(pair, carry, core=core, point=point):
            rows = whole[core, pl.ds(pl.multiple_of(96 * pair, 96), 96), 1152:].astype(jnp.float32)
            for part in range(2):
                point[pl.ds(pl.multiple_of(48 * pair, 48), 48), part * 384 : part * 384 + 384] = concat(
                    rows[24 * part : 24 * part + 24], rows[48 + 24 * part : 72 + 24 * part]
                ).astype(jnp.bfloat16)
            return carry

        lax.fori_loop(0, 16, rows_of, 0)
    for core in range(2):
        running = jnp.zeros((320, 384), jnp.float32)
        for k in range(3):
            tap = padded[:, k * TAP_DILATION : k * TAP_DILATION + 64, :].reshape(320, 1536)
            running = running + jnp.dot(
                tap, whole[core, :, k * 384 : k * 384 + 384], preferred_element_type=jnp.float32
            )
        preact[:, core * 384 : core * 384 + 384] = running
        activated[:, core * 384 : core * 384 + 384] = gelu_tanh(running).astype(jnp.bfloat16)
    for part, (base, point) in enumerate(((base_a, point_a), (base_b, point_b))):
        lanes = slice(part * 768, part * 768 + 768)
        near = near_own[:, lanes].astype(jnp.float32) + near_other[:, lanes].astype(jnp.float32)
        base[...] = (
            inputs[:, lanes].astype(jnp.float32)
            + jnp.dot(activated[...], point[...], preferred_element_type=jnp.float32)
        ) - near * 0.25


def whole_block(shape):
    return pl.BlockSpec(shape, lambda *i: (0,) * len(shape))


def forward_pass(orders, cores, arrays, pieces):
    outs = [((320, 768), jnp.float32), ((320, 768), jnp.bfloat16)]
    outs += [((320, 768), jnp.float32)] * 2 + [((768, 768), jnp.bfloat16)] * 2
    return pl.pallas_call(
        forward_kernel,
        grid_spec=pltpu.PrefetchScalarGridSpec(
            num_scalar_prefetch=2,
            grid=(1,),
            in_specs=[whole_block(array.shape) for array in arrays]
            + [pl.BlockSpec(memory_space=pl.ANY)] * len(pieces),
            out_specs=[whole_block(shape) for shape, _ in outs],
            scratch_shapes=[pltpu.VMEM((2, 1536, 1536), jnp.bfloat16), pltpu.SemaphoreType.DMA(())],
        ),
        out_shape=[jax.ShapeDtypeStruct(shape, kind) for shape, kind in outs],
        name="forward",
    )(orders, cores, *arrays, *pieces)


def turn_kernel(order, hidden, hidden_other, out, turned):
    for k in range(3):
        low = k * TAP_DILATION
        for part, source in enumerate((hidden, hidden_other)):
            tap = source[:, low : low + 64, :].reshape(320, 1536)
            turned[:, part * 320 : part * 320 + 320] = tap.astype(jnp.float32).T

        def slot(i, carry, k=k):
            row = pl.multiple_of(order[i] * 48, 16)
            to = pl.multiple_of(i * 48, 48)
            out[k, pl.ds(to, 48), :] = turned[pl.ds(row, 48), :].astype(jnp.bfloat16)
            return carry

        lax.fori_loop(0, 32, slot, 0)


def turn(order, hidden, hidden_other):
    return pl.pallas_call(
        turn_kernel,
        grid_spec=pltpu.PrefetchScalarGridSpec(
            num_scalar_prefetch=1,
            grid=(1,),
            in_specs=[whole_block(hidden.shape)] * 2,
            out_specs=whole_block((3, 1536, 640)),
            scratch_shapes=[pltpu.VMEM((1536, 640), jnp.float32)],
        ),
        out_shape=jax.ShapeDtypeStruct((3, 1536, 640), jnp.bfloat16),
        name="turn",
    )(order, hidden, hidden_other)


def turn_act_kernel(order, activated, activated_other, out, turned):
    turned[:, :320] = activated[...].astype(jnp.float32).T
    turned[:, 320:] = activated_other[...].astype(jnp.float32).T

    def pair(i, carry):
        rows = [turned[pl.ds(pl.multiple_of(order[2 * i + j] * 24, 8), 24), :] for j in range(2)]
        out[pl.ds(pl.multiple_of(i * 48, 48), 48), :] = concat(*rows).astype(jnp.bfloat16)
        return carry

    lax.fori_loop(0, 16, pair, 0)


def turn_act(order, activated, activated_other):
    return pl.pallas_call(
        turn_act_kernel,
        grid_spec=pltpu.PrefetchScalarGridSpec(
            num_scalar_prefetch=1,
            grid=(1,),
            in_specs=[whole_block(activated.shape)] * 2,
            out_specs=whole_block((768, 640)),
            scratch_shapes=[pltpu.VMEM((768, 640), jnp.float32)],
        ),
        out_shape=jax.ShapeDtypeStruct((768, 640), jnp.bfloat16),
        name="turn_act",
    )(order, activated, activated_other)


def gradient_kernel(turned, turned_act, pre, out_grad, out):
    def store(lanes, product, power):
        factor = jnp.exp2(-power)
        out[384:, lanes] = jnp.broadcast_to(power, (16, 384))
        for first, size, part in product:
            out[first : first + size, lanes] = part * factor

    for k in range(3):
        product = jnp.dot(turned[k], pre[...], preferred_element_type=jnp.float32)
        power = power_of(jnp.max(jnp.abs(product), axis=0, keepdims=True))
        store(slice(384 * k, 384 * k + 384), [(0, 384, product)], power)
    product = jnp.dot(turned_act[...], out_grad[...], preferred_element_type=jnp.float32)
    peak = jnp.max(jnp.abs(product), axis=0, keepdims=True)
    parts = [
        (48 * i + 24 * part, 24, product[24 * i : 24 * i + 24, 384 * part : 384 * part + 384])
        for i in range(8)
        for part in range(2)
    ]
    store(slice(1152, 1536), parts, power_of(jnp.maximum(peak[:, :384], peak[:, 384:])))


def gradient_chunk(index, turned, turned_act, pre, out_grad):
    return pl.pallas_call(
        gradient_kernel,
        grid=(1,),
        in_specs=[
            pl.BlockSpec((3, 384, 640), lambda i: (0, index, 0)),
            pl.BlockSpec((192, 640), lambda i: (index, 0)),
            whole_block(pre.shape),
            whole_block(out_grad.shape),
        ],
        out_specs=whole_block((400, 1536)),
        out_shape=jax.ShapeDtypeStruct((400, 1536), jnp.float32),
        name="gradient",
    )(turned, turned_act, pre, out_grad)


def in_order(core, own, other, axis):
    return jnp.where(
        core == 0,
        jnp.concatenate([own, other], axis=axis),
        jnp.concatenate([other, own], axis=axis),
    )


def half_of(value, index, axis):
    size = value.shape[axis] // 2
    return lax.dynamic_slice_in_dim(value, index * size, size, axis)


def shards(activations, teacher_maps, projection, dilated_weight, pointwise_weight):
    teacher = lax.axis_index("teacher")
    seq = lax.axis_index("seq")
    yh, core = teacher // 2, teacher % 2
    x, yl, z = seq // 8, (seq // 4) % 2, seq % 4
    wins, bins, channels = activations.shape
    rows = wins * bins
    total_rows = rows * 128
    branch = dilated_weight.shape[2]
    half = branch // 2
    inputs = activations.reshape(rows, channels)
    forward = [(g * 32 + i, g * 32 + i + 1) for g in range(4) for i in range(31)]
    backward = [(b, a) for a, b in forward]
    low = send(activations[:, -TAP_DILATION:], forward)
    high = send(activations[:, :TAP_DILATION], backward)
    padded = jnp.concatenate([low, activations, high], axis=1)
    padded_other = send(padded, CORE)
    order, order_w = block_orders(core, x, yl, z)
    order_other = block_orders(1 - core, x, yl, z)[1]
    cores = jnp.stack([core, 1 - core]).astype(jnp.int32)

    own_dil = lax.dynamic_slice_in_dim(dilated_weight, core * half, half, 2).reshape(48, 3 * half)
    own_pw = half_of(pointwise_weight, core, 1)
    own_block = jnp.concatenate([own_dil, concat(own_pw[:, :half], own_pw[:, half:])], axis=1)

    wide = channels // 2
    block = projection[0][None]
    near = concat(block, send(block, NEAR))
    first_w = concat(*ring_gather(own_block[None], True))
    first = ring_gather(near, True)
    second_w = ring_gather(first_w, False)
    low_w, high_w = concat(*second_w[:2]), concat(*second_w[2:])
    first_a, first_b = [concat(*[v[:, :, column : column + wide] for v in first]) for column in (0, wide)]
    pieces_a = ring_gather(first_a, False)
    pieces_w = [low_w, high_w, send(low_w, NEAR), send(high_w, FAR_NEAR)]
    pieces_b = ring_gather(first_b, False)
    pieces_other = [send(piece, CORE) for piece in pieces_w[:2]]
    pieces_other += [send(piece, CORE) for piece in pieces_w[2:]]

    inputs_f = inputs.astype(jnp.float32)
    local = jnp.concatenate([jnp.sum(inputs_f, axis=0), jnp.sum(inputs_f * inputs_f, axis=0)])
    sums = sum_everywhere(local.reshape(24, 128)).reshape(2, channels)
    channel_mean = sums[0] / total_rows
    channel_var = sums[1] / total_rows - channel_mean * channel_mean
    scale = lax.rsqrt(channel_var + 1e-05)
    place = lax.broadcasted_iota(jnp.int32, (1, bins + 2 * TAP_DILATION, 1), 1) + seq * bins
    inside = (place >= TAP_DILATION) & (place < 32 * bins + TAP_DILATION)

    def hidden_of(value):
        normed = (value.astype(jnp.float32) - channel_mean) * scale
        return jnp.where(inside, gelu_tanh(normed), 0.0).astype(jnp.bfloat16)

    hidden, hidden_other = hidden_of(padded), hidden_of(padded_other)

    maps = teacher_maps.reshape(4, rows, teacher_maps.shape[3])
    far_groups = jnp.stack([(1 - yh) * 2 + 1 - core, (1 - yh) * 2 + core]).astype(jnp.int32)
    near_groups = jnp.stack([yh * 2 + 1 - core, yh * 2 + core]).astype(jnp.int32)
    arrived = []
    for pieces in (pieces_a, pieces_b):
        other, own = teacher_terms(order, far_groups, maps, pieces)
        far_sum = own.astype(jnp.float32) + send(other, CORE).astype(jnp.float32)
        packed = pack(far_sum, power_of(jnp.max(jnp.abs(far_sum), axis=0, keepdims=True)))
        arrived.append(send(packed, FAR))
    other, own = teacher_terms(order, near_groups, maps, pieces_a + pieces_b)

    preact, activated, *base, point_a, point_b = forward_pass(
        jnp.stack([order_w, order_other]), cores, [hidden, inputs, own, send(other, CORE)], pieces_w + pieces_other
    )
    out_grads, squared = [], 0.0
    for value, terms in zip(base, arrived, strict=True):
        misfit = value - unpack(terms) * 0.25
        squared = squared + jnp.sum(misfit * misfit)
        out_grads.append((misfit / channels).astype(jnp.bfloat16))
    back_grad = sum(
        lax.dot_general(v, w, (((1,), (1,)), ((), ())), preferred_element_type=jnp.float32)
        for v, w in zip(out_grads, (point_a, point_b), strict=True)
    )
    preact_grad = (back_grad * gelu_slope(preact)).astype(jnp.bfloat16)

    turned = turn(order, hidden, hidden_other)
    turned_act = turn_act(order, activated, send(activated, CORE))
    out_own = jnp.where(core == 0, *out_grads)
    out_both = concat(out_own, send(jnp.where(core == 0, *out_grads[::-1]), CORE))
    pre_both = concat(
        half_of(preact_grad, core, 1), send(half_of(preact_grad, 1 - core, 1), CORE)
    )
    arrived = []
    for index in (3, 1, 2, 0):
        chunk = gradient_chunk(index, turned, turned_act, pre_both, out_both)
        if index:
            arrived.append(send(chunk.astype(jnp.float16), RING[False, STEPS[index]]))
    squares = sum_everywhere(jnp.broadcast_to(after(squared, chunk), (8, 128)))
    loss_mean = 0.5 * squares[0, 0] / (channels * total_rows)
    block = finish_reduce(*add_up(unpack(chunk), power_in(chunk), arrived))
    other = send(block, CORE)

    def dilated_columns(v):
        return v[:, : 3 * half].reshape(48, 3, half)

    def pw_columns(v):
        v = v[:, 3 * half :].reshape(2, branch // 32, half)
        return v.transpose(1, 0, 2).reshape(branch // 32, branch)

    dilated_grad = in_order(core, dilated_columns(block), dilated_columns(other), 2)
    pointwise_grad = in_order(core, pw_columns(block), pw_columns(other), 1)
    return (loss_mean, dilated_grad, pointwise_grad)


def solution(mesh):
    in_specs = (
        P("teacher", "seq", None),
        P("teacher", None, "seq", None),
        P("teacher", "seq", None),
        P("seq", None, None),
        P("seq", None),
    )
    out_specs = (P(), P("seq", None, None), P("seq", None))

    return jax.shard_map(shards, mesh=mesh, in_specs=in_specs, out_specs=out_specs, check_vma=False)
```

```python
import jax
import jax.numpy as jnp
import numpy as np
from jax import lax
from jax.experimental import pallas as pl
from jax.experimental.pallas import tpu as pltpu
from jax.sharding import PartitionSpec as P


TAP_DILATION = 16
AXES = ("teacher", "seq")
SHAPE = (2, 2, 4, 2, 4)
STEPS = (0, -1, 1, 2)

slope_const = 0.7978845608
cubic_const = 0.044715


def pairs_of(move):
    pairs = []
    for source in range(int(np.prod(SHAPE))):
        at = [int(v) for v in np.unravel_index(source, SHAPE)]
        pairs.append((source, int(np.ravel_multi_index(move(*at), SHAPE))))
    return pairs


def along(first, step):
    def move(yh, core, x, yl, z):
        if (core == 0) == first:
            return (yh, core, (x + step) % 4, yl, z)
        return (yh, core, x, yl, (z + step) % 4)

    return pairs_of(move)


CORE = pairs_of(lambda yh, core, x, yl, z: (yh, 1 - core, x, yl, z))
FAR = pairs_of(lambda yh, core, x, yl, z: (1 - yh, core, x, yl, z))
NEAR = pairs_of(lambda yh, core, x, yl, z: (yh, core, x, 1 - yl, z))
FAR_NEAR = pairs_of(lambda yh, core, x, yl, z: (1 - yh, core, x, 1 - yl, z))
RING = {(first, step): along(first, step) for first in (True, False) for step in (1, -1, 2)}


def send(value, pairs):
    return lax.ppermute(value, AXES, pairs)


def gelu_tanh(value):
    inside = slope_const * (value + cubic_const * value * value * value)
    return 0.5 * value * (1.0 + jnp.tanh(inside))


def gelu_slope(value):
    inside = slope_const * (value + cubic_const * value * value * value)
    tangent = jnp.tanh(inside)
    return 0.5 * (1.0 + tangent) + 0.5 * value * (1.0 - tangent * tangent) * slope_const * (
        1.0 + 3.0 * cubic_const * value * value
    )


def block_orders(core, x, yl, z):
    first = jnp.where(core == 0, x, z)
    second = jnp.where(core == 0, z, x)

    def block(far, near, side):
        one = (first + near + 4) % 4
        two = (second + far + 4) % 4
        at_x = jnp.where(core == 0, one, two)
        at_z = jnp.where(core == 0, two, one)
        return (at_x * 2 + (yl + side) % 2) * 4 + at_z

    sides = (0, 1)
    inner = [block(far, near, side) for far in STEPS for near in STEPS for side in sides]
    outer = [block(far, near, side) for side in sides for far in STEPS for near in STEPS]
    return jnp.stack(inner).astype(jnp.int32), jnp.stack(outer).astype(jnp.int32)


def concat(*values):
    return jnp.concatenate(values)


def after(value, *earlier):
    return lax.optimization_barrier((value, *earlier))[0]


def ring_gather(value, first):
    return [value] + [send(value, RING[first, step]) for step in (1, -1, 2)]


def power_of(peak):
    return jnp.clip(jnp.floor(jnp.log2(jnp.maximum(peak, 1e-30))) - 13.0, -110.0, 127.0)


def pack(value, power):
    scaled = (value * jnp.exp2(-power)).astype(jnp.float16)
    return concat(scaled, jnp.broadcast_to(power, (16, value.shape[1])).astype(jnp.float16))


def power_in(packed):
    return packed[-16:-15].astype(jnp.float32)


def unpack(packed):
    return packed[:-16].astype(jnp.float32) * jnp.exp2(power_in(packed))


def sum_everywhere(value):
    value = value + send(value, CORE)
    for first in (True, False):
        value = value + send(value, RING[first, 1]) + send(value, RING[first, -1]) + send(value, RING[first, 2])
    return value + send(value, NEAR) + send(value, FAR) + send(value, FAR_NEAR)


def add_up(own, own_power, arrived):
    power = own_power
    for packed in arrived:
        own = own + unpack(packed)
        power = jnp.maximum(power, power_in(packed))
    return own, power + 2.0


def finish_reduce(own, power):
    rows = own.shape[0] // 8
    arrived = [
        send(pack(own[2 * rows * (i + 1) : 2 * rows * (i + 2)], power), RING[True, step])
        for i, step in enumerate(STEPS[1:])
    ]
    own, power = add_up(own[: 2 * rows], power, arrived)
    keep, give = pack(own[:rows], power), pack(own[rows:], power)
    arrived = [send(give, NEAR), send(keep, FAR), send(give, FAR_NEAR)]
    return add_up(own[:rows], power, arrived)[0]


def block_copies(order, pieces, target, sem):
    copies, place = [], 0
    for piece in pieces:
        for at in range(piece.shape[0]):
            row = pl.multiple_of(order[place] * 48, 16)
            copies.append(pltpu.make_async_copy(piece.at[at], target(row), sem))
            place += 1
    return copies


def run_copies(copies):
    for copy in copies:
        copy.start()
    for copy in copies:
        copy.wait()


def teacher_kernel(order, groups, maps_other, maps_own, *refs):
    count = len(refs) - 4
    other, own, whole, sem = refs[count:]
    width = whole.shape[1]
    each = refs[0].shape[2]
    copies = []
    for part in range(count // 4):
        copies += block_copies(
            order,
            refs[4 * part : 4 * part + 4],
            lambda row, part=part: whole.at[pl.ds(row, 48), part * each : (part + 1) * each],
            sem,
        )
    run_copies(copies)
    for maps, out in ((maps_other, other), (maps_own, own)):
        terms = jnp.dot(maps[0], whole[...], preferred_element_type=jnp.float32)
        out[:320, :] = terms.astype(jnp.bfloat16)
        if out.shape[0] > 320:
            power = power_of(jnp.max(jnp.abs(terms), axis=0, keepdims=True)) + 1.0
            out[320:, :] = jnp.broadcast_to(power, (16, width)).astype(jnp.bfloat16)


def teacher_terms(order, groups, maps, pieces, extra):
    rows, depth = maps.shape[1:]
    width = pieces[0].shape[2] * len(pieces) // 4
    return pl.pallas_call(
        teacher_kernel,
        grid_spec=pltpu.PrefetchScalarGridSpec(
            num_scalar_prefetch=2,
            grid=(1,),
            in_specs=[
                pl.BlockSpec((1, rows, depth), lambda i, order, groups: (groups[0], 0, 0)),
                pl.BlockSpec((1, rows, depth), lambda i, order, groups: (groups[1], 0, 0)),
            ]
            + [pl.BlockSpec(memory_space=pl.ANY)] * len(pieces),
            out_specs=[whole_block((rows + extra, width))] * 2,
            scratch_shapes=[pltpu.VMEM((depth, width), jnp.bfloat16), pltpu.SemaphoreType.DMA(())],
        ),
        out_shape=[jax.ShapeDtypeStruct((rows + extra, width), jnp.bfloat16)] * 2,
        compiler_params=pltpu.CompilerParams(vmem_limit_bytes=30 * 2**20),
        name="teacher",
    )(order, groups, maps, maps, *pieces)


def forward_kernel(orders, cores, hidden, inputs, near_own, near_other, *refs):
    pieces = refs[:8]
    preact, activated, base_a, base_b, point_a, point_b, whole, point, sems = refs[8:]
    copies = [
        block_copies(
            orders.at[part],
            pieces[4 * part : 4 * part + 4],
            lambda row, part=part: whole.at[part, pl.ds(row, 48), :],
            sems.at[part],
        )
        for part in range(2)
    ]
    for part in range(2):
        for copy in copies[part]:
            copy.start()
    for part in range(2):
        for copy in copies[part]:
            copy.wait()
        core = cores[part]

        def rows_of(pair, carry, part=part, core=core):
            rows = whole[part, pl.ds(pl.multiple_of(96 * pair, 96), 96), 1152:].astype(jnp.float32)
            for side in range(2):
                point[core, pl.ds(pl.multiple_of(48 * pair, 48), 48), side * 384 : side * 384 + 384] = concat(
                    rows[24 * side : 24 * side + 24], rows[48 + 24 * side : 72 + 24 * side]
                ).astype(jnp.bfloat16)
            return carry

        lax.fori_loop(0, 16, rows_of, 0)
        running = jnp.zeros((320, 384), jnp.float32)
        for k in range(3):
            tap = hidden[:, k * TAP_DILATION : k * TAP_DILATION + 64, :].reshape(320, 1536)
            running = running + jnp.dot(
                tap, whole[part, :, k * 384 : k * 384 + 384], preferred_element_type=jnp.float32
            )
        lanes = pl.ds(pl.multiple_of(core * 384, 128), 384)
        preact[:, lanes] = running
        activated[:, lanes] = gelu_tanh(running).astype(jnp.bfloat16)
    for part, (base, out) in enumerate(((base_a, point_a), (base_b, point_b))):
        lanes = slice(part * 768, part * 768 + 768)
        out[...] = point[part]
        near = near_own[:, lanes].astype(jnp.float32) + near_other[:, lanes].astype(jnp.float32)
        base[...] = (
            inputs[:, lanes].astype(jnp.float32)
            + jnp.dot(activated[...], point[part], preferred_element_type=jnp.float32)
        ) - near * 0.25


def whole_block(shape):
    return pl.BlockSpec(shape, lambda *i: (0,) * len(shape))


def forward_pass(orders, cores, arrays, pieces):
    outs = [((320, 768), jnp.float32), ((320, 768), jnp.bfloat16)]
    outs += [((320, 768), jnp.float32)] * 2 + [((768, 768), jnp.bfloat16)] * 2
    return pl.pallas_call(
        forward_kernel,
        grid_spec=pltpu.PrefetchScalarGridSpec(
            num_scalar_prefetch=2,
            grid=(1,),
            in_specs=[whole_block(array.shape) for array in arrays]
            + [pl.BlockSpec(memory_space=pl.ANY)] * len(pieces),
            out_specs=[whole_block(shape) for shape, _ in outs],
            scratch_shapes=[
                pltpu.VMEM((2, 1536, 1536), jnp.bfloat16),
                pltpu.VMEM((2, 768, 768), jnp.bfloat16),
                pltpu.SemaphoreType.DMA((2,)),
            ],
        ),
        out_shape=[jax.ShapeDtypeStruct(shape, kind) for shape, kind in outs],
        compiler_params=pltpu.CompilerParams(vmem_limit_bytes=45 * 2**20),
        name="forward",
    )(orders, cores, *arrays, *pieces)


def turn_kernel(order, hidden, hidden_other, out, turned):
    for k in range(3):
        low = k * TAP_DILATION
        for part, source in enumerate((hidden, hidden_other)):
            tap = source[:, low : low + 64, :].reshape(320, 1536)
            turned[:, part * 320 : part * 320 + 320] = tap.T

        def slot(i, carry, k=k):
            row = pl.multiple_of(order[i] * 48, 16)
            to = pl.multiple_of(i * 48, 48)
            out[k, pl.ds(to, 48), :] = turned[pl.ds(row, 48), :]
            return carry

        lax.fori_loop(0, 32, slot, 0)


def turn(order, hidden, hidden_other):
    return pl.pallas_call(
        turn_kernel,
        grid_spec=pltpu.PrefetchScalarGridSpec(
            num_scalar_prefetch=1,
            grid=(1,),
            in_specs=[whole_block(hidden.shape)] * 2,
            out_specs=whole_block((3, 1536, 640)),
            scratch_shapes=[pltpu.VMEM((1536, 640), jnp.bfloat16)],
        ),
        out_shape=jax.ShapeDtypeStruct((3, 1536, 640), jnp.bfloat16),
        compiler_params=pltpu.CompilerParams(vmem_limit_bytes=30 * 2**20),
        name="turn",
    )(order, hidden, hidden_other)


def turn_act_kernel(order, activated, activated_other, out, turned):
    turned[:, :320] = activated[...].astype(jnp.float32).T
    turned[:, 320:] = activated_other[...].astype(jnp.float32).T

    def pair(i, carry):
        rows = [turned[pl.ds(pl.multiple_of(order[2 * i + j] * 24, 8), 24), :] for j in range(2)]
        out[pl.ds(pl.multiple_of(i * 48, 48), 48), :] = concat(*rows).astype(jnp.bfloat16)
        return carry

    lax.fori_loop(0, 16, pair, 0)


def turn_act(order, activated, activated_other):
    return pl.pallas_call(
        turn_act_kernel,
        grid_spec=pltpu.PrefetchScalarGridSpec(
            num_scalar_prefetch=1,
            grid=(1,),
            in_specs=[whole_block(activated.shape)] * 2,
            out_specs=whole_block((768, 640)),
            scratch_shapes=[pltpu.VMEM((768, 640), jnp.float32)],
        ),
        out_shape=jax.ShapeDtypeStruct((768, 640), jnp.bfloat16),
        compiler_params=pltpu.CompilerParams(vmem_limit_bytes=16 * 2**20),
        name="turn_act",
    )(order, activated, activated_other)


def gradient_kernel(turned, turned_act, pre, out_grad, out):
    def store(lanes, product, power):
        factor = jnp.exp2(-power)
        out[384:, lanes] = jnp.broadcast_to(power, (16, 384))
        for first, size, part in product:
            out[first : first + size, lanes] = part * factor

    for k in range(3):
        product = jnp.dot(turned[k], pre[...], preferred_element_type=jnp.float32)
        power = power_of(jnp.max(jnp.abs(product), axis=0, keepdims=True))
        store(slice(384 * k, 384 * k + 384), [(0, 384, product)], power)
    product = jnp.dot(turned_act[...], out_grad[...], preferred_element_type=jnp.float32)
    peak = jnp.max(jnp.abs(product), axis=0, keepdims=True)
    parts = [
        (48 * i + 24 * part, 24, product[24 * i : 24 * i + 24, 384 * part : 384 * part + 384])
        for i in range(8)
        for part in range(2)
    ]
    store(slice(1152, 1536), parts, power_of(jnp.maximum(peak[:, :384], peak[:, 384:])))


def gradient_chunk(index, turned, turned_act, pre, out_grad):
    return pl.pallas_call(
        gradient_kernel,
        grid=(1,),
        in_specs=[
            pl.BlockSpec((3, 384, 640), lambda i: (0, index, 0)),
            pl.BlockSpec((192, 640), lambda i: (index, 0)),
            whole_block(pre.shape),
            whole_block(out_grad.shape),
        ],
        out_specs=pl.BlockSpec(memory_space=pltpu.VMEM),
        out_shape=pltpu.VMEM((400, 1536), jnp.float32),
        compiler_params=pltpu.CompilerParams(vmem_limit_bytes=20 * 2**20),
        name="gradient",
    )(turned, turned_act, pre, out_grad)


def in_order(core, own, other, axis):
    return jnp.where(
        core == 0,
        jnp.concatenate([own, other], axis=axis),
        jnp.concatenate([other, own], axis=axis),
    )


def half_of(value, index, axis):
    size = value.shape[axis] // 2
    return lax.dynamic_slice_in_dim(value, index * size, size, axis)


def shards(activations, teacher_maps, projection, dilated_weight, pointwise_weight):
    teacher = lax.axis_index("teacher")
    seq = lax.axis_index("seq")
    yh, core = teacher // 2, teacher % 2
    x, yl, z = seq // 8, (seq // 4) % 2, seq % 4
    wins, bins, channels = activations.shape
    rows = wins * bins
    total_rows = rows * 128
    branch = dilated_weight.shape[2]
    half = branch // 2
    inputs = activations.reshape(rows, channels)
    forward = [(g * 32 + i, g * 32 + i + 1) for g in range(4) for i in range(31)]
    backward = [(b, a) for a, b in forward]
    low = send(activations[:, -TAP_DILATION:], forward)
    high = send(activations[:, :TAP_DILATION], backward)
    padded = jnp.concatenate([low, activations, high], axis=1)
    padded_other = send(padded, CORE)
    order, order_w = block_orders(core, x, yl, z)
    order_other = block_orders(1 - core, x, yl, z)[1]
    cores = jnp.stack([core, 1 - core]).astype(jnp.int32)

    own_dil = lax.dynamic_slice_in_dim(dilated_weight, core * half, half, 2).reshape(48, 3 * half)
    own_pw = half_of(pointwise_weight, core, 1)
    own_block = jnp.concatenate([own_dil, concat(own_pw[:, :half], own_pw[:, half:])], axis=1)

    wide = channels // 2
    block = projection[0][None]
    near = concat(block, send(block, NEAR))
    first_w = concat(*ring_gather(own_block[None], True))
    first = ring_gather(near, True)
    second_w = ring_gather(first_w, False)
    low_w, high_w = concat(*second_w[:2]), concat(*second_w[2:])
    first_a, first_b = [concat(*[v[:, :, column : column + wide] for v in first]) for column in (0, wide)]
    pieces_a = ring_gather(first_a, False)
    pieces_w = [low_w, high_w, send(low_w, NEAR), send(high_w, FAR_NEAR)]
    pieces_b = ring_gather(first_b, False)
    pieces_other = [send(piece, CORE) for piece in pieces_w[:2]]
    pieces_other += [send(piece, CORE) for piece in pieces_w[2:]]

    inputs_f = inputs.astype(jnp.float32)
    local = jnp.concatenate([jnp.sum(inputs_f, axis=0), jnp.sum(inputs_f * inputs_f, axis=0)])
    sums = sum_everywhere(local.reshape(24, 128)).reshape(2, channels)
    channel_mean = sums[0] / total_rows
    channel_var = sums[1] / total_rows - channel_mean * channel_mean
    scale = lax.rsqrt(channel_var + 1e-05)
    place = lax.broadcasted_iota(jnp.int32, (1, bins + 2 * TAP_DILATION, 1), 1) + seq * bins
    inside = (place >= TAP_DILATION) & (place < 32 * bins + TAP_DILATION)

    def hidden_of(value):
        normed = (value.astype(jnp.float32) - channel_mean) * scale
        return jnp.where(inside, gelu_tanh(normed), 0.0).astype(jnp.bfloat16)

    hidden, hidden_other = hidden_of(padded), hidden_of(padded_other)

    maps = teacher_maps.reshape(4, rows, teacher_maps.shape[3])
    far_groups = jnp.stack([(1 - yh) * 2 + 1 - core, (1 - yh) * 2 + core]).astype(jnp.int32)
    near_groups = jnp.stack([yh * 2 + 1 - core, yh * 2 + core]).astype(jnp.int32)
    arrived = []
    for pieces in (pieces_a, pieces_b):
        other, own = teacher_terms(order, far_groups, maps, pieces, 16)
        other = send(other, CORE)
        power = jnp.maximum(own[320:321], other[320:321]).astype(jnp.float32)
        packed = pack(own[:320].astype(jnp.float32) + other[:320].astype(jnp.float32), power)
        arrived.append(send(packed, FAR))
    other, own = teacher_terms(order, near_groups, maps, pieces_a + pieces_b, 0)

    preact, activated, *base, point_a, point_b = forward_pass(
        jnp.stack([order_w, order_other]), cores, [hidden, inputs, own, send(other, CORE)], pieces_w + pieces_other
    )
    out_grads, squared = [], 0.0
    for value, terms in zip(base, arrived, strict=True):
        misfit = value - unpack(terms) * 0.25
        squared = squared + jnp.sum(misfit * misfit)
        out_grads.append((misfit / channels).astype(jnp.bfloat16))
    back_grad = sum(
        lax.dot_general(v, w, (((1,), (1,)), ((), ())), preferred_element_type=jnp.float32)
        for v, w in zip(out_grads, (point_a, point_b), strict=True)
    )
    preact_grad = (back_grad * gelu_slope(preact)).astype(jnp.bfloat16)

    turned = turn(order, hidden, hidden_other)
    turned_act = turn_act(order, activated, send(activated, CORE))
    out_own = jnp.where(core == 0, *out_grads)
    out_both = concat(out_own, send(jnp.where(core == 0, *out_grads[::-1]), CORE))
    pre_both = concat(
        half_of(preact_grad, core, 1), send(half_of(preact_grad, 1 - core, 1), CORE)
    )
    arrived = []
    for index in (3, 1, 2, 0):
        chunk = gradient_chunk(index, turned, turned_act, pre_both, out_both)
        if index:
            arrived.append(send(chunk.astype(jnp.float16), RING[False, STEPS[index]]))
    squares = sum_everywhere(jnp.broadcast_to(after(squared, chunk), (8, 128)))
    loss_mean = 0.5 * squares[0, 0] / (channels * total_rows)
    block = finish_reduce(*add_up(unpack(chunk), power_in(chunk), arrived))
    other = send(block, CORE)

    def dilated_columns(v):
        return v[:, : 3 * half].reshape(48, 3, half)

    def pw_columns(v):
        v = v[:, 3 * half :].reshape(2, branch // 32, half)
        return v.transpose(1, 0, 2).reshape(branch // 32, branch)

    dilated_grad = in_order(core, dilated_columns(block), dilated_columns(other), 2)
    pointwise_grad = in_order(core, pw_columns(block), pw_columns(other), 1)
    return (loss_mean, dilated_grad, pointwise_grad)


def solution(mesh):
    in_specs = (
        P("teacher", "seq", None),
        P("teacher", None, "seq", None),
        P("teacher", "seq", None),
        P("seq", None, None),
        P("seq", None),
    )
    out_specs = (P(), P("seq", None, None), P("seq", None))

    return jax.shard_map(shards, mesh=mesh, in_specs=in_specs, out_specs=out_specs, check_vma=False)
```

```python
import jax
import jax.numpy as jnp
import numpy as np
from jax import lax
from jax.experimental import pallas as pl
from jax.experimental.pallas import tpu as pltpu
from jax.sharding import PartitionSpec as P


TAP_DILATION = 16
AXES = ("teacher", "seq")
SHAPE = (2, 2, 4, 2, 4)
STEPS = (0, -1, 1, 2)

slope_const = 0.7978845608
cubic_const = 0.044715


def pairs_of(move):
    pairs = []
    for source in range(int(np.prod(SHAPE))):
        at = [int(v) for v in np.unravel_index(source, SHAPE)]
        pairs.append((source, int(np.ravel_multi_index(move(*at), SHAPE))))
    return pairs


def along(first, step):
    def move(yh, core, x, yl, z):
        if (core == 0) == first:
            return (yh, core, (x + step) % 4, yl, z)
        return (yh, core, x, yl, (z + step) % 4)

    return pairs_of(move)


CORE = pairs_of(lambda yh, core, x, yl, z: (yh, 1 - core, x, yl, z))
FAR = pairs_of(lambda yh, core, x, yl, z: (1 - yh, core, x, yl, z))
NEAR = pairs_of(lambda yh, core, x, yl, z: (yh, core, x, 1 - yl, z))
FAR_NEAR = pairs_of(lambda yh, core, x, yl, z: (1 - yh, core, x, 1 - yl, z))
RING = {(first, step): along(first, step) for first in (True, False) for step in (1, -1, 2)}


def send(value, pairs):
    return lax.ppermute(value, AXES, pairs)


def gelu_tanh(value):
    inside = slope_const * (value + cubic_const * value * value * value)
    return 0.5 * value * (1.0 + jnp.tanh(inside))


def gelu_slope(value):
    inside = slope_const * (value + cubic_const * value * value * value)
    tangent = jnp.tanh(inside)
    return 0.5 * (1.0 + tangent) + 0.5 * value * (1.0 - tangent * tangent) * slope_const * (
        1.0 + 3.0 * cubic_const * value * value
    )


def block_orders(core, x, yl, z):
    first = jnp.where(core == 0, x, z)
    second = jnp.where(core == 0, z, x)

    def block(far, near, side):
        one = (first + near + 4) % 4
        two = (second + far + 4) % 4
        at_x = jnp.where(core == 0, one, two)
        at_z = jnp.where(core == 0, two, one)
        return (at_x * 2 + (yl + side) % 2) * 4 + at_z

    sides = (0, 1)
    inner = [block(far, near, side) for far in STEPS for near in STEPS for side in sides]
    outer = [block(far, near, side) for side in sides for far in STEPS for near in STEPS]
    return jnp.stack(inner).astype(jnp.int32), jnp.stack(outer).astype(jnp.int32)


def concat(*values):
    return jnp.concatenate(values)


def after(value, *earlier):
    return lax.optimization_barrier((value, *earlier))[0]


def ring_gather(value, first):
    return [value] + [send(value, RING[first, step]) for step in (1, -1, 2)]


def power_of(peak):
    return jnp.clip(jnp.floor(jnp.log2(jnp.maximum(peak, 1e-30))) - 13.0, -110.0, 127.0)


def pack(value, power):
    scaled = (value * jnp.exp2(-power)).astype(jnp.float16)
    return concat(scaled, jnp.broadcast_to(power, (16, value.shape[1])).astype(jnp.float16))


def power_in(packed):
    return packed[-16:-15].astype(jnp.float32)


def unpack(packed):
    return packed[:-16].astype(jnp.float32) * jnp.exp2(power_in(packed))


def sum_everywhere(value):
    value = value + send(value, CORE)
    value = value + send(value, NEAR) + send(value, FAR) + send(value, FAR_NEAR)
    for first in (True, False):
        value = value + send(value, RING[first, 1]) + send(value, RING[first, -1]) + send(value, RING[first, 2])
    return value


def add_up(own, own_power, arrived):
    power = own_power
    for packed in arrived:
        own = own + unpack(packed)
        power = jnp.maximum(power, power_in(packed))
    return own, power + 2.0


def finish_reduce(own, power):
    rows = own.shape[0] // 8
    arrived = [
        send(pack(own[2 * rows * (i + 1) : 2 * rows * (i + 2)], power), RING[True, step])
        for i, step in enumerate(STEPS[1:])
    ]
    own, power = add_up(own[: 2 * rows], power, arrived)
    keep, give = pack(own[:rows], power), pack(own[rows:], power)
    arrived = [send(give, NEAR), send(keep, FAR), send(give, FAR_NEAR)]
    return add_up(own[:rows], power, arrived)[0]


def block_copies(order, pieces, target, sem):
    copies, place = [], 0
    for piece in pieces:
        for at in range(piece.shape[0]):
            row = pl.multiple_of(order[place] * 48, 16)
            copies.append(pltpu.make_async_copy(piece.at[at], target(row), sem))
            place += 1
    return copies


def run_copies(copies):
    for copy in copies:
        copy.start()
    for copy in copies:
        copy.wait()


def teacher_kernel(order, groups, maps_other, maps_own, *refs):
    count = len(refs) - 4
    other, own, whole, sem = refs[count:]
    width = whole.shape[1]
    each = refs[0].shape[2]
    copies = []
    for part in range(count // 4):
        copies += block_copies(
            order,
            refs[4 * part : 4 * part + 4],
            lambda row, part=part: whole.at[pl.ds(row, 48), part * each : (part + 1) * each],
            sem,
        )
    run_copies(copies)
    for maps, out in ((maps_other, other), (maps_own, own)):
        terms = jnp.dot(maps[0], whole[...], preferred_element_type=jnp.float32)
        out[:320, :] = terms.astype(jnp.bfloat16)
        if out.shape[0] > 320:
            power = power_of(jnp.max(jnp.abs(terms), axis=0, keepdims=True)) + 1.0
            out[320:, :] = jnp.broadcast_to(power, (16, width)).astype(jnp.bfloat16)


def teacher_terms(order, groups, maps, pieces, extra):
    rows, depth = maps.shape[1:]
    width = pieces[0].shape[2] * len(pieces) // 4
    return pl.pallas_call(
        teacher_kernel,
        grid_spec=pltpu.PrefetchScalarGridSpec(
            num_scalar_prefetch=2,
            grid=(1,),
            in_specs=[
                pl.BlockSpec((1, rows, depth), lambda i, order, groups: (groups[0], 0, 0)),
                pl.BlockSpec((1, rows, depth), lambda i, order, groups: (groups[1], 0, 0)),
            ]
            + [pl.BlockSpec(memory_space=pl.ANY)] * len(pieces),
            out_specs=[whole_block((rows + extra, width))] * 2,
            scratch_shapes=[pltpu.VMEM((depth, width), jnp.bfloat16), pltpu.SemaphoreType.DMA(())],
        ),
        out_shape=[jax.ShapeDtypeStruct((rows + extra, width), jnp.bfloat16)] * 2,
        compiler_params=pltpu.CompilerParams(vmem_limit_bytes=30 * 2**20),
        name="teacher",
    )(order, groups, maps, maps, *pieces)


def forward_kernel(orders, cores, hidden, inputs, near_own, near_other, *refs):
    pieces = refs[:8]
    preact, activated, base_a, base_b, point_a, point_b, whole, point, sems = refs[8:]
    copies = [
        block_copies(
            orders.at[part],
            pieces[4 * part : 4 * part + 4],
            lambda row, part=part: whole.at[part, pl.ds(row, 48), :],
            sems.at[part],
        )
        for part in range(2)
    ]
    for part in range(2):
        for copy in copies[part]:
            copy.start()
    for part in range(2):
        for copy in copies[part]:
            copy.wait()
        core = cores[part]

        def rows_of(pair, carry, part=part, core=core):
            rows = whole[part, pl.ds(pl.multiple_of(96 * pair, 96), 96), 1152:].astype(jnp.float32)
            for side in range(2):
                point[core, pl.ds(pl.multiple_of(48 * pair, 48), 48), side * 384 : side * 384 + 384] = concat(
                    rows[24 * side : 24 * side + 24], rows[48 + 24 * side : 72 + 24 * side]
                ).astype(jnp.bfloat16)
            return carry

        lax.fori_loop(0, 16, rows_of, 0)
        running = jnp.zeros((320, 384), jnp.float32)
        for k in range(3):
            tap = hidden[:, k * TAP_DILATION : k * TAP_DILATION + 64, :].reshape(320, 1536)
            running = running + jnp.dot(
                tap, whole[part, :, k * 384 : k * 384 + 384], preferred_element_type=jnp.float32
            )
        lanes = pl.ds(pl.multiple_of(core * 384, 128), 384)
        preact[:, lanes] = running
        activated[:, lanes] = gelu_tanh(running).astype(jnp.bfloat16)
    for part, (base, out) in enumerate(((base_a, point_a), (base_b, point_b))):
        lanes = slice(part * 768, part * 768 + 768)
        out[...] = point[part]
        near = near_own[:, lanes].astype(jnp.float32) + near_other[:, lanes].astype(jnp.float32)
        base[...] = (
            inputs[:, lanes].astype(jnp.float32)
            + jnp.dot(activated[...], point[part], preferred_element_type=jnp.float32)
        ) - near * 0.25


def whole_block(shape):
    return pl.BlockSpec(shape, lambda *i: (0,) * len(shape))


def forward_pass(orders, cores, arrays, pieces):
    outs = [((320, 768), jnp.float32), ((320, 768), jnp.bfloat16)]
    outs += [((320, 768), jnp.float32)] * 2 + [((768, 768), jnp.bfloat16)] * 2
    return pl.pallas_call(
        forward_kernel,
        grid_spec=pltpu.PrefetchScalarGridSpec(
            num_scalar_prefetch=2,
            grid=(1,),
            in_specs=[whole_block(array.shape) for array in arrays]
            + [pl.BlockSpec(memory_space=pl.ANY)] * len(pieces),
            out_specs=[whole_block(shape) for shape, _ in outs],
            scratch_shapes=[
                pltpu.VMEM((2, 1536, 1536), jnp.bfloat16),
                pltpu.VMEM((2, 768, 768), jnp.bfloat16),
                pltpu.SemaphoreType.DMA((2,)),
            ],
        ),
        out_shape=[pltpu.HBM(shape, kind) for shape, kind in outs],
        compiler_params=pltpu.CompilerParams(vmem_limit_bytes=45 * 2**20),
        name="forward",
    )(orders, cores, *arrays, *pieces)


def turn_kernel(order, hidden, hidden_other, out, turned):
    for k in range(3):
        low = k * TAP_DILATION
        for part, source in enumerate((hidden, hidden_other)):
            tap = source[:, low : low + 64, :].reshape(320, 1536)
            turned[:, part * 320 : part * 320 + 320] = tap.T

        def slot(i, carry, k=k):
            row = pl.multiple_of(order[i] * 48, 16)
            to = pl.multiple_of(i * 48, 48)
            out[k, pl.ds(to, 48), :] = turned[pl.ds(row, 48), :]
            return carry

        lax.fori_loop(0, 32, slot, 0)


def turn(order, hidden, hidden_other):
    return pl.pallas_call(
        turn_kernel,
        grid_spec=pltpu.PrefetchScalarGridSpec(
            num_scalar_prefetch=1,
            grid=(1,),
            in_specs=[whole_block(hidden.shape)] * 2,
            out_specs=whole_block((3, 1536, 640)),
            scratch_shapes=[pltpu.VMEM((1536, 640), jnp.bfloat16)],
        ),
        out_shape=pltpu.HBM((3, 1536, 640), jnp.bfloat16),
        compiler_params=pltpu.CompilerParams(vmem_limit_bytes=30 * 2**20),
        name="turn",
    )(order, hidden, hidden_other)


def turn_act_kernel(order, activated, activated_other, out, turned):
    turned[:, :320] = activated[...].astype(jnp.float32).T
    turned[:, 320:] = activated_other[...].astype(jnp.float32).T

    def pair(i, carry):
        rows = [turned[pl.ds(pl.multiple_of(order[2 * i + j] * 24, 8), 24), :] for j in range(2)]
        out[pl.ds(pl.multiple_of(i * 48, 48), 48), :] = concat(*rows).astype(jnp.bfloat16)
        return carry

    lax.fori_loop(0, 16, pair, 0)


def turn_act(order, activated, activated_other):
    return pl.pallas_call(
        turn_act_kernel,
        grid_spec=pltpu.PrefetchScalarGridSpec(
            num_scalar_prefetch=1,
            grid=(1,),
            in_specs=[whole_block(activated.shape)] * 2,
            out_specs=whole_block((768, 640)),
            scratch_shapes=[pltpu.VMEM((768, 640), jnp.float32)],
        ),
        out_shape=jax.ShapeDtypeStruct((768, 640), jnp.bfloat16),
        compiler_params=pltpu.CompilerParams(vmem_limit_bytes=16 * 2**20),
        name="turn_act",
    )(order, activated, activated_other)


def gradient_kernel(turned, turned_act, pre, out_grad, out):
    def store(lanes, product, power):
        factor = jnp.exp2(-power)
        out[384:, lanes] = jnp.broadcast_to(power, (16, 384))
        for first, size, part in product:
            out[first : first + size, lanes] = part * factor

    for k in range(3):
        product = jnp.dot(turned[k], pre[...], preferred_element_type=jnp.float32)
        power = power_of(jnp.max(jnp.abs(product), axis=0, keepdims=True))
        store(slice(384 * k, 384 * k + 384), [(0, 384, product)], power)
    product = jnp.dot(turned_act[...], out_grad[...], preferred_element_type=jnp.float32)
    peak = jnp.max(jnp.abs(product), axis=0, keepdims=True)
    parts = [
        (48 * i + 24 * part, 24, product[24 * i : 24 * i + 24, 384 * part : 384 * part + 384])
        for i in range(8)
        for part in range(2)
    ]
    store(slice(1152, 1536), parts, power_of(jnp.maximum(peak[:, :384], peak[:, 384:])))


def gradient_chunk(index, turned, turned_act, pre, out_grad):
    return pl.pallas_call(
        gradient_kernel,
        grid=(1,),
        in_specs=[
            pl.BlockSpec((3, 384, 640), lambda i: (0, index, 0)),
            pl.BlockSpec((192, 640), lambda i: (index, 0)),
            whole_block(pre.shape),
            whole_block(out_grad.shape),
        ],
        out_specs=pl.BlockSpec(memory_space=pltpu.VMEM),
        out_shape=pltpu.VMEM((400, 1536), jnp.float32),
        compiler_params=pltpu.CompilerParams(vmem_limit_bytes=20 * 2**20),
        name="gradient",
    )(turned, turned_act, pre, out_grad)


def in_order(core, own, other, axis):
    return jnp.where(
        core == 0,
        jnp.concatenate([own, other], axis=axis),
        jnp.concatenate([other, own], axis=axis),
    )


def half_of(value, index, axis):
    size = value.shape[axis] // 2
    return lax.dynamic_slice_in_dim(value, index * size, size, axis)


def shards(activations, teacher_maps, projection, dilated_weight, pointwise_weight):
    teacher = lax.axis_index("teacher")
    seq = lax.axis_index("seq")
    yh, core = teacher // 2, teacher % 2
    x, yl, z = seq // 8, (seq // 4) % 2, seq % 4
    wins, bins, channels = activations.shape
    rows = wins * bins
    total_rows = rows * 128
    branch = dilated_weight.shape[2]
    half = branch // 2
    inputs = activations.reshape(rows, channels)
    forward = [(g * 32 + i, g * 32 + i + 1) for g in range(4) for i in range(31)]
    backward = [(b, a) for a, b in forward]
    low = send(activations[:, -TAP_DILATION:], forward)
    high = send(activations[:, :TAP_DILATION], backward)
    padded = jnp.concatenate([low, activations, high], axis=1)
    padded_other = send(padded, CORE)
    order, order_w = block_orders(core, x, yl, z)
    order_other = block_orders(1 - core, x, yl, z)[1]
    cores = jnp.stack([core, 1 - core]).astype(jnp.int32)

    own_dil = lax.dynamic_slice_in_dim(dilated_weight, core * half, half, 2).reshape(48, 3 * half)
    own_pw = half_of(pointwise_weight, core, 1)
    own_block = jnp.concatenate([own_dil, concat(own_pw[:, :half], own_pw[:, half:])], axis=1)

    wide = channels // 2
    block = projection[0][None]
    near = concat(block, send(block, NEAR))
    first_w = concat(*ring_gather(own_block[None], True))
    first = ring_gather(near, True)
    second_w = ring_gather(first_w, False)
    low_w, high_w = concat(*second_w[:2]), concat(*second_w[2:])
    first_a, first_b = [concat(*[v[:, :, column : column + wide] for v in first]) for column in (0, wide)]
    pieces_a = ring_gather(first_a, False)
    pieces_w = [low_w, high_w, send(low_w, NEAR), send(high_w, FAR_NEAR)]
    pieces_b = ring_gather(first_b, False)
    pieces_other = [send(piece, CORE) for piece in pieces_w[:2]]
    pieces_other += [send(piece, CORE) for piece in pieces_w[2:]]

    inputs_f = inputs.astype(jnp.float32)
    local = jnp.concatenate([jnp.sum(inputs_f, axis=0), jnp.sum(inputs_f * inputs_f, axis=0)])
    sums = sum_everywhere(local.reshape(24, 128)).reshape(2, channels)
    channel_mean = sums[0] / total_rows
    channel_var = sums[1] / total_rows - channel_mean * channel_mean
    scale = lax.rsqrt(channel_var + 1e-05)
    place = lax.broadcasted_iota(jnp.int32, (1, bins + 2 * TAP_DILATION, 1), 1) + seq * bins
    inside = (place >= TAP_DILATION) & (place < 32 * bins + TAP_DILATION)

    def hidden_of(value):
        normed = (value.astype(jnp.float32) - channel_mean) * scale
        return jnp.where(inside, gelu_tanh(normed), 0.0).astype(jnp.bfloat16)

    hidden, hidden_other = hidden_of(padded), hidden_of(padded_other)

    maps = teacher_maps.reshape(4, rows, teacher_maps.shape[3])
    far_groups = jnp.stack([(1 - yh) * 2 + 1 - core, (1 - yh) * 2 + core]).astype(jnp.int32)
    near_groups = jnp.stack([yh * 2 + 1 - core, yh * 2 + core]).astype(jnp.int32)
    arrived = []
    for pieces in (pieces_a, pieces_b):
        other, own = teacher_terms(order, far_groups, maps, pieces, 16)
        other = send(other, CORE)
        power = jnp.maximum(own[320:321], other[320:321]).astype(jnp.float32)
        packed = pack(own[:320].astype(jnp.float32) + other[:320].astype(jnp.float32), power)
        arrived.append(send(packed, FAR))
    other, own = teacher_terms(order, near_groups, maps, pieces_a + pieces_b, 0)

    other = send(other, CORE)

    preact, activated, *base, point_a, point_b = forward_pass(
        jnp.stack([order_w, order_other]), cores, [hidden, inputs, own, other], pieces_w + pieces_other
    )
    out_grads, squared = [], 0.0
    for value, terms in zip(base, arrived, strict=True):
        misfit = value - unpack(terms) * 0.25
        squared = squared + jnp.sum(misfit * misfit)
        out_grads.append((misfit / channels).astype(jnp.bfloat16))
    back_grad = sum(
        lax.dot_general(v, w, (((1,), (1,)), ((), ())), preferred_element_type=jnp.float32)
        for v, w in zip(out_grads, (point_a, point_b), strict=True)
    )
    preact_grad = (back_grad * gelu_slope(preact)).astype(jnp.bfloat16)

    turned = turn(order, hidden, hidden_other)
    turned_act = turn_act(order, activated, send(activated, CORE))
    out_own = jnp.where(core == 0, *out_grads)
    out_both = concat(out_own, send(jnp.where(core == 0, *out_grads[::-1]), CORE))
    pre_both = concat(
        half_of(preact_grad, core, 1), send(half_of(preact_grad, 1 - core, 1), CORE)
    )
    arrived = []
    for index in (3, 1, 2, 0):
        chunk = gradient_chunk(index, turned, turned_act, pre_both, out_both)
        if index:
            arrived.append(send(chunk.astype(jnp.float16), RING[False, STEPS[index]]))
    squares = sum_everywhere(jnp.broadcast_to(after(squared, chunk), (8, 128)))
    loss_mean = 0.5 * squares[0, 0] / (channels * total_rows)
    block = finish_reduce(*add_up(unpack(chunk), power_in(chunk), arrived))
    other = send(block, CORE)

    def dilated_columns(v):
        return v[:, : 3 * half].reshape(48, 3, half)

    def pw_columns(v):
        v = v[:, 3 * half :].reshape(2, branch // 32, half)
        return v.transpose(1, 0, 2).reshape(branch // 32, branch)

    dilated_grad = in_order(core, dilated_columns(block), dilated_columns(other), 2)
    pointwise_grad = in_order(core, pw_columns(block), pw_columns(other), 1)
    return (loss_mean, dilated_grad, pointwise_grad)


def solution(mesh):
    in_specs = (
        P("teacher", "seq", None),
        P("teacher", None, "seq", None),
        P("teacher", "seq", None),
        P("seq", None, None),
        P("seq", None),
    )
    out_specs = (P(), P("seq", None, None), P("seq", None))

    return jax.shard_map(shards, mesh=mesh, in_specs=in_specs, out_specs=out_specs, check_vma=False)
```

```python
import jax
import jax.numpy as jnp
import numpy as np
from jax import lax
from jax.experimental import pallas as pl
from jax.experimental.pallas import tpu as pltpu
from jax.sharding import PartitionSpec as P


TAP_DILATION = 16
AXES = ("teacher", "seq")
SHAPE = (2, 2, 4, 2, 4)
STEPS = (0, -1, 1, 2)

slope_const = 0.7978845608
cubic_const = 0.044715


def pairs_of(move):
    pairs = []
    for source in range(int(np.prod(SHAPE))):
        at = [int(v) for v in np.unravel_index(source, SHAPE)]
        pairs.append((source, int(np.ravel_multi_index(move(*at), SHAPE))))
    return pairs


def along(first, step):
    def move(yh, core, x, yl, z):
        if (core == 0) == first:
            return (yh, core, (x + step) % 4, yl, z)
        return (yh, core, x, yl, (z + step) % 4)

    return pairs_of(move)


CORE = pairs_of(lambda yh, core, x, yl, z: (yh, 1 - core, x, yl, z))
FAR = pairs_of(lambda yh, core, x, yl, z: (1 - yh, core, x, yl, z))
NEAR = pairs_of(lambda yh, core, x, yl, z: (yh, core, x, 1 - yl, z))
FAR_NEAR = pairs_of(lambda yh, core, x, yl, z: (1 - yh, core, x, 1 - yl, z))
RING = {(first, step): along(first, step) for first in (True, False) for step in (1, -1, 2)}


def send(value, pairs):
    return lax.ppermute(value, AXES, pairs)


def gelu_tanh(value):
    inside = slope_const * (value + cubic_const * value * value * value)
    return 0.5 * value * (1.0 + jnp.tanh(inside))


def gelu_slope(value):
    inside = slope_const * (value + cubic_const * value * value * value)
    tangent = jnp.tanh(inside)
    return 0.5 * (1.0 + tangent) + 0.5 * value * (1.0 - tangent * tangent) * slope_const * (
        1.0 + 3.0 * cubic_const * value * value
    )


def block_order(core, x, yl, z):
    first = jnp.where(core == 0, x, z)
    second = jnp.where(core == 0, z, x)
    order = []
    for far in STEPS:
        for near in STEPS:
            for side in (0, 1):
                one = (first + near + 4) % 4
                two = (second + far + 4) % 4
                at_x = jnp.where(core == 0, one, two)
                at_z = jnp.where(core == 0, two, one)
                order.append((at_x * 2 + (yl + side) % 2) * 4 + at_z)
    return jnp.stack(order).astype(jnp.int32)


def concat(*values):
    return jnp.concatenate(values)


def after(value, *earlier):
    return lax.optimization_barrier((value, *earlier))[0]


def ring_gather(value, first):
    return [value] + [send(value, RING[first, step]) for step in (1, -1, 2)]


def power_of(peak):
    return jnp.clip(jnp.floor(jnp.log2(jnp.maximum(peak, 1e-30))) - 13.0, -110.0, 127.0)


def pack(value, power, loss=None):
    rows = jnp.broadcast_to(power, (16, value.shape[1]))
    if loss is not None:
        exponent = jnp.floor(jnp.log2(jnp.maximum(loss, 1e-30)))
        rest = loss * jnp.exp2(-exponent)
        upper = jnp.floor(rest * 512.0) / 512.0
        which = lax.broadcasted_iota(jnp.int32, rows.shape, 0)
        for row, part in enumerate((exponent, upper, (rest - upper) * 1024.0)):
            rows = jnp.where(which == row + 1, part, rows)
    scaled = (value * jnp.exp2(-power)).astype(jnp.float16)
    return concat(scaled, rows.astype(jnp.float16))


def power_in(packed):
    return packed[-16:-15].astype(jnp.float32)


def unpack(packed):
    return packed[:-16].astype(jnp.float32) * jnp.exp2(power_in(packed))


def loss_in(packed):
    exponent, upper, lower = [packed[row : row + 1, :1].astype(jnp.float32) for row in (-15, -14, -13)]
    return jnp.exp2(exponent) * (upper + lower / 1024.0)


def sum_everywhere(value):
    value = value + send(value, CORE)
    value = value + send(value, NEAR) + send(value, FAR) + send(value, FAR_NEAR)
    for first in (True, False):
        value = value + send(value, RING[first, 1]) + send(value, RING[first, -1]) + send(value, RING[first, 2])
    return value


def add_up(own, own_power, arrived):
    power = own_power
    for packed in arrived:
        own = own + unpack(packed)
        power = jnp.maximum(power, power_in(packed))
    return own, power + 2.0


def finish_reduce(own, power, loss):
    rows = own.shape[0] // 8
    arrived = [
        send(pack(own[2 * rows * (i + 1) : 2 * rows * (i + 2)], power, loss), RING[True, step])
        for i, step in enumerate(STEPS[1:])
    ]
    own, power = add_up(own[: 2 * rows], power, arrived)
    loss = loss + sum(loss_in(packed) for packed in arrived)
    keep, give = pack(own[:rows], power, loss), pack(own[rows:], power, loss)
    arrived = [send(give, NEAR), send(keep, FAR), send(give, FAR_NEAR)]
    return add_up(own[:rows], power, arrived)[0], loss + sum(loss_in(packed) for packed in arrived)


def load_blocks(order, pieces, target, sem):
    for index, piece in enumerate(pieces):

        def start(at, carry, index=index, piece=piece):
            row = pl.multiple_of(order[8 * index + at] * 48, 16)
            pltpu.make_async_copy(piece.at[at], target(row), sem).start()
            return carry

        lax.fori_loop(0, 8, start, 0)


def teacher_kernel(order, groups, maps_other, maps_own, *refs):
    count = len(refs) - 4
    other, own, whole, sem = refs[count:]
    width = whole.shape[1]
    each = refs[0].shape[2]
    for part in range(count // 4):
        load_blocks(
            order,
            refs[4 * part : 4 * part + 4],
            lambda row, part=part: whole.at[pl.ds(row, 48), part * each : (part + 1) * each],
            sem,
        )
    pltpu.make_async_copy(whole, whole, sem).wait()
    for maps, out in ((maps_other, other), (maps_own, own)):
        terms = jnp.dot(maps[0], whole[...], preferred_element_type=jnp.float32)
        out[:320, :] = terms.astype(jnp.bfloat16)
        if out.shape[0] > 320:
            power = power_of(jnp.max(jnp.abs(terms), axis=0, keepdims=True)) + 1.0
            out[320:, :] = jnp.broadcast_to(power, (16, width)).astype(jnp.bfloat16)


def teacher_terms(order, groups, maps, pieces, extra):
    rows, depth = maps.shape[1:]
    width = pieces[0].shape[2] * len(pieces) // 4
    return pl.pallas_call(
        teacher_kernel,
        grid_spec=pltpu.PrefetchScalarGridSpec(
            num_scalar_prefetch=2,
            grid=(1,),
            in_specs=[
                pl.BlockSpec((1, rows, depth), lambda i, order, groups: (groups[0], 0, 0)),
                pl.BlockSpec((1, rows, depth), lambda i, order, groups: (groups[1], 0, 0)),
            ]
            + [pl.BlockSpec(memory_space=pl.ANY)] * len(pieces),
            out_specs=[whole_block((rows + extra, width))] * 2,
            scratch_shapes=[pltpu.VMEM((depth, width), jnp.bfloat16), pltpu.SemaphoreType.DMA(())],
        ),
        out_shape=[jax.ShapeDtypeStruct((rows + extra, width), jnp.bfloat16)] * 2,
        compiler_params=pltpu.CompilerParams(vmem_limit_bytes=30 * 2**20),
        name="teacher",
    )(order, groups, maps, maps, *pieces)


def forward_kernel(orders, cores, hidden, inputs, near_own, near_other, *refs):
    pieces = refs[:8]
    preact, activated, base_a, base_b, point_a, point_b, whole, point, sems = refs[8:]
    for part in range(2):
        load_blocks(
            orders.at[part],
            pieces[4 * part : 4 * part + 4],
            lambda row, part=part: whole.at[part, pl.ds(row, 48), :],
            sems.at[part],
        )
    for part in range(2):
        pltpu.make_async_copy(whole.at[part], whole.at[part], sems.at[part]).wait()
        core = cores[part]

        def rows_of(pair, carry, part=part, core=core):
            rows = whole[part, pl.ds(pl.multiple_of(96 * pair, 96), 96), 1152:].astype(jnp.float32)
            for side in range(2):
                point[core, pl.ds(pl.multiple_of(48 * pair, 48), 48), side * 384 : side * 384 + 384] = concat(
                    rows[24 * side : 24 * side + 24], rows[48 + 24 * side : 72 + 24 * side]
                ).astype(jnp.bfloat16)
            return carry

        lax.fori_loop(0, 16, rows_of, 0)
        running = jnp.zeros((320, 384), jnp.float32)
        for k in range(3):
            tap = hidden[:, k * TAP_DILATION : k * TAP_DILATION + 64, :].reshape(320, 1536)
            running = running + jnp.dot(
                tap, whole[part, :, k * 384 : k * 384 + 384], preferred_element_type=jnp.float32
            )
        lanes = pl.ds(pl.multiple_of(core * 384, 128), 384)
        preact[:, lanes] = running
        activated[:, lanes] = gelu_tanh(running).astype(jnp.bfloat16)
    for part, (base, out) in enumerate(((base_a, point_a), (base_b, point_b))):
        lanes = slice(part * 768, part * 768 + 768)
        out[...] = point[part]
        near = near_own[:, lanes].astype(jnp.float32) + near_other[:, lanes].astype(jnp.float32)
        base[...] = (
            inputs[:, lanes].astype(jnp.float32)
            + jnp.dot(activated[...], point[part], preferred_element_type=jnp.float32)
        ) - near * 0.25


def whole_block(shape):
    return pl.BlockSpec(shape, lambda *i: (0,) * len(shape))


def forward_pass(orders, cores, arrays, pieces):
    outs = [((320, 768), jnp.float32), ((320, 768), jnp.bfloat16)]
    outs += [((320, 768), jnp.float32)] * 2 + [((768, 768), jnp.bfloat16)] * 2
    return pl.pallas_call(
        forward_kernel,
        grid_spec=pltpu.PrefetchScalarGridSpec(
            num_scalar_prefetch=2,
            grid=(1,),
            in_specs=[whole_block(array.shape) for array in arrays]
            + [pl.BlockSpec(memory_space=pl.ANY)] * len(pieces),
            out_specs=[whole_block(shape) for shape, _ in outs],
            scratch_shapes=[
                pltpu.VMEM((2, 1536, 1536), jnp.bfloat16),
                pltpu.VMEM((2, 768, 768), jnp.bfloat16),
                pltpu.SemaphoreType.DMA((2,)),
            ],
        ),
        out_shape=[pltpu.HBM(shape, kind) for shape, kind in outs],
        compiler_params=pltpu.CompilerParams(vmem_limit_bytes=45 * 2**20),
        name="forward",
    )(orders, cores, *arrays, *pieces)


def turn_kernel(order, hidden, hidden_other, out, turned):
    def tap_of(k, carry):
        low = pl.multiple_of(k * TAP_DILATION, TAP_DILATION)
        for part, source in enumerate((hidden, hidden_other)):
            tap = source[:, pl.ds(low, 64), :].reshape(320, 1536)
            turned[:, part * 320 : part * 320 + 320] = tap.T

        def slot(i, inner):
            row = pl.multiple_of(order[i] * 48, 16)
            to = pl.multiple_of(i * 48, 48)
            out[k, pl.ds(to, 48), :] = turned[pl.ds(row, 48), :]
            return inner

        return lax.fori_loop(0, 32, slot, carry)

    lax.fori_loop(0, 3, tap_of, 0)


def turn(order, hidden, hidden_other):
    return pl.pallas_call(
        turn_kernel,
        grid_spec=pltpu.PrefetchScalarGridSpec(
            num_scalar_prefetch=1,
            grid=(1,),
            in_specs=[whole_block(hidden.shape)] * 2,
            out_specs=whole_block((3, 1536, 640)),
            scratch_shapes=[pltpu.VMEM((1536, 640), jnp.bfloat16)],
        ),
        out_shape=pltpu.HBM((3, 1536, 640), jnp.bfloat16),
        compiler_params=pltpu.CompilerParams(vmem_limit_bytes=30 * 2**20),
        name="turn",
    )(order, hidden, hidden_other)


def turn_act_kernel(order, activated, activated_other, out, turned):
    turned[:, :320] = activated[...].astype(jnp.float32).T
    turned[:, 320:] = activated_other[...].astype(jnp.float32).T

    def pair(i, carry):
        rows = [turned[pl.ds(pl.multiple_of(order[2 * i + j] * 24, 8), 24), :] for j in range(2)]
        out[pl.ds(pl.multiple_of(i * 48, 48), 48), :] = concat(*rows).astype(jnp.bfloat16)
        return carry

    lax.fori_loop(0, 16, pair, 0)


def turn_act(order, activated, activated_other):
    return pl.pallas_call(
        turn_act_kernel,
        grid_spec=pltpu.PrefetchScalarGridSpec(
            num_scalar_prefetch=1,
            grid=(1,),
            in_specs=[whole_block(activated.shape)] * 2,
            out_specs=whole_block((768, 640)),
            scratch_shapes=[pltpu.VMEM((768, 640), jnp.float32)],
        ),
        out_shape=jax.ShapeDtypeStruct((768, 640), jnp.bfloat16),
        compiler_params=pltpu.CompilerParams(vmem_limit_bytes=16 * 2**20),
        name="turn_act",
    )(order, activated, activated_other)


def gradient_kernel(turned, turned_act, pre, out_grad, out):
    def store(lanes, product, power):
        factor = jnp.exp2(-power)
        out[384:, lanes] = jnp.broadcast_to(power, (16, 384))
        for first, size, part in product:
            out[first : first + size, lanes] = part * factor

    def tap_of(k, carry):
        product = jnp.dot(turned[k], pre[...], preferred_element_type=jnp.float32)
        power = power_of(jnp.max(jnp.abs(product), axis=0, keepdims=True))
        store(pl.ds(pl.multiple_of(k * 384, 384), 384), [(0, 384, product)], power)
        return carry

    lax.fori_loop(0, 3, tap_of, 0)
    product = jnp.dot(turned_act[...], out_grad[...], preferred_element_type=jnp.float32)
    peak = jnp.max(jnp.abs(product), axis=0, keepdims=True)
    parts = [
        (48 * i + 24 * part, 24, product[24 * i : 24 * i + 24, 384 * part : 384 * part + 384])
        for i in range(8)
        for part in range(2)
    ]
    store(slice(1152, 1536), parts, power_of(jnp.maximum(peak[:, :384], peak[:, 384:])))


def gradient_chunk(index, turned, turned_act, pre, out_grad):
    return pl.pallas_call(
        gradient_kernel,
        grid=(1,),
        in_specs=[
            pl.BlockSpec((3, 384, 640), lambda i: (0, index, 0)),
            pl.BlockSpec((192, 640), lambda i: (index, 0)),
            whole_block(pre.shape),
            whole_block(out_grad.shape),
        ],
        out_specs=pl.BlockSpec(memory_space=pltpu.VMEM),
        out_shape=pltpu.VMEM((400, 1536), jnp.float32),
        compiler_params=pltpu.CompilerParams(vmem_limit_bytes=20 * 2**20),
        name="gradient",
    )(turned, turned_act, pre, out_grad)


def in_order(core, own, other, axis):
    return jnp.where(
        core == 0,
        jnp.concatenate([own, other], axis=axis),
        jnp.concatenate([other, own], axis=axis),
    )


def half_of(value, index, axis):
    size = value.shape[axis] // 2
    return lax.dynamic_slice_in_dim(value, index * size, size, axis)


def shards(activations, teacher_maps, projection, dilated_weight, pointwise_weight):
    teacher = lax.axis_index("teacher")
    seq = lax.axis_index("seq")
    yh, core = teacher // 2, teacher % 2
    x, yl, z = seq // 8, (seq // 4) % 2, seq % 4
    wins, bins, channels = activations.shape
    rows = wins * bins
    total_rows = rows * 128
    branch = dilated_weight.shape[2]
    half = branch // 2
    inputs = activations.reshape(rows, channels)
    forward = [(g * 32 + i, g * 32 + i + 1) for g in range(4) for i in range(31)]
    backward = [(b, a) for a, b in forward]
    low = send(activations[:, -TAP_DILATION:], forward)
    high = send(activations[:, :TAP_DILATION], backward)
    padded = jnp.concatenate([low, activations, high], axis=1)
    padded_other = send(padded, CORE)
    order = block_order(core, x, yl, z)
    order_other = block_order(1 - core, x, yl, z)
    cores = jnp.stack([core, 1 - core]).astype(jnp.int32)

    own_dil = lax.dynamic_slice_in_dim(dilated_weight, core * half, half, 2).reshape(48, 3 * half)
    own_pw = half_of(pointwise_weight, core, 1)
    own_block = jnp.concatenate([own_dil, concat(own_pw[:, :half], own_pw[:, half:])], axis=1)

    wide = channels // 2
    block = jnp.concatenate([projection[0], own_block], axis=1)[None]
    near = concat(block, send(block, NEAR))
    first = ring_gather(near, True)
    first_a, first_b, first_w = [
        concat(*[v[:, :, low:high] for v in first])
        for low, high in ((0, wide), (wide, channels), (channels, 2 * channels))
    ]
    pieces_a = ring_gather(first_a, False)
    pieces_b = ring_gather(first_b, False)
    pieces_w = ring_gather(first_w, False)
    pieces_other = [send(pieces_w[0], CORE)]
    pieces_other += [send(piece, CORE) for piece in pieces_w[1:]]

    inputs_f = inputs.astype(jnp.float32)
    local = jnp.concatenate([jnp.sum(inputs_f, axis=0), jnp.sum(inputs_f * inputs_f, axis=0)])
    sums = sum_everywhere(local.reshape(24, 128)).reshape(2, channels)
    channel_mean = sums[0] / total_rows
    channel_var = sums[1] / total_rows - channel_mean * channel_mean
    scale = lax.rsqrt(channel_var + 1e-05)
    place = lax.broadcasted_iota(jnp.int32, (1, bins + 2 * TAP_DILATION, 1), 1) + seq * bins
    inside = (place >= TAP_DILATION) & (place < 32 * bins + TAP_DILATION)

    def hidden_of(value):
        normed = (value.astype(jnp.float32) - channel_mean) * scale
        return jnp.where(inside, gelu_tanh(normed), 0.0).astype(jnp.bfloat16)

    hidden, hidden_other = hidden_of(padded), hidden_of(padded_other)

    maps = teacher_maps.reshape(4, rows, teacher_maps.shape[3])
    far_groups = jnp.stack([(1 - yh) * 2 + 1 - core, (1 - yh) * 2 + core]).astype(jnp.int32)
    near_groups = jnp.stack([yh * 2 + 1 - core, yh * 2 + core]).astype(jnp.int32)
    arrived = []
    for pieces in (pieces_a, pieces_b):
        other, own = teacher_terms(order, far_groups, maps, pieces, 16)
        other = send(other, CORE)
        power = jnp.maximum(own[320:321], other[320:321]).astype(jnp.float32)
        packed = pack(own[:320].astype(jnp.float32) + other[:320].astype(jnp.float32), power)
        arrived.append(send(packed, FAR))
    other, own = teacher_terms(order, near_groups, maps, pieces_a + pieces_b, 0)

    other = send(other, CORE)

    preact, activated, *base, point_a, point_b = forward_pass(
        jnp.stack([order, order_other]), cores, [hidden, inputs, own, other], pieces_w + pieces_other
    )
    out_grads, squared = [], 0.0
    for value, terms in zip(base, arrived, strict=True):
        misfit = value - unpack(terms) * 0.25
        squared = squared + jnp.sum(misfit * misfit)
        out_grads.append((misfit / channels).astype(jnp.bfloat16))
    back_grad = sum(
        lax.dot_general(v, w, (((1,), (1,)), ((), ())), preferred_element_type=jnp.float32)
        for v, w in zip(out_grads, (point_a, point_b), strict=True)
    )
    preact_grad = (back_grad * gelu_slope(preact)).astype(jnp.bfloat16)

    turned = turn(order, hidden, hidden_other)
    turned_act = turn_act(order, activated, send(activated, CORE))
    out_own = jnp.where(core == 0, *out_grads)
    out_both = concat(out_own, send(jnp.where(core == 0, *out_grads[::-1]), CORE))
    pre_both = concat(
        half_of(preact_grad, core, 1), send(half_of(preact_grad, 1 - core, 1), CORE)
    )
    arrived = []
    for index in (3, 1, 2, 0):
        chunk = gradient_chunk(index, turned, turned_act, pre_both, out_both)
        if index:
            arrived.append(send(chunk.astype(jnp.float16), RING[False, STEPS[index]]))
    loss = jnp.broadcast_to(after(squared, chunk), (8, 128))
    loss = loss + sum(send(loss, RING[False, step]) for step in STEPS[1:])
    block, loss = finish_reduce(*add_up(unpack(chunk), power_in(chunk), arrived), loss[:1, :1])
    other = send(block, CORE)
    loss = jnp.broadcast_to(loss, (8, 128))
    loss_mean = 0.5 * (loss + send(loss, CORE))[0, 0] / (channels * total_rows)

    def dilated_columns(v):
        return v[:, : 3 * half].reshape(48, 3, half)

    def pw_columns(v):
        v = v[:, 3 * half :].reshape(2, branch // 32, half)
        return v.transpose(1, 0, 2).reshape(branch // 32, branch)

    dilated_grad = in_order(core, dilated_columns(block), dilated_columns(other), 2)
    pointwise_grad = in_order(core, pw_columns(block), pw_columns(other), 1)
    return (loss_mean, dilated_grad, pointwise_grad)


def solution(mesh):
    in_specs = (
        P("teacher", "seq", None),
        P("teacher", None, "seq", None),
        P("teacher", "seq", None),
        P("seq", None, None),
        P("seq", None),
    )
    out_specs = (P(), P("seq", None, None), P("seq", None))

    return jax.shard_map(shards, mesh=mesh, in_specs=in_specs, out_specs=out_specs, check_vma=False)
```

```python
import jax
import jax.numpy as jnp
import numpy as np
from jax import lax
from jax.experimental import pallas as pl
from jax.experimental.pallas import tpu as pltpu
from jax.sharding import PartitionSpec as P


TAP_DILATION = 16
AXES = ("teacher", "seq")
SHAPE = (2, 2, 4, 2, 4)
STEPS = (0, -1, 1, 2)

slope_const = 0.7978845608
cubic_const = 0.044715


def pairs_of(move):
    pairs = []
    for source in range(int(np.prod(SHAPE))):
        at = [int(v) for v in np.unravel_index(source, SHAPE)]
        pairs.append((source, int(np.ravel_multi_index(move(*at), SHAPE))))
    return pairs


def along(first, step):
    def move(yh, core, x, yl, z):
        if (core == 0) == first:
            return (yh, core, (x + step) % 4, yl, z)
        return (yh, core, x, yl, (z + step) % 4)

    return pairs_of(move)


CORE = pairs_of(lambda yh, core, x, yl, z: (yh, 1 - core, x, yl, z))
FAR = pairs_of(lambda yh, core, x, yl, z: (1 - yh, core, x, yl, z))
NEAR = pairs_of(lambda yh, core, x, yl, z: (yh, core, x, 1 - yl, z))
FAR_NEAR = pairs_of(lambda yh, core, x, yl, z: (1 - yh, core, x, 1 - yl, z))
RING = {(first, step): along(first, step) for first in (True, False) for step in (1, -1, 2)}


def send(value, pairs):
    return lax.ppermute(value, AXES, pairs)


def gelu_tanh(value):
    inside = slope_const * (value + cubic_const * value * value * value)
    return 0.5 * value * (1.0 + jnp.tanh(inside))


def gelu_slope(value):
    inside = slope_const * (value + cubic_const * value * value * value)
    tangent = jnp.tanh(inside)
    return 0.5 * (1.0 + tangent) + 0.5 * value * (1.0 - tangent * tangent) * slope_const * (
        1.0 + 3.0 * cubic_const * value * value
    )


def block_order(core, x, yl, z):
    first = jnp.where(core == 0, x, z)
    second = jnp.where(core == 0, z, x)
    order = []
    for far in STEPS:
        for near in STEPS:
            for side in (0, 1):
                one = (first + near + 4) % 4
                two = (second + far + 4) % 4
                at_x = jnp.where(core == 0, one, two)
                at_z = jnp.where(core == 0, two, one)
                order.append((at_x * 2 + (yl + side) % 2) * 4 + at_z)
    return jnp.stack(order).astype(jnp.int32)


def concat(*values):
    return jnp.concatenate(values)


def after(value, *earlier):
    return lax.optimization_barrier((value, *earlier))[0]


def ring_gather(value, first):
    return [value] + [send(value, RING[first, step]) for step in (1, -1, 2)]


def power_of(peak):
    return jnp.clip(jnp.floor(jnp.log2(jnp.maximum(peak, 1e-30))) - 13.0, -110.0, 127.0)


def pack(value, power, loss=None):
    rows = jnp.broadcast_to(power, (16, value.shape[1]))
    if loss is not None:
        exponent = jnp.floor(jnp.log2(jnp.maximum(loss, 1e-30)))
        rest = loss * jnp.exp2(-exponent)
        upper = jnp.floor(rest * 512.0) / 512.0
        which = lax.broadcasted_iota(jnp.int32, rows.shape, 0)
        for row, part in enumerate((exponent, upper, (rest - upper) * 1024.0)):
            rows = jnp.where(which == row + 1, part, rows)
    scaled = (value * jnp.exp2(-power)).astype(jnp.float16)
    return concat(scaled, rows.astype(jnp.float16))


def power_in(packed):
    return packed[-16:-15].astype(jnp.float32)


def unpack(packed):
    return packed[:-16].astype(jnp.float32) * jnp.exp2(power_in(packed))


def loss_in(packed):
    exponent, upper, lower = [packed[row : row + 1].astype(jnp.float32) for row in (-15, -14, -13)]
    return jnp.exp2(exponent) * (upper + lower / 1024.0)


def sum_everywhere(value):
    value = value + send(value, CORE)
    value = value + send(value, NEAR) + send(value, FAR) + send(value, FAR_NEAR)
    for first in (True, False):
        value = value + send(value, RING[first, 1]) + send(value, RING[first, -1]) + send(value, RING[first, 2])
    return value


def add_up(own, own_power, arrived):
    power = own_power
    for packed in arrived:
        own = own + unpack(packed)
        power = jnp.maximum(power, power_in(packed))
    return own, power + 2.0


def finish_reduce(own, power, loss):
    rows = own.shape[0] // 8
    arrived = [
        send(pack(own[2 * rows * (i + 1) : 2 * rows * (i + 2)], power, loss), RING[True, step])
        for i, step in enumerate(STEPS[1:])
    ]
    own, power = add_up(own[: 2 * rows], power, arrived)
    loss = loss + sum(loss_in(packed) for packed in arrived)
    keep, give = pack(own[:rows], power, loss), pack(own[rows:], power, loss)
    arrived = [send(give, NEAR), send(keep, FAR), send(give, FAR_NEAR)]
    return add_up(own[:rows], power, arrived)[0], loss + sum(loss_in(packed) for packed in arrived)


def load_blocks(order, pieces, target, sem):
    for index, piece in enumerate(pieces):

        def start(at, carry, index=index, piece=piece):
            row = pl.multiple_of(order[8 * index + at] * 48, 16)
            pltpu.make_async_copy(piece.at[at], target(row), sem).start()
            return carry

        lax.fori_loop(0, 8, start, 0)


def teacher_kernel(order, groups, maps_other, maps_own, *refs):
    count = len(refs) - 4
    other, own, whole, sem = refs[count:]
    width = whole.shape[1]
    each = refs[0].shape[2]
    for part in range(count // 4):
        load_blocks(
            order,
            refs[4 * part : 4 * part + 4],
            lambda row, part=part: whole.at[pl.ds(row, 48), part * each : (part + 1) * each],
            sem,
        )
    pltpu.make_async_copy(whole, whole, sem).wait()

    def columns(i, carry):
        lanes = pl.ds(pl.multiple_of(i * 768, 768), 768)
        for maps, out in ((maps_other, other), (maps_own, own)):
            terms = jnp.dot(maps[0], whole[:, lanes], preferred_element_type=jnp.float32)
            out[:320, lanes] = terms.astype(jnp.bfloat16)
            if out.shape[0] > 320:
                power = power_of(jnp.max(jnp.abs(terms), axis=0, keepdims=True)) + 1.0
                out[320:, lanes] = jnp.broadcast_to(power, (16, 768)).astype(jnp.bfloat16)
        return carry

    lax.fori_loop(0, width // 768, columns, 0)


def teacher_terms(order, groups, maps, pieces, extra):
    rows, depth = maps.shape[1:]
    width = pieces[0].shape[2] * len(pieces) // 4
    return pl.pallas_call(
        teacher_kernel,
        grid_spec=pltpu.PrefetchScalarGridSpec(
            num_scalar_prefetch=2,
            grid=(1,),
            in_specs=[
                pl.BlockSpec((1, rows, depth), lambda i, order, groups: (groups[0], 0, 0)),
                pl.BlockSpec((1, rows, depth), lambda i, order, groups: (groups[1], 0, 0)),
            ]
            + [pl.BlockSpec(memory_space=pl.ANY)] * len(pieces),
            out_specs=[whole_block((rows + extra, width))] * 2,
            scratch_shapes=[pltpu.VMEM((depth, width), jnp.bfloat16), pltpu.SemaphoreType.DMA(())],
        ),
        out_shape=[jax.ShapeDtypeStruct((rows + extra, width), jnp.bfloat16)] * 2,
        compiler_params=pltpu.CompilerParams(vmem_limit_bytes=30 * 2**20),
        name="teacher",
    )(order, groups, maps, maps, *pieces)


def forward_kernel(orders, cores, hidden, inputs, near_own, near_other, *refs):
    pieces = refs[:8]
    preact, activated, base, point, whole, sems = refs[8:]
    for part in range(2):
        load_blocks(
            orders.at[part],
            pieces[4 * part : 4 * part + 4],
            lambda row, part=part: whole.at[part, pl.ds(row, 48), :],
            sems.at[part],
        )

    def half(part, carry):
        pltpu.make_async_copy(whole.at[part], whole.at[part], sems.at[part]).wait()
        core = cores[part]

        def rows_of(pair, inner):
            rows = whole[part, pl.ds(pl.multiple_of(96 * pair, 96), 96), 1152:].astype(jnp.float32)
            for side in range(2):
                point[core, pl.ds(pl.multiple_of(48 * pair, 48), 48), side * 384 : side * 384 + 384] = concat(
                    rows[24 * side : 24 * side + 24], rows[48 + 24 * side : 72 + 24 * side]
                ).astype(jnp.bfloat16)
            return inner

        lax.fori_loop(0, 16, rows_of, 0)
        running = jnp.zeros((320, 384), jnp.float32)
        for k in range(3):
            tap = hidden[:, k * TAP_DILATION : k * TAP_DILATION + 64, :].reshape(320, 1536)
            running = running + jnp.dot(
                tap, whole[part, :, k * 384 : k * 384 + 384], preferred_element_type=jnp.float32
            )
        lanes = pl.ds(pl.multiple_of(core * 384, 128), 384)
        preact[:, lanes] = running
        activated[:, lanes] = gelu_tanh(running).astype(jnp.bfloat16)
        return carry

    lax.fori_loop(0, 2, half, 0)

    def student(part, carry):
        lanes = pl.ds(pl.multiple_of(part * 768, 768), 768)
        near = near_own[:, lanes].astype(jnp.float32) + near_other[:, lanes].astype(jnp.float32)
        base[part] = (
            inputs[:, lanes].astype(jnp.float32)
            + jnp.dot(activated[...], point[part], preferred_element_type=jnp.float32)
        ) - near * 0.25
        return carry

    lax.fori_loop(0, 2, student, 0)


def whole_block(shape):
    return pl.BlockSpec(shape, lambda *i: (0,) * len(shape))


def forward_pass(orders, cores, arrays, pieces):
    outs = [((320, 768), jnp.float32), ((320, 768), jnp.bfloat16)]
    outs += [((2, 320, 768), jnp.float32), ((2, 768, 768), jnp.bfloat16)]
    return pl.pallas_call(
        forward_kernel,
        grid_spec=pltpu.PrefetchScalarGridSpec(
            num_scalar_prefetch=2,
            grid=(1,),
            in_specs=[whole_block(array.shape) for array in arrays]
            + [pl.BlockSpec(memory_space=pl.ANY)] * len(pieces),
            out_specs=[whole_block(shape) for shape, _ in outs],
            scratch_shapes=[
                pltpu.VMEM((2, 1536, 1536), jnp.bfloat16),
                pltpu.SemaphoreType.DMA((2,)),
            ],
        ),
        out_shape=[pltpu.HBM(shape, kind) for shape, kind in outs],
        compiler_params=pltpu.CompilerParams(vmem_limit_bytes=45 * 2**20),
        name="forward",
    )(orders, cores, *arrays, *pieces)


def turn_kernel(order, hidden, hidden_other, out, turned):
    def tap_of(k, carry):
        low = pl.multiple_of(k * TAP_DILATION, TAP_DILATION)
        for part, source in enumerate((hidden, hidden_other)):
            tap = source[:, pl.ds(low, 64), :].reshape(320, 1536)
            turned[:, part * 320 : part * 320 + 320] = tap.T

        def slot(i, inner):
            row = pl.multiple_of(order[i] * 48, 16)
            to = pl.multiple_of(i * 48, 48)
            out[k, pl.ds(to, 48), :] = turned[pl.ds(row, 48), :]
            return inner

        return lax.fori_loop(0, 32, slot, carry)

    lax.fori_loop(0, 3, tap_of, 0)


def turn(order, hidden, hidden_other):
    return pl.pallas_call(
        turn_kernel,
        grid_spec=pltpu.PrefetchScalarGridSpec(
            num_scalar_prefetch=1,
            grid=(1,),
            in_specs=[whole_block(hidden.shape)] * 2,
            out_specs=whole_block((3, 1536, 640)),
            scratch_shapes=[pltpu.VMEM((1536, 640), jnp.bfloat16)],
        ),
        out_shape=pltpu.HBM((3, 1536, 640), jnp.bfloat16),
        compiler_params=pltpu.CompilerParams(vmem_limit_bytes=30 * 2**20),
        name="turn",
    )(order, hidden, hidden_other)


def turn_act_kernel(order, activated, activated_other, out, turned):
    turned[:, :320] = activated[...].astype(jnp.float32).T
    turned[:, 320:] = activated_other[...].astype(jnp.float32).T

    def pair(i, carry):
        rows = [turned[pl.ds(pl.multiple_of(order[2 * i + j] * 24, 8), 24), :] for j in range(2)]
        out[pl.ds(pl.multiple_of(i * 48, 48), 48), :] = concat(*rows).astype(jnp.bfloat16)
        return carry

    lax.fori_loop(0, 16, pair, 0)


def turn_act(order, activated, activated_other):
    return pl.pallas_call(
        turn_act_kernel,
        grid_spec=pltpu.PrefetchScalarGridSpec(
            num_scalar_prefetch=1,
            grid=(1,),
            in_specs=[whole_block(activated.shape)] * 2,
            out_specs=whole_block((768, 640)),
            scratch_shapes=[pltpu.VMEM((768, 640), jnp.float32)],
        ),
        out_shape=jax.ShapeDtypeStruct((768, 640), jnp.bfloat16),
        compiler_params=pltpu.CompilerParams(vmem_limit_bytes=16 * 2**20),
        name="turn_act",
    )(order, activated, activated_other)


def gradient_kernel(turned, turned_act, pre, out_grad, out, scratch):
    def scale(lanes, peak):
        power = power_of(peak)
        out[384:, lanes] = jnp.broadcast_to(power, (16, 384))
        return jnp.exp2(-power)

    def tap_of(k, carry):
        product = jnp.dot(turned[k], pre[...], preferred_element_type=jnp.float32)
        lanes = pl.ds(pl.multiple_of(k * 384, 384), 384)
        out[:384, lanes] = product * scale(lanes, jnp.max(jnp.abs(product), axis=0, keepdims=True))
        return carry

    lax.fori_loop(0, 3, tap_of, 0)
    product = jnp.dot(turned_act[...], out_grad[...], preferred_element_type=jnp.float32)
    scratch[...] = product
    peak = jnp.max(jnp.abs(product), axis=0, keepdims=True)
    factor = scale(slice(1152, 1536), jnp.maximum(peak[:, :384], peak[:, 384:]))

    def rows_of(i, carry):
        rows = scratch[pl.ds(pl.multiple_of(24 * i, 8), 24), :]
        to = pl.multiple_of(48 * i, 8)
        out[pl.ds(to, 24), 1152:] = rows[:, :384] * factor
        out[pl.ds(to + 24, 24), 1152:] = rows[:, 384:] * factor
        return carry

    lax.fori_loop(0, 8, rows_of, 0)


def gradient_chunk(index, turned, turned_act, pre, out_grad):
    return pl.pallas_call(
        gradient_kernel,
        grid=(1,),
        in_specs=[
            pl.BlockSpec((3, 384, 640), lambda i: (0, index, 0)),
            pl.BlockSpec((192, 640), lambda i: (index, 0)),
            whole_block(pre.shape),
            whole_block(out_grad.shape),
        ],
        out_specs=pl.BlockSpec(memory_space=pltpu.VMEM),
        out_shape=pltpu.VMEM((400, 1536), jnp.float32),
        scratch_shapes=[pltpu.VMEM((192, 768), jnp.float32)],
        compiler_params=pltpu.CompilerParams(vmem_limit_bytes=20 * 2**20),
        name="gradient",
    )(turned, turned_act, pre, out_grad)


def in_order(core, own, other, axis):
    return jnp.where(
        core == 0,
        jnp.concatenate([own, other], axis=axis),
        jnp.concatenate([other, own], axis=axis),
    )


def half_of(value, index, axis):
    size = value.shape[axis] // 2
    return lax.dynamic_slice_in_dim(value, index * size, size, axis)


def shards(activations, teacher_maps, projection, dilated_weight, pointwise_weight):
    teacher = lax.axis_index("teacher")
    seq = lax.axis_index("seq")
    yh, core = teacher // 2, teacher % 2
    x, yl, z = seq // 8, (seq // 4) % 2, seq % 4
    wins, bins, channels = activations.shape
    rows = wins * bins
    total_rows = rows * 128
    branch = dilated_weight.shape[2]
    half = branch // 2
    inputs = activations.reshape(rows, channels)
    forward = [(g * 32 + i, g * 32 + i + 1) for g in range(4) for i in range(31)]
    backward = [(b, a) for a, b in forward]
    low = send(activations[:, -TAP_DILATION:], forward)
    high = send(activations[:, :TAP_DILATION], backward)
    padded = jnp.concatenate([low, activations, high], axis=1)
    padded_other = send(padded, CORE)
    order = block_order(core, x, yl, z)
    order_other = block_order(1 - core, x, yl, z)
    cores = jnp.stack([core, 1 - core]).astype(jnp.int32)

    own_dil = lax.dynamic_slice_in_dim(dilated_weight, core * half, half, 2).reshape(48, 3 * half)
    own_pw = half_of(pointwise_weight, core, 1)
    own_block = jnp.concatenate([own_dil, concat(own_pw[:, :half], own_pw[:, half:])], axis=1)

    wide = channels // 2
    block = jnp.concatenate([projection[0], own_block], axis=1)[None]
    near = concat(block, send(block, NEAR))
    first = ring_gather(near, True)
    first_a, first_b, first_w = [
        concat(*[v[:, :, low:high] for v in first])
        for low, high in ((0, wide), (wide, channels), (channels, 2 * channels))
    ]
    pieces_a = ring_gather(first_a, False)
    pieces_b = ring_gather(first_b, False)
    pieces_w = ring_gather(first_w, False)
    pieces_other = [send(pieces_w[0], CORE)]
    pieces_other += [send(piece, CORE) for piece in pieces_w[1:]]

    inputs_f = inputs.astype(jnp.float32)
    local = jnp.concatenate([jnp.sum(inputs_f, axis=0), jnp.sum(inputs_f * inputs_f, axis=0)])
    sums = sum_everywhere(local.reshape(24, 128)).reshape(2, channels)
    channel_mean = sums[0] / total_rows
    channel_var = sums[1] / total_rows - channel_mean * channel_mean
    scale = lax.rsqrt(channel_var + 1e-05)
    place = lax.broadcasted_iota(jnp.int32, (1, bins + 2 * TAP_DILATION, 1), 1) + seq * bins
    inside = (place >= TAP_DILATION) & (place < 32 * bins + TAP_DILATION)

    def hidden_of(value):
        normed = (value.astype(jnp.float32) - channel_mean) * scale
        return jnp.where(inside, gelu_tanh(normed), 0.0).astype(jnp.bfloat16)

    hidden, hidden_other = hidden_of(padded), hidden_of(padded_other)

    maps = teacher_maps.reshape(4, rows, teacher_maps.shape[3])
    far_groups = jnp.stack([(1 - yh) * 2 + 1 - core, (1 - yh) * 2 + core]).astype(jnp.int32)
    near_groups = jnp.stack([yh * 2 + 1 - core, yh * 2 + core]).astype(jnp.int32)
    arrived = []
    for pieces in (pieces_a, pieces_b):
        other, own = teacher_terms(order, far_groups, maps, pieces, 16)
        other = send(other, CORE)
        power = jnp.maximum(own[320:321], other[320:321]).astype(jnp.float32)
        packed = pack(own[:320].astype(jnp.float32) + other[:320].astype(jnp.float32), power)
        arrived.append(send(packed, FAR))
    other, own = teacher_terms(order, near_groups, maps, pieces_a + pieces_b, 0)

    other = send(other, CORE)

    preact, activated, base, point = forward_pass(
        jnp.stack([order, order_other]), cores, [hidden, inputs, own, other], pieces_w + pieces_other
    )
    out_grads, squared = [], []
    for value, terms in zip(base, arrived, strict=True):
        misfit = value - unpack(terms) * 0.25
        squared.append(jnp.sum(misfit * misfit, axis=0))
        out_grads.append((misfit / channels).astype(jnp.bfloat16))
    back_grad = sum(
        lax.dot_general(v, w, (((1,), (1,)), ((), ())), preferred_element_type=jnp.float32)
        for v, w in zip(out_grads, point, strict=True)
    )
    preact_grad = (back_grad * gelu_slope(preact)).astype(jnp.bfloat16)

    turned = turn(order, hidden, hidden_other)
    turned_act = turn_act(order, activated, send(activated, CORE))
    out_own = jnp.where(core == 0, *out_grads)
    swapped = send(
        jnp.concatenate(
            [jnp.where(core == 0, *out_grads[::-1]), half_of(preact_grad, 1 - core, 1)], axis=1
        ),
        CORE,
    )
    out_both = concat(out_own, swapped[:, :wide])
    pre_both = concat(half_of(preact_grad, core, 1), swapped[:, wide:])
    arrived = []
    for index in (3, 1, 2, 0):
        chunk = gradient_chunk(index, turned, turned_act, pre_both, out_both)
        if index:
            arrived.append(send(chunk.astype(jnp.float16), RING[False, STEPS[index]]))
    loss = jnp.broadcast_to(after(concat(*squared), chunk), (8, channels))
    loss = loss + sum(send(loss, RING[False, step]) for step in STEPS[1:])
    block, loss = finish_reduce(*add_up(unpack(chunk), power_in(chunk), arrived), loss[:1])
    other = send(concat(block, jnp.broadcast_to(loss, (8, channels))), CORE)
    loss_mean = 0.5 * jnp.sum(loss + other[48:49]) / (channels * total_rows)
    other = other[:48]

    def dilated_columns(v):
        return v[:, : 3 * half].reshape(48, 3, half)

    def pw_columns(v):
        v = v[:, 3 * half :].reshape(2, branch // 32, half)
        return v.transpose(1, 0, 2).reshape(branch // 32, branch)

    dilated_grad = in_order(core, dilated_columns(block), dilated_columns(other), 2)
    pointwise_grad = in_order(core, pw_columns(block), pw_columns(other), 1)
    return (loss_mean, dilated_grad, pointwise_grad)


def solution(mesh):
    in_specs = (
        P("teacher", "seq", None),
        P("teacher", None, "seq", None),
        P("teacher", "seq", None),
        P("seq", None, None),
        P("seq", None),
    )
    out_specs = (P(), P("seq", None, None), P("seq", None))

    return jax.shard_map(shards, mesh=mesh, in_specs=in_specs, out_specs=out_specs, check_vma=False)
```

```python
import jax
import jax.numpy as jnp
import numpy as np
from jax import lax
from jax.experimental import pallas as pl
from jax.experimental.pallas import tpu as pltpu
from jax.sharding import PartitionSpec as P


TAP_DILATION = 16
AXES = ("teacher", "seq")
SHAPE = (2, 2, 4, 2, 4)
STEPS = (0, -1, 1, 2)

slope_const = 0.7978845608
cubic_const = 0.044715


def pairs_of(move):
    pairs = []
    for source in range(int(np.prod(SHAPE))):
        at = [int(v) for v in np.unravel_index(source, SHAPE)]
        pairs.append((source, int(np.ravel_multi_index(move(*at), SHAPE))))
    return pairs


def along(first, step):
    def move(yh, core, x, yl, z):
        if (core == 0) == first:
            return (yh, core, (x + step) % 4, yl, z)
        return (yh, core, x, yl, (z + step) % 4)

    return pairs_of(move)


CORE = pairs_of(lambda yh, core, x, yl, z: (yh, 1 - core, x, yl, z))
FAR = pairs_of(lambda yh, core, x, yl, z: (1 - yh, core, x, yl, z))
NEAR = pairs_of(lambda yh, core, x, yl, z: (yh, core, x, 1 - yl, z))
FAR_NEAR = pairs_of(lambda yh, core, x, yl, z: (1 - yh, core, x, 1 - yl, z))
RING = {(first, step): along(first, step) for first in (True, False) for step in (1, -1, 2)}


def send(value, pairs):
    return lax.ppermute(value, AXES, pairs)


def gelu_tanh(value):
    inside = slope_const * (value + cubic_const * value * value * value)
    return 0.5 * value * (1.0 + jnp.tanh(inside))


def gelu_slope(value):
    inside = slope_const * (value + cubic_const * value * value * value)
    tangent = jnp.tanh(inside)
    return 0.5 * (1.0 + tangent) + 0.5 * value * (1.0 - tangent * tangent) * slope_const * (
        1.0 + 3.0 * cubic_const * value * value
    )


def block_order(core, x, yl, z):
    first = jnp.where(core == 0, x, z)
    second = jnp.where(core == 0, z, x)
    order = []
    for far in STEPS:
        for near in STEPS:
            for side in (0, 1):
                one = (first + near + 4) % 4
                two = (second + far + 4) % 4
                at_x = jnp.where(core == 0, one, two)
                at_z = jnp.where(core == 0, two, one)
                order.append((at_x * 2 + (yl + side) % 2) * 4 + at_z)
    return jnp.stack(order).astype(jnp.int32)


def concat(*values):
    return jnp.concatenate(values)


def after(value, *earlier):
    return lax.optimization_barrier((value, *earlier))[0]


def ring_gather(value, first):
    return [value] + [send(value, RING[first, step]) for step in (1, -1, 2)]


def power_of(peak):
    return jnp.clip(jnp.floor(jnp.log2(jnp.maximum(peak, 1e-30))) - 13.0, -110.0, 127.0)


def pack(value, power, loss=None):
    rows = jnp.broadcast_to(power, (16, value.shape[1]))
    if loss is not None:
        exponent = jnp.floor(jnp.log2(jnp.maximum(loss, 1e-30)))
        rest = loss * jnp.exp2(-exponent)
        upper = jnp.floor(rest * 512.0) / 512.0
        which = lax.broadcasted_iota(jnp.int32, rows.shape, 0)
        for row, part in enumerate((exponent, upper, (rest - upper) * 1024.0)):
            rows = jnp.where(which == row + 1, part, rows)
    scaled = (value * jnp.exp2(-power)).astype(jnp.float16)
    return concat(scaled, rows.astype(jnp.float16))


def power_in(packed):
    return packed[-16:-15].astype(jnp.float32)


def unpack(packed):
    return packed[:-16].astype(jnp.float32) * jnp.exp2(power_in(packed))


def loss_in(packed):
    exponent, upper, lower = [packed[row : row + 1].astype(jnp.float32) for row in (-15, -14, -13)]
    return jnp.exp2(exponent) * (upper + lower / 1024.0)


def sum_everywhere(value):
    value = value + send(value, CORE)
    value = value + send(value, NEAR)
    value = value + send(value, FAR)
    for first in (True, False):
        value = value + send(value, RING[first, 1]) + send(value, RING[first, -1]) + send(value, RING[first, 2])
    return value


def add_up(own, own_power, arrived):
    power = own_power
    for packed in arrived:
        own = own + unpack(packed)
        power = jnp.maximum(power, power_in(packed))
    return own, power + 2.0


def finish_reduce(own, power, loss):
    rows = own.shape[0] // 8
    arrived = [
        send(pack(own[2 * rows * (i + 1) : 2 * rows * (i + 2)], power, loss), RING[True, step])
        for i, step in enumerate(STEPS[1:])
    ]
    own, power = add_up(own[: 2 * rows], power, arrived)
    loss = loss + sum(loss_in(packed) for packed in arrived)
    keep, give = pack(own[:rows], power, loss), pack(own[rows:], power, loss)
    arrived = [send(give, NEAR), send(keep, FAR), send(give, FAR_NEAR)]
    return add_up(own[:rows], power, arrived)[0], loss + sum(loss_in(packed) for packed in arrived)


def load_blocks(order, pieces, target, sem):
    for index, piece in enumerate(pieces):

        def start(at, carry, index=index, piece=piece):
            row = pl.multiple_of(order[8 * index + at] * 48, 16)
            pltpu.make_async_copy(piece.at[at], target(row), sem).start()
            return carry

        lax.fori_loop(0, 8, start, 0)


def teacher_kernel(order, groups, maps, *refs):
    count = len(refs) - 4
    other, own, whole, sem = refs[count:]
    width = whole.shape[1]
    each = refs[0].shape[2]
    step = pl.program_id(0)

    @pl.when(step == 0)
    def _():
        for part in range(count // 4):
            load_blocks(
                order,
                refs[4 * part : 4 * part + 4],
                lambda row, part=part: whole.at[pl.ds(row, 48), part * each : (part + 1) * each],
                sem,
            )
        pltpu.make_async_copy(whole, whole, sem).wait()

    def columns(i, carry):
        lanes = pl.ds(pl.multiple_of(i * 768, 768), 768)
        terms = jnp.dot(maps[0], whole[:, lanes], preferred_element_type=jnp.float32)
        power = power_of(jnp.max(jnp.abs(terms), axis=0, keepdims=True)) + 1.0
        for index, out in enumerate((other, own)):

            @pl.when(step == index)
            def _(out=out):
                out[:320, lanes] = terms.astype(jnp.bfloat16)
                if out.shape[0] > 320:
                    out[320:, lanes] = jnp.broadcast_to(power, (16, 768)).astype(jnp.bfloat16)

        return carry

    lax.fori_loop(0, width // 768, columns, 0)


def teacher_terms(order, groups, maps, pieces, extra):
    rows, depth = maps.shape[1:]
    width = pieces[0].shape[2] * len(pieces) // 4
    return pl.pallas_call(
        teacher_kernel,
        grid_spec=pltpu.PrefetchScalarGridSpec(
            num_scalar_prefetch=2,
            grid=(2,),
            in_specs=[pl.BlockSpec((1, rows, depth), lambda i, order, groups: (groups[i], 0, 0))]
            + [pl.BlockSpec(memory_space=pl.ANY)] * len(pieces),
            out_specs=[whole_block((rows + extra, width))] * 2,
            scratch_shapes=[pltpu.VMEM((depth, width), jnp.bfloat16), pltpu.SemaphoreType.DMA(())],
        ),
        out_shape=[jax.ShapeDtypeStruct((rows + extra, width), jnp.bfloat16)] * 2,
        compiler_params=pltpu.CompilerParams(vmem_limit_bytes=30 * 2**20),
        name="teacher",
    )(order, groups, maps, *pieces)


def forward_kernel(orders, cores, hidden, inputs, near_own, near_other, *refs):
    pieces = refs[:8]
    preact, activated, base, point, whole, sems = refs[8:]
    for part in range(2):
        load_blocks(
            orders.at[part],
            pieces[4 * part : 4 * part + 4],
            lambda row, part=part: whole.at[part, pl.ds(row, 48), :],
            sems.at[part],
        )

    def half(part, carry):
        pltpu.make_async_copy(whole.at[part], whole.at[part], sems.at[part]).wait()
        core = cores[part]

        def rows_of(pair, inner):
            rows = whole[part, pl.ds(pl.multiple_of(96 * pair, 96), 96), 1152:].astype(jnp.float32)
            for side in range(2):
                point[core, pl.ds(pl.multiple_of(48 * pair, 48), 48), side * 384 : side * 384 + 384] = concat(
                    rows[24 * side : 24 * side + 24], rows[48 + 24 * side : 72 + 24 * side]
                ).astype(jnp.bfloat16)
            return inner

        lax.fori_loop(0, 16, rows_of, 0)
        running = jnp.zeros((320, 384), jnp.float32)
        for k in range(3):
            tap = hidden[:, k * TAP_DILATION : k * TAP_DILATION + 64, :].reshape(320, 1536)
            running = running + jnp.dot(
                tap, whole[part, :, k * 384 : k * 384 + 384], preferred_element_type=jnp.float32
            )
        lanes = pl.ds(pl.multiple_of(core * 384, 128), 384)
        preact[:, lanes] = running
        activated[:, lanes] = gelu_tanh(running).astype(jnp.bfloat16)
        return carry

    lax.fori_loop(0, 2, half, 0)

    def student(part, carry):
        lanes = pl.ds(pl.multiple_of(part * 768, 768), 768)
        near = near_own[:, lanes].astype(jnp.float32) + near_other[:, lanes].astype(jnp.float32)
        base[part] = (
            inputs[:, lanes].astype(jnp.float32)
            + jnp.dot(activated[...], point[part], preferred_element_type=jnp.float32)
        ) - near * 0.25
        return carry

    lax.fori_loop(0, 2, student, 0)


def whole_block(shape):
    return pl.BlockSpec(shape, lambda *i: (0,) * len(shape))


def forward_pass(orders, cores, arrays, pieces):
    outs = [((320, 768), jnp.float32), ((320, 768), jnp.bfloat16)]
    outs += [((2, 320, 768), jnp.float32), ((2, 768, 768), jnp.bfloat16)]
    return pl.pallas_call(
        forward_kernel,
        grid_spec=pltpu.PrefetchScalarGridSpec(
            num_scalar_prefetch=2,
            grid=(1,),
            in_specs=[whole_block(array.shape) for array in arrays]
            + [pl.BlockSpec(memory_space=pl.ANY)] * len(pieces),
            out_specs=[whole_block(shape) for shape, _ in outs],
            scratch_shapes=[
                pltpu.VMEM((2, 1536, 1536), jnp.bfloat16),
                pltpu.SemaphoreType.DMA((2,)),
            ],
        ),
        out_shape=[pltpu.HBM(shape, kind) for shape, kind in outs],
        compiler_params=pltpu.CompilerParams(vmem_limit_bytes=45 * 2**20),
        name="forward",
    )(orders, cores, *arrays, *pieces)


def turn_kernel(order, hidden, hidden_other, out, turned):
    def tap_of(k, carry):
        low = pl.multiple_of(k * TAP_DILATION, TAP_DILATION)
        for part, source in enumerate((hidden, hidden_other)):
            tap = source[:, pl.ds(low, 64), :].reshape(320, 1536)
            turned[:, part * 320 : part * 320 + 320] = tap.T

        def slot(i, inner):
            row = pl.multiple_of(order[i] * 48, 16)
            to = pl.multiple_of(i * 48, 48)
            out[k, pl.ds(to, 48), :] = turned[pl.ds(row, 48), :]
            return inner

        return lax.fori_loop(0, 32, slot, carry)

    lax.fori_loop(0, 3, tap_of, 0)


def turn(order, hidden, hidden_other):
    return pl.pallas_call(
        turn_kernel,
        grid_spec=pltpu.PrefetchScalarGridSpec(
            num_scalar_prefetch=1,
            grid=(1,),
            in_specs=[whole_block(hidden.shape)] * 2,
            out_specs=whole_block((3, 1536, 640)),
            scratch_shapes=[pltpu.VMEM((1536, 640), jnp.bfloat16)],
        ),
        out_shape=pltpu.HBM((3, 1536, 640), jnp.bfloat16),
        compiler_params=pltpu.CompilerParams(vmem_limit_bytes=30 * 2**20),
        name="turn",
    )(order, hidden, hidden_other)


def turn_act_kernel(order, activated, activated_other, out, turned):
    turned[:, :320] = activated[...].astype(jnp.float32).T
    turned[:, 320:] = activated_other[...].astype(jnp.float32).T

    def pair(i, carry):
        rows = [turned[pl.ds(pl.multiple_of(order[2 * i + j] * 24, 8), 24), :] for j in range(2)]
        out[pl.ds(pl.multiple_of(i * 48, 48), 48), :] = concat(*rows).astype(jnp.bfloat16)
        return carry

    lax.fori_loop(0, 16, pair, 0)


def turn_act(order, activated, activated_other):
    return pl.pallas_call(
        turn_act_kernel,
        grid_spec=pltpu.PrefetchScalarGridSpec(
            num_scalar_prefetch=1,
            grid=(1,),
            in_specs=[whole_block(activated.shape)] * 2,
            out_specs=whole_block((768, 640)),
            scratch_shapes=[pltpu.VMEM((768, 640), jnp.float32)],
        ),
        out_shape=jax.ShapeDtypeStruct((768, 640), jnp.bfloat16),
        compiler_params=pltpu.CompilerParams(vmem_limit_bytes=16 * 2**20),
        name="turn_act",
    )(order, activated, activated_other)


def gradient_kernel(turned, turned_act, pre, out_grad, out, scratch):
    def scale(lanes, peak):
        power = power_of(peak)
        out[384:, lanes] = jnp.broadcast_to(power, (16, 384))
        return jnp.exp2(-power)

    def tap_of(k, carry):
        product = jnp.dot(turned[k], pre[...], preferred_element_type=jnp.float32)
        lanes = pl.ds(pl.multiple_of(k * 384, 384), 384)
        out[:384, lanes] = product * scale(lanes, jnp.max(jnp.abs(product), axis=0, keepdims=True))
        return carry

    lax.fori_loop(0, 3, tap_of, 0)
    product = jnp.dot(turned_act[...], out_grad[...], preferred_element_type=jnp.float32)
    scratch[...] = product
    peak = jnp.max(jnp.abs(product), axis=0, keepdims=True)
    factor = scale(slice(1152, 1536), jnp.maximum(peak[:, :384], peak[:, 384:]))

    def rows_of(i, carry):
        rows = scratch[pl.ds(pl.multiple_of(24 * i, 8), 24), :]
        to = pl.multiple_of(48 * i, 8)
        out[pl.ds(to, 24), 1152:] = rows[:, :384] * factor
        out[pl.ds(to + 24, 24), 1152:] = rows[:, 384:] * factor
        return carry

    lax.fori_loop(0, 8, rows_of, 0)


def gradient_chunk(index, turned, turned_act, pre, out_grad):
    return pl.pallas_call(
        gradient_kernel,
        grid=(1,),
        in_specs=[
            pl.BlockSpec((3, 384, 640), lambda i: (0, index, 0)),
            pl.BlockSpec((192, 640), lambda i: (index, 0)),
            whole_block(pre.shape),
            whole_block(out_grad.shape),
        ],
        out_specs=pl.BlockSpec(memory_space=pltpu.VMEM),
        out_shape=pltpu.VMEM((400, 1536), jnp.float32),
        scratch_shapes=[pltpu.VMEM((192, 768), jnp.float32)],
        compiler_params=pltpu.CompilerParams(vmem_limit_bytes=20 * 2**20),
        name="gradient",
    )(turned, turned_act, pre, out_grad)


def in_order(core, own, other, axis):
    return jnp.where(
        core == 0,
        jnp.concatenate([own, other], axis=axis),
        jnp.concatenate([other, own], axis=axis),
    )


def half_of(value, index, axis):
    size = value.shape[axis] // 2
    return lax.dynamic_slice_in_dim(value, index * size, size, axis)


def shards(activations, teacher_maps, projection, dilated_weight, pointwise_weight):
    teacher = lax.axis_index("teacher")
    seq = lax.axis_index("seq")
    yh, core = teacher // 2, teacher % 2
    x, yl, z = seq // 8, (seq // 4) % 2, seq % 4
    wins, bins, channels = activations.shape
    rows = wins * bins
    total_rows = rows * 128
    branch = dilated_weight.shape[2]
    half = branch // 2
    inputs = activations.reshape(rows, channels)
    forward = [(g * 32 + i, g * 32 + i + 1) for g in range(4) for i in range(31)]
    backward = [(b, a) for a, b in forward]
    low = send(activations[:, -TAP_DILATION:], forward)
    high = send(activations[:, :TAP_DILATION], backward)
    padded = jnp.concatenate([low, activations, high], axis=1)
    padded_other = send(padded, CORE)
    order = block_order(core, x, yl, z)
    order_other = block_order(1 - core, x, yl, z)
    cores = jnp.stack([core, 1 - core]).astype(jnp.int32)

    own_dil = lax.dynamic_slice_in_dim(dilated_weight, core * half, half, 2).reshape(48, 3 * half)
    own_pw = half_of(pointwise_weight, core, 1)
    own_block = jnp.concatenate([own_dil, concat(own_pw[:, :half], own_pw[:, half:])], axis=1)

    wide = channels // 2
    block = jnp.concatenate([projection[0], own_block], axis=1)[None]
    arrived = send(block, NEAR)
    near_p, near_w = [
        concat(block[:, :, low : low + channels], arrived[:, :, low : low + channels]) for low in (0, channels)
    ]
    first = ring_gather(near_p, True)
    first_a, first_b = [concat(*[v[:, :, low : low + wide] for v in first]) for low in (0, wide)]
    first_w = concat(*ring_gather(near_w, True))
    pieces_a = ring_gather(first_a, False)
    pieces_b = ring_gather(first_b, False)
    pieces_w = ring_gather(first_w, False)
    pieces_other = [send(pieces_w[0], CORE)]
    pieces_other += [send(piece, CORE) for piece in pieces_w[1:]]

    inputs_f = inputs.astype(jnp.float32)
    local = jnp.concatenate([jnp.sum(inputs_f, axis=0), jnp.sum(inputs_f * inputs_f, axis=0)])
    sums = sum_everywhere(local.reshape(24, 128)).reshape(2, channels)
    channel_mean = sums[0] / total_rows
    channel_var = sums[1] / total_rows - channel_mean * channel_mean
    scale = lax.rsqrt(channel_var + 1e-05)
    place = lax.broadcasted_iota(jnp.int32, (1, bins + 2 * TAP_DILATION, 1), 1) + seq * bins
    inside = (place >= TAP_DILATION) & (place < 32 * bins + TAP_DILATION)

    def hidden_of(value):
        normed = (value.astype(jnp.float32) - channel_mean) * scale
        return jnp.where(inside, gelu_tanh(normed), 0.0).astype(jnp.bfloat16)

    hidden, hidden_other = hidden_of(padded), hidden_of(padded_other)

    maps = teacher_maps.reshape(4, rows, teacher_maps.shape[3])
    far_groups = jnp.stack([(1 - yh) * 2 + 1 - core, (1 - yh) * 2 + core]).astype(jnp.int32)
    near_groups = jnp.stack([yh * 2 + 1 - core, yh * 2 + core]).astype(jnp.int32)
    arrived = []
    for pieces in (pieces_a, pieces_b):
        other, own = teacher_terms(order, far_groups, maps, pieces, 16)
        other = send(other, CORE)
        power = jnp.maximum(own[320:321], other[320:321]).astype(jnp.float32)
        packed = pack(own[:320].astype(jnp.float32) + other[:320].astype(jnp.float32), power)
        arrived.append(send(packed, FAR))
    other, own = teacher_terms(order, near_groups, maps, pieces_a + pieces_b, 0)

    other = send(other, CORE)

    preact, activated, base, point = forward_pass(
        jnp.stack([order, order_other]), cores, [hidden, inputs, own, other], pieces_w + pieces_other
    )
    out_grads, squared = [], []
    for value, terms in zip(base, arrived, strict=True):
        misfit = value - unpack(terms) * 0.25
        squared.append(jnp.sum(misfit * misfit, axis=0))
        out_grads.append((misfit / channels).astype(jnp.bfloat16))
    back_grad = sum(
        lax.dot_general(v, w, (((1,), (1,)), ((), ())), preferred_element_type=jnp.float32)
        for v, w in zip(out_grads, point, strict=True)
    )
    preact_grad = (back_grad * gelu_slope(preact)).astype(jnp.bfloat16)

    turned = turn(order, hidden, hidden_other)
    turned_act = turn_act(order, activated, send(activated, CORE))
    out_own = jnp.where(core == 0, *out_grads)
    swapped = send(
        jnp.concatenate(
            [jnp.where(core == 0, *out_grads[::-1]), half_of(preact_grad, 1 - core, 1)], axis=1
        ),
        CORE,
    )
    out_both = concat(out_own, swapped[:, :wide])
    pre_both = concat(half_of(preact_grad, core, 1), swapped[:, wide:])
    arrived = []
    for index in (3, 1, 2, 0):
        chunk = gradient_chunk(index, turned, turned_act, pre_both, out_both)
        if index:
            arrived.append(send(chunk.astype(jnp.float16), RING[False, STEPS[index]]))
    loss = jnp.broadcast_to(after(concat(*squared), chunk), (8, channels))
    loss = loss + sum(send(loss, RING[False, step]) for step in STEPS[1:])
    block, loss = finish_reduce(*add_up(unpack(chunk), power_in(chunk), arrived), loss[:1])
    other = send(concat(block, jnp.broadcast_to(loss, (8, channels))), CORE)
    loss_mean = 0.5 * jnp.sum(loss + other[48:49]) / (channels * total_rows)
    other = other[:48]

    def dilated_columns(v):
        return v[:, : 3 * half].reshape(48, 3, half)

    def pw_columns(v):
        v = v[:, 3 * half :].reshape(2, branch // 32, half)
        return v.transpose(1, 0, 2).reshape(branch // 32, branch)

    dilated_grad = in_order(core, dilated_columns(block), dilated_columns(other), 2)
    pointwise_grad = in_order(core, pw_columns(block), pw_columns(other), 1)
    return (loss_mean, dilated_grad, pointwise_grad)


def solution(mesh):
    in_specs = (
        P("teacher", "seq", None),
        P("teacher", None, "seq", None),
        P("teacher", "seq", None),
        P("seq", None, None),
        P("seq", None),
    )
    out_specs = (P(), P("seq", None, None), P("seq", None))

    return jax.shard_map(shards, mesh=mesh, in_specs=in_specs, out_specs=out_specs, check_vma=False)
```

```python
import jax
import jax.numpy as jnp
import numpy as np
from jax import lax
from jax.experimental import pallas as pl
from jax.experimental.pallas import tpu as pltpu
from jax.sharding import PartitionSpec as P


TAP_DILATION = 16
AXES = ("teacher", "seq")
SHAPE = (2, 2, 4, 2, 4)
STEPS = (0, -1, 1, 2)

slope_const = 0.7978845608
cubic_const = 0.044715


def pairs_of(move):
    pairs = []
    for source in range(int(np.prod(SHAPE))):
        at = [int(v) for v in np.unravel_index(source, SHAPE)]
        pairs.append((source, int(np.ravel_multi_index(move(*at), SHAPE))))
    return pairs


def along(first, step):
    def move(yh, core, x, yl, z):
        if (core == 0) == first:
            return (yh, core, (x + step) % 4, yl, z)
        return (yh, core, x, yl, (z + step) % 4)

    return pairs_of(move)


CORE = pairs_of(lambda yh, core, x, yl, z: (yh, 1 - core, x, yl, z))
FAR = pairs_of(lambda yh, core, x, yl, z: (1 - yh, core, x, yl, z))
NEAR = pairs_of(lambda yh, core, x, yl, z: (yh, core, x, 1 - yl, z))
FAR_NEAR = pairs_of(lambda yh, core, x, yl, z: (1 - yh, core, x, 1 - yl, z))
RING = {(first, step): along(first, step) for first in (True, False) for step in (1, -1, 2)}


def send(value, pairs):
    return lax.ppermute(value, AXES, pairs)


def gelu_tanh(value):
    inside = slope_const * (value + cubic_const * value * value * value)
    return 0.5 * value * (1.0 + jnp.tanh(inside))


def gelu_slope(value):
    inside = slope_const * (value + cubic_const * value * value * value)
    tangent = jnp.tanh(inside)
    return 0.5 * (1.0 + tangent) + 0.5 * value * (1.0 - tangent * tangent) * slope_const * (
        1.0 + 3.0 * cubic_const * value * value
    )


def block_order(core, x, yl, z):
    first = jnp.where(core == 0, x, z)
    second = jnp.where(core == 0, z, x)
    order = []
    for far in STEPS:
        for near in STEPS:
            for side in (0, 1):
                one = (first + near + 4) % 4
                two = (second + far + 4) % 4
                at_x = jnp.where(core == 0, one, two)
                at_z = jnp.where(core == 0, two, one)
                order.append((at_x * 2 + (yl + side) % 2) * 4 + at_z)
    return jnp.stack(order).astype(jnp.int32)


def concat(*values):
    return jnp.concatenate(values)


def after(value, *earlier):
    return lax.optimization_barrier((value, *earlier))[0]


def ring_gather(value, first):
    return [value] + [send(value, RING[first, step]) for step in (1, -1, 2)]


def power_of(peak):
    return jnp.clip(jnp.floor(jnp.log2(jnp.maximum(peak, 1e-30))) - 13.0, -110.0, 127.0)


def pack(value, power, loss=None):
    rows = jnp.broadcast_to(power, (16, value.shape[1]))
    if loss is not None:
        exponent = jnp.floor(jnp.log2(jnp.maximum(loss, 1e-30)))
        rest = loss * jnp.exp2(-exponent)
        upper = jnp.floor(rest * 512.0) / 512.0
        which = lax.broadcasted_iota(jnp.int32, rows.shape, 0)
        for row, part in enumerate((exponent, upper, (rest - upper) * 1024.0)):
            rows = jnp.where(which == row + 1, part, rows)
    scaled = (value * jnp.exp2(-power)).astype(jnp.float16)
    return concat(scaled, rows.astype(jnp.float16))


def power_in(packed):
    return packed[-16:-15].astype(jnp.float32)


def unpack(packed):
    return packed[:-16].astype(jnp.float32) * jnp.exp2(power_in(packed))


def loss_in(packed):
    exponent, upper, lower = [packed[row : row + 1].astype(jnp.float32) for row in (-15, -14, -13)]
    return jnp.exp2(exponent) * (upper + lower / 1024.0)


def sum_everywhere(value, earlier):
    value = value + send(value, CORE)
    value = value + send(value, NEAR) + send(value, FAR) + send(value, FAR_NEAR)
    for index, first in ((1, True), (2, False)):
        arrived = [send(value, RING[first, step]) for step in STEPS[1:]]
        if index == 1:
            arrived = lax.optimization_barrier((*arrived, earlier))[:3]
        value = value + sum(arrived)
    return value


def add_up(own, own_power, arrived):
    power = own_power
    for packed in arrived:
        own = own + unpack(packed)
        power = jnp.maximum(power, power_in(packed))
    return own, power + 2.0


def finish_reduce(own, power, loss):
    rows = own.shape[0] // 8
    arrived = [
        send(pack(own[2 * rows * (i + 1) : 2 * rows * (i + 2)], power, loss), RING[True, step])
        for i, step in enumerate(STEPS[1:])
    ]
    own, power = add_up(own[: 2 * rows], power, arrived)
    loss = loss + sum(loss_in(packed) for packed in arrived)
    keep, give = pack(own[:rows], power, loss), pack(own[rows:], power, loss)
    arrived = [send(give, NEAR), send(keep, FAR), send(give, FAR_NEAR)]
    return add_up(own[:rows], power, arrived)[0], loss + sum(loss_in(packed) for packed in arrived)


def load_blocks(order, pieces, target, sem):
    for index, piece in enumerate(pieces):

        def start(at, carry, index=index, piece=piece):
            row = pl.multiple_of(order[8 * index + at] * 48, 16)
            pltpu.make_async_copy(piece.at[at], target(row), sem).start()
            return carry

        lax.fori_loop(0, 8, start, 0)


def teacher_kernel(order, groups, maps_other, maps_own, *refs):
    count = len(refs) - 4
    other, own, whole, sem = refs[count:]
    width = whole.shape[1]
    each = refs[0].shape[2]
    for part in range(count // 4):
        load_blocks(
            order,
            refs[4 * part : 4 * part + 4],
            lambda row, part=part: whole.at[pl.ds(row, 48), part * each : (part + 1) * each],
            sem,
        )
    pltpu.make_async_copy(whole, whole, sem).wait()

    def columns(i, carry):
        lanes = pl.ds(pl.multiple_of(i * 768, 768), 768)
        for maps, out in ((maps_other, other), (maps_own, own)):
            terms = jnp.dot(maps[0], whole[:, lanes], preferred_element_type=jnp.float32)
            out[:320, lanes] = terms.astype(jnp.bfloat16)
            if out.shape[0] > 320:
                power = power_of(jnp.max(jnp.abs(terms), axis=0, keepdims=True)) + 1.0
                out[320:, lanes] = jnp.broadcast_to(power, (16, 768)).astype(jnp.bfloat16)
        return carry

    lax.fori_loop(0, width // 768, columns, 0)


def teacher_terms(order, groups, maps, pieces, extra):
    rows, depth = maps.shape[1:]
    width = pieces[0].shape[2] * len(pieces) // 4
    return pl.pallas_call(
        teacher_kernel,
        grid_spec=pltpu.PrefetchScalarGridSpec(
            num_scalar_prefetch=2,
            grid=(1,),
            in_specs=[
                pl.BlockSpec((1, rows, depth), lambda i, order, groups: (groups[0], 0, 0)),
                pl.BlockSpec((1, rows, depth), lambda i, order, groups: (groups[1], 0, 0)),
            ]
            + [pl.BlockSpec(memory_space=pl.ANY)] * len(pieces),
            out_specs=[whole_block((rows + extra, width))] * 2,
            scratch_shapes=[pltpu.VMEM((depth, width), jnp.bfloat16), pltpu.SemaphoreType.DMA(())],
        ),
        out_shape=[jax.ShapeDtypeStruct((rows + extra, width), jnp.bfloat16)] * 2,
        compiler_params=pltpu.CompilerParams(vmem_limit_bytes=30 * 2**20),
        name="teacher",
    )(order, groups, maps, maps, *pieces)


def forward_kernel(orders, cores, hidden, inputs, near_own, near_other, *refs):
    pieces = refs[:8]
    preact, activated, base, point, whole, sems = refs[8:]
    for part in range(2):
        load_blocks(
            orders.at[part],
            pieces[4 * part : 4 * part + 4],
            lambda row, part=part: whole.at[part, pl.ds(row, 48), :],
            sems.at[part],
        )

    def half(part, carry):
        pltpu.make_async_copy(whole.at[part], whole.at[part], sems.at[part]).wait()
        core = cores[part]

        def rows_of(pair, inner):
            rows = whole[part, pl.ds(pl.multiple_of(96 * pair, 96), 96), 1152:].astype(jnp.float32)
            for side in range(2):
                point[core, pl.ds(pl.multiple_of(48 * pair, 48), 48), side * 384 : side * 384 + 384] = concat(
                    rows[24 * side : 24 * side + 24], rows[48 + 24 * side : 72 + 24 * side]
                ).astype(jnp.bfloat16)
            return inner

        lax.fori_loop(0, 16, rows_of, 0)
        running = jnp.zeros((320, 384), jnp.float32)
        for k in range(3):
            tap = hidden[:, k * TAP_DILATION : k * TAP_DILATION + 64, :].reshape(320, 1536)
            running = running + jnp.dot(
                tap, whole[part, :, k * 384 : k * 384 + 384], preferred_element_type=jnp.float32
            )
        lanes = pl.ds(pl.multiple_of(core * 384, 128), 384)
        preact[:, lanes] = running
        activated[:, lanes] = gelu_tanh(running).astype(jnp.bfloat16)
        return carry

    lax.fori_loop(0, 2, half, 0)

    def student(part, carry):
        lanes = pl.ds(pl.multiple_of(part * 768, 768), 768)
        near = near_own[:, lanes].astype(jnp.float32) + near_other[:, lanes].astype(jnp.float32)
        base[part] = (
            inputs[:, lanes].astype(jnp.float32)
            + jnp.dot(activated[...], point[part], preferred_element_type=jnp.float32)
        ) - near * 0.25
        return carry

    lax.fori_loop(0, 2, student, 0)


def whole_block(shape):
    return pl.BlockSpec(shape, lambda *i: (0,) * len(shape))


def forward_pass(orders, cores, arrays, pieces):
    outs = [((320, 768), jnp.float32), ((320, 768), jnp.bfloat16)]
    outs += [((2, 320, 768), jnp.float32), ((2, 768, 768), jnp.bfloat16)]
    return pl.pallas_call(
        forward_kernel,
        grid_spec=pltpu.PrefetchScalarGridSpec(
            num_scalar_prefetch=2,
            grid=(1,),
            in_specs=[whole_block(array.shape) for array in arrays]
            + [pl.BlockSpec(memory_space=pl.ANY)] * len(pieces),
            out_specs=[whole_block(shape) for shape, _ in outs],
            scratch_shapes=[
                pltpu.VMEM((2, 1536, 1536), jnp.bfloat16),
                pltpu.SemaphoreType.DMA((2,)),
            ],
        ),
        out_shape=[(pltpu.VMEM if i == 1 else pltpu.HBM)(*out) for i, out in enumerate(outs)],
        compiler_params=pltpu.CompilerParams(vmem_limit_bytes=45 * 2**20),
        name="forward",
    )(orders, cores, *arrays, *pieces)


def turn_kernel(order, hidden, hidden_other, out, turned):
    def tap_of(k, carry):
        low = pl.multiple_of(k * TAP_DILATION, TAP_DILATION)
        for part, source in enumerate((hidden, hidden_other)):
            tap = source[:, pl.ds(low, 64), :].reshape(320, 1536)
            turned[:, part * 320 : part * 320 + 320] = tap.T

        def slot(i, inner):
            row = pl.multiple_of(order[i] * 48, 16)
            to = pl.multiple_of(i * 48, 48)
            out[k, pl.ds(to, 48), :] = turned[pl.ds(row, 48), :]
            return inner

        return lax.fori_loop(0, 32, slot, carry)

    lax.fori_loop(0, 3, tap_of, 0)


def turn(order, hidden, hidden_other):
    return pl.pallas_call(
        turn_kernel,
        grid_spec=pltpu.PrefetchScalarGridSpec(
            num_scalar_prefetch=1,
            grid=(1,),
            in_specs=[whole_block(hidden.shape)] * 2,
            out_specs=whole_block((3, 1536, 640)),
            scratch_shapes=[pltpu.VMEM((1536, 640), jnp.bfloat16)],
        ),
        out_shape=pltpu.HBM((3, 1536, 640), jnp.bfloat16),
        compiler_params=pltpu.CompilerParams(vmem_limit_bytes=30 * 2**20),
        name="turn",
    )(order, hidden, hidden_other)


def turn_act_kernel(order, activated, activated_other, out, turned):
    turned[:, :320] = activated[...].astype(jnp.float32).T
    turned[:, 320:] = activated_other[...].astype(jnp.float32).T

    def pair(i, carry):
        rows = [turned[pl.ds(pl.multiple_of(order[2 * i + j] * 24, 8), 24), :] for j in range(2)]
        out[pl.ds(pl.multiple_of(i * 48, 48), 48), :] = concat(*rows).astype(jnp.bfloat16)
        return carry

    lax.fori_loop(0, 16, pair, 0)


def turn_act(order, activated, activated_other):
    return pl.pallas_call(
        turn_act_kernel,
        grid_spec=pltpu.PrefetchScalarGridSpec(
            num_scalar_prefetch=1,
            grid=(1,),
            in_specs=[whole_block(activated.shape)] * 2,
            out_specs=whole_block((768, 640)),
            scratch_shapes=[pltpu.VMEM((768, 640), jnp.float32)],
        ),
        out_shape=jax.ShapeDtypeStruct((768, 640), jnp.bfloat16),
        compiler_params=pltpu.CompilerParams(vmem_limit_bytes=16 * 2**20),
        name="turn_act",
    )(order, activated, activated_other)


def gradient_kernel(turned, turned_act, pre, out_grad, out, scratch):
    def scale(lanes, peak):
        power = power_of(peak)
        out[384:, lanes] = jnp.broadcast_to(power, (16, 384))
        return jnp.exp2(-power)

    def tap_of(k, carry):
        product = jnp.dot(turned[k], pre[...], preferred_element_type=jnp.float32)
        lanes = pl.ds(pl.multiple_of(k * 384, 384), 384)
        out[:384, lanes] = product * scale(lanes, jnp.max(jnp.abs(product), axis=0, keepdims=True))
        return carry

    lax.fori_loop(0, 3, tap_of, 0)
    product = jnp.dot(turned_act[...], out_grad[...], preferred_element_type=jnp.float32)
    scratch[...] = product
    peak = jnp.max(jnp.abs(product), axis=0, keepdims=True)
    factor = scale(slice(1152, 1536), jnp.maximum(peak[:, :384], peak[:, 384:]))

    def rows_of(i, carry):
        rows = scratch[pl.ds(pl.multiple_of(24 * i, 8), 24), :]
        to = pl.multiple_of(48 * i, 8)
        out[pl.ds(to, 24), 1152:] = rows[:, :384] * factor
        out[pl.ds(to + 24, 24), 1152:] = rows[:, 384:] * factor
        return carry

    lax.fori_loop(0, 8, rows_of, 0)


def gradient_chunk(index, turned, turned_act, pre, out_grad):
    return pl.pallas_call(
        gradient_kernel,
        grid=(1,),
        in_specs=[
            pl.BlockSpec((3, 384, 640), lambda i: (0, index, 0)),
            pl.BlockSpec((192, 640), lambda i: (index, 0)),
            whole_block(pre.shape),
            whole_block(out_grad.shape),
        ],
        out_specs=pl.BlockSpec(memory_space=pltpu.VMEM),
        out_shape=pltpu.VMEM((400, 1536), jnp.float32),
        scratch_shapes=[pltpu.VMEM((192, 768), jnp.float32)],
        compiler_params=pltpu.CompilerParams(vmem_limit_bytes=20 * 2**20),
        name="gradient",
    )(turned, turned_act, pre, out_grad)


def in_order(core, own, other, axis):
    return jnp.where(
        core == 0,
        jnp.concatenate([own, other], axis=axis),
        jnp.concatenate([other, own], axis=axis),
    )


def half_of(value, index, axis):
    size = value.shape[axis] // 2
    return lax.dynamic_slice_in_dim(value, index * size, size, axis)


def shards(activations, teacher_maps, projection, dilated_weight, pointwise_weight):
    teacher = lax.axis_index("teacher")
    seq = lax.axis_index("seq")
    yh, core = teacher // 2, teacher % 2
    x, yl, z = seq // 8, (seq // 4) % 2, seq % 4
    wins, bins, channels = activations.shape
    rows = wins * bins
    total_rows = rows * 128
    branch = dilated_weight.shape[2]
    half = branch // 2
    inputs = activations.reshape(rows, channels)
    forward = [(g * 32 + i, g * 32 + i + 1) for g in range(4) for i in range(31)]
    backward = [(b, a) for a, b in forward]
    low = send(activations[:, -TAP_DILATION:], forward)
    high = send(activations[:, :TAP_DILATION], backward)
    order = block_order(core, x, yl, z)
    order_other = block_order(1 - core, x, yl, z)
    cores = jnp.stack([core, 1 - core]).astype(jnp.int32)

    own_dil = lax.dynamic_slice_in_dim(dilated_weight, core * half, half, 2).reshape(48, 3 * half)
    own_pw = half_of(pointwise_weight, core, 1)
    own_block = jnp.concatenate([own_dil, concat(own_pw[:, :half], own_pw[:, half:])], axis=1)

    wide = channels // 2
    block = jnp.concatenate([projection[0], own_block], axis=1)[None]
    near = concat(block, send(block, NEAR))
    first = ring_gather(near, True)
    first_a, first_b, first_w = [
        concat(*[v[:, :, low:high] for v in first])
        for low, high in ((0, wide), (wide, channels), (channels, 2 * channels))
    ]
    pieces_a = ring_gather(first_a, False)
    pieces_b = ring_gather(first_b, False)
    pieces_w = ring_gather(first_w, False)
    pieces_other = [send(pieces_w[0], CORE)]
    pieces_other += [send(piece, CORE) for piece in pieces_w[1:]]

    low, high = lax.optimization_barrier((low, high, pieces_a[1]))[:2]
    padded = jnp.concatenate([low, activations, high], axis=1)
    padded_other = send(padded, CORE)

    inputs_f = inputs.astype(jnp.float32)
    local = jnp.concatenate([jnp.sum(inputs_f, axis=0), jnp.sum(inputs_f * inputs_f, axis=0)])
    sums = sum_everywhere(local.reshape(24, 128), first_a).reshape(2, channels)
    channel_mean = sums[0] / total_rows
    channel_var = sums[1] / total_rows - channel_mean * channel_mean
    scale = lax.rsqrt(channel_var + 1e-05)
    place = lax.broadcasted_iota(jnp.int32, (1, bins + 2 * TAP_DILATION, 1), 1) + seq * bins
    inside = (place >= TAP_DILATION) & (place < 32 * bins + TAP_DILATION)

    def hidden_of(value):
        normed = (value.astype(jnp.float32) - channel_mean) * scale
        return jnp.where(inside, gelu_tanh(normed), 0.0).astype(jnp.bfloat16)

    hidden, hidden_other = hidden_of(padded), hidden_of(padded_other)

    maps = teacher_maps.reshape(4, rows, teacher_maps.shape[3])
    far_groups = jnp.stack([(1 - yh) * 2 + 1 - core, (1 - yh) * 2 + core]).astype(jnp.int32)
    near_groups = jnp.stack([yh * 2 + 1 - core, yh * 2 + core]).astype(jnp.int32)
    arrived = []
    for pieces in (pieces_a, pieces_b):
        other, own = teacher_terms(order, far_groups, maps, pieces, 16)
        other = send(other, CORE)
        power = jnp.maximum(own[320:321], other[320:321]).astype(jnp.float32)
        packed = pack(own[:320].astype(jnp.float32) + other[:320].astype(jnp.float32), power)
        arrived.append(send(packed, FAR))
    other, own = teacher_terms(order, near_groups, maps, pieces_a + pieces_b, 0)

    other = send(other, CORE)

    preact, activated, base, point = forward_pass(
        jnp.stack([order, order_other]), cores, [hidden, inputs, own, other], pieces_w + pieces_other
    )
    out_grads, squared = [], []
    for value, terms in zip(base, arrived, strict=True):
        misfit = value - unpack(terms) * 0.25
        squared.append(jnp.sum(misfit * misfit, axis=0))
        out_grads.append((misfit / channels).astype(jnp.bfloat16))
    back_grad = sum(
        lax.dot_general(v, w, (((1,), (1,)), ((), ())), preferred_element_type=jnp.float32)
        for v, w in zip(out_grads, point, strict=True)
    )
    preact_grad = (back_grad * gelu_slope(preact)).astype(jnp.bfloat16)

    turned = turn(order, hidden, hidden_other)
    turned_act = turn_act(order, activated, send(activated, CORE))
    out_own = jnp.where(core == 0, *out_grads)
    swapped = send(
        jnp.concatenate(
            [jnp.where(core == 0, *out_grads[::-1]), half_of(preact_grad, 1 - core, 1)], axis=1
        ),
        CORE,
    )
    out_both = concat(out_own, swapped[:, :wide])
    pre_both = concat(half_of(preact_grad, core, 1), swapped[:, wide:])
    arrived = []
    for index in (3, 1, 2, 0):
        chunk = gradient_chunk(index, turned, turned_act, pre_both, out_both)
        if index:
            arrived.append(send(chunk.astype(jnp.float16), RING[False, STEPS[index]]))
    loss = jnp.broadcast_to(after(concat(*squared), chunk), (8, channels))
    loss = loss + sum(send(loss, RING[False, step]) for step in STEPS[1:])
    block, loss = finish_reduce(*add_up(unpack(chunk), power_in(chunk), arrived), loss[:1])
    other = send(concat(block, jnp.broadcast_to(loss, (8, channels))), CORE)
    loss_mean = 0.5 * jnp.sum(loss + other[48:49]) / (channels * total_rows)
    other = other[:48]

    def dilated_columns(v):
        return v[:, : 3 * half].reshape(48, 3, half)

    def pw_columns(v):
        v = v[:, 3 * half :].reshape(2, branch // 32, half)
        return v.transpose(1, 0, 2).reshape(branch // 32, branch)

    dilated_grad = in_order(core, dilated_columns(block), dilated_columns(other), 2)
    pointwise_grad = in_order(core, pw_columns(block), pw_columns(other), 1)
    return (loss_mean, dilated_grad, pointwise_grad)


def solution(mesh):
    in_specs = (
        P("teacher", "seq", None),
        P("teacher", None, "seq", None),
        P("teacher", "seq", None),
        P("seq", None, None),
        P("seq", None),
    )
    out_specs = (P(), P("seq", None, None), P("seq", None))

    return jax.shard_map(shards, mesh=mesh, in_specs=in_specs, out_specs=out_specs, check_vma=False)
```
